256 devices in a mesh: tm: 8 (over y_hi, x), dp: 32 (over z, y_lo, core).
Axes of the slice: x: 4, y: 4 (y_hi: 2, y_lo: 2; y = y_hi * 2 + y_lo), z: 8, core: 2. Of those that a mesh axis runs over, the one named last changes fastest.
Arguments:
- features: bfloat16 [32, 3072, 1024], P('dp', 'tm'), may hold values from -6 to 6
- cotangent: bfloat16 [32, 3072, 1024], P('dp', 'tm'), may hold values from -6 to 6
- lengths: int32 [32], P('dp'), may hold values from 768 to 3072, as said below
- norm_gain: float32 [1024], replicated, may hold values from 0.5 to 1.5
- lift_weight: bfloat16 [1024, 2048], replicated, may hold values from -0.1875 to 0.1875
- conv_kernel: float32 [9, 1024], replicated, may hold values from -2 to 2
- proj_weight: bfloat16 [1024, 1024], replicated, may hold values from -0.1875 to 0.1875
Outputs:
- output: bfloat16 [32, 3072, 1024], P('dp', 'tm')
- grad_features: bfloat16 [32, 3072, 1024], P('dp', 'tm')
- grads: float32 [3155968], P(('tm', 'dp'))
The draws below stay inside these ranges and needn't reach their ends.
Inputs may be any that keep to these rules, and one draw needn't show every extreme that they name: `lengths`: one recording has exactly 3072 valid frames and another exactly 768.
All inputs are finite; a program needn't handle non-finite values.
Results may differ from the reference program's by a relative error of at most 0.015.
Values may be sent and summed in bfloat16 or wider, within the bound.
No kernel may reach another device: no remote copies, remote signals or barrier semaphores. Data moves between devices by JAX's collectives and lax.ppermute only.
A program may use at most 128 MiB of HBM per device.

```python
import jax
import jax.numpy as jnp
from jax import lax

D = 1024
KERNEL = 9
RECS = 32
FRAMES = 3072


def draw_lengths(key, part):
    key_drawn, key_order = jax.random.split(jax.random.fold_in(key, 7))
    drawn = jax.random.randint(key_drawn, (RECS,), FRAMES // 4, FRAMES + 1)
    shuffled = jax.random.permutation(key_order, RECS)
    position = jnp.arange(RECS)
    drawn = jnp.where(position == shuffled[0], FRAMES, drawn)
    drawn = jnp.where(position == shuffled[1], FRAMES // 4, drawn)
    return drawn.astype(jnp.int32)


def level_of(own_key, extent, pieces, smallest, high):
    level, own = 1.0, jax.random.fold_in(own_key, 6)
    for dim, shards_of in pieces:
        heights = jnp.exp(jax.random.uniform(jax.random.fold_in(own, dim), (shards_of,), jnp.float32, smallest / len(pieces), high / len(pieces)))
        level = level * jnp.repeat(heights, extent[dim] // shards_of).reshape([-1 if axis == dim else 1 for axis in range(len(extent))])
    return level


def scatter_about(own_key, extent, width, reach, shards=(), dtype=jnp.bfloat16):
    values = jax.random.normal(own_key, extent, jnp.float32) * width
    if len(shards) > 0:
        values = level_of(own_key, extent, shards, -0.22, 0.18) * values
    return jnp.clip(values, min=-reach, max=reach).astype(dtype)


def setup_inputs(seed: int = 0) -> dict:
    keys = jax.random.split(jax.random.key(seed), 8)
    features = scatter_about(keys[0], (RECS, FRAMES, D), 1.0, 6.0, ((0, 32), (1, 8)))
    cotangent = scatter_about(keys[1], (RECS, FRAMES, D), 1.0, 6.0, ((0, 32), (1, 8)))
    lengths = draw_lengths(jax.random.fold_in(keys[7], 71), 0)
    norm_gain = jnp.clip(1.0 + 0.1 * jax.random.normal(keys[3], (D,), jnp.float32), 0.5, 1.5)
    lift_weight = scatter_about(keys[4], (D, 2 * D), D ** -0.5, 0.1875)
    conv_kernel = scatter_about(keys[5], (KERNEL, D), KERNEL ** -0.5, 2.0, (), jnp.float32)
    proj_weight = scatter_about(keys[6], (D, D), D ** -0.5, 0.1875)
    return {"features": features, "cotangent": cotangent, "lengths": lengths, "norm_gain": norm_gain, "lift_weight": lift_weight, "conv_kernel": conv_kernel, "proj_weight": proj_weight}


eps_norm = 1e-05

def block_pass(record, record_grad, validity, norm_gain, lift_weight, conv_kernel, proj_weight):
    frame_count = record.shape[0]
    model_width = record.shape[1]
    kernel_taps = conv_kernel.shape[0]
    kernel_reach = kernel_taps // 2
    values = record.astype(jnp.float32)
    center = values - lax.optimization_barrier(jnp.mean(values, axis=-1, keepdims=True))
    inverse_std = lax.rsqrt(lax.optimization_barrier(jnp.mean(center * center, axis=-1, keepdims=True)) + eps_norm)
    unit_rows = center * inverse_std
    normed = (unit_rows * norm_gain).astype(jnp.bfloat16)
    lifted = jnp.dot(normed, lift_weight, preferred_element_type=jnp.float32)
    first_half = lifted[:, :model_width]
    gate_sigmoid = jax.nn.sigmoid(lifted[:, model_width:])
    gated_rows = (first_half * gate_sigmoid * validity).astype(jnp.bfloat16)
    padded = jnp.pad(gated_rows.astype(jnp.float32), ((kernel_reach, kernel_reach), (0, 0)))
    convolved = conv_kernel[0] * padded[0:frame_count]
    for offset in range(1, kernel_taps):
        convolved = convolved + conv_kernel[offset] * padded[offset:offset + frame_count]
    activated = jax.nn.silu(convolved).astype(jnp.bfloat16)
    branch = jnp.dot(activated, proj_weight, preferred_element_type=jnp.float32)
    output = (values + validity * branch).astype(jnp.bfloat16)
    grad_values = record_grad.astype(jnp.float32)
    grad_branch = (grad_values * validity).astype(jnp.bfloat16)
    grad_act = lax.dot_general(grad_branch, proj_weight, (((1,), (1,)), ((), ())), preferred_element_type=jnp.float32)
    conv_sigmoid = jax.nn.sigmoid(convolved)
    grad_conv = (grad_act * conv_sigmoid * (1.0 + convolved * (1.0 - conv_sigmoid))).astype(jnp.bfloat16)
    conv_grad32 = grad_conv.astype(jnp.float32)
    padded_grad = jnp.pad(conv_grad32, ((kernel_reach, kernel_reach), (0, 0)))
    grad_gated = conv_kernel[0] * padded_grad[2 * kernel_reach:2 * kernel_reach + frame_count]
    for offset in range(1, kernel_taps):
        begin_at = 2 * kernel_reach - offset
        grad_gated = grad_gated + conv_kernel[offset] * padded_grad[begin_at:begin_at + frame_count]
    masked = grad_gated * validity
    grad_first = masked * gate_sigmoid
    grad_second = masked * first_half * gate_sigmoid * (1.0 - gate_sigmoid)
    grad_lifted = jnp.concatenate([grad_first, grad_second], axis=-1).astype(jnp.bfloat16)
    grad_normed = lax.dot_general(grad_lifted, lift_weight, (((1,), (1,)), ((), ())), preferred_element_type=jnp.float32)
    grad_unit = grad_normed * norm_gain
    grad_input = inverse_std * (grad_unit - lax.optimization_barrier(jnp.mean(grad_unit, axis=-1, keepdims=True)) - unit_rows * lax.optimization_barrier(jnp.mean(grad_unit * unit_rows, axis=-1, keepdims=True)))
    grad_features = (grad_values + grad_input).astype(jnp.bfloat16)
    term_lift = lax.dot_general(normed, grad_lifted, (((0,), (0,)), ((), ())), preferred_element_type=jnp.float32)
    term_proj = lax.dot_general(activated, grad_branch, (((0,), (0,)), ((), ())), preferred_element_type=jnp.float32)
    term_kernel = jnp.stack([lax.optimization_barrier(jnp.sum(conv_grad32 * padded[offset:offset + frame_count], axis=0)) for offset in range(kernel_taps)])
    term_gain = lax.optimization_barrier(jnp.sum(grad_normed * unit_rows, axis=0))
    return (output, grad_features, (term_lift, term_proj, term_kernel, term_gain))

def reference(features, cotangent, lengths, norm_gain, lift_weight, conv_kernel, proj_weight):
    model_width = features.shape[2]
    kernel_taps = conv_kernel.shape[0]

    def one_record(totals, inputs):
        record, record_grad, length = inputs
        validity = (jnp.arange(FRAMES) < length).astype(jnp.float32)[:, None]
        output, grad_features, terms = block_pass(record, record_grad, validity, norm_gain, lift_weight, conv_kernel, proj_weight)
        totals = jax.tree.map(jnp.add, totals, terms)
        return (totals, (output, grad_features))
    initial = (jnp.zeros((model_width, 2 * model_width), jnp.float32), jnp.zeros((model_width, model_width), jnp.float32), jnp.zeros((kernel_taps, model_width), jnp.float32), jnp.zeros((model_width,), jnp.float32))
    totals, stacked = lax.scan(one_record, initial, (features, cotangent, lengths))
    grad_scale = (RECS * FRAMES) ** (-0.5)
    grads = jnp.concatenate([totals[0].reshape(-1), totals[1].reshape(-1), totals[2].reshape(-1), totals[3]]) * grad_scale
    return (stacked[0], stacked[1], grads)
```

```python
import jax
import jax.numpy as jnp
from jax import lax
from jax.sharding import Mesh, PartitionSpec as P

eps_norm = 1e-05
BF = jnp.bfloat16
F32 = jnp.float32
HALO = 8
WIN = 12


def tail_blocks(blocks, axes):
    n = blocks.shape[0]
    me = lax.axis_index(axes)
    got = [lax.dynamic_index_in_dim(blocks, me, 0, keepdims=False)]
    for step in (1, n - 1, 2):
        send = lax.dynamic_index_in_dim(blocks, lax.rem(me + step, n), 0, keepdims=False)
        got.append(lax.ppermute(send, axes, [(i, (i + step) % n) for i in range(n)]))
    return got


def add_up(parts):
    total = parts[0].astype(F32)
    for part in parts[1:]:
        total = total + part.astype(F32)
    return total


def swap_blocks(blocks, axis):
    return lax.all_to_all(blocks, axis, split_axis=0, concat_axis=0, tiled=True)


def reduce_terms(tiles_a, tiles_b, extra):
    half = WIN // 2
    a1 = tiles_a.transpose(1, 0, 3, 2, 4, 5, 6).reshape(4, 32 * half, 8, 128)
    a1 = jnp.concatenate([a1, jnp.broadcast_to(extra[None], (4, 5, 8, 128))], axis=1)
    b1 = tiles_b.transpose(0, 3, 1, 2, 4, 5, 6).reshape(4, 32 * half, 8, 128)
    b2 = add_up(tail_blocks(b1, ("yh", "yl"))).astype(BF)
    a2 = swap_blocks(a1, "x").astype(F32).sum(axis=0).astype(BF)
    a2x = a2[32 * half :]
    a2 = a2[: 32 * half].reshape(4, 8 * half, 8, 128)
    a2 = jnp.concatenate([a2, jnp.broadcast_to(a2x[None], (4, 5, 8, 128))], axis=1)
    a3 = add_up(tail_blocks(a2, ("yh", "yl"))).astype(BF)
    b3 = swap_blocks(b2.reshape(4, 8 * half, 8, 128), "x").astype(F32).sum(axis=0).astype(BF)
    c3 = jnp.concatenate(
        [
            a3[: 8 * half].reshape(8, half, 8, 128),
            b3.reshape(8, half, 8, 128),
            jnp.broadcast_to(a3[8 * half :][None], (8, 5, 8, 128)),
        ],
        axis=1,
    )
    return swap_blocks(c3, "z").astype(F32).sum(axis=0)


ALL = ("yh", "x", "z", "yl", "c")


def own_chunk(total, chunk, grad_scale):
    core = lax.axis_index("c")
    chip = lax.axis_index(("yh", "x", "z", "yl"))
    other = lax.ppermute(total, "c", [(0, 1), (1, 0)])
    head = total[:6]
    next0 = lax.ppermute(head, ALL, [(2 * j, 2 * j - 1) for j in range(1, 128)])
    next1 = lax.ppermute(head, ALL, [(2 * j + 1, 2 * j - 1) for j in range(1, 128)])
    first = core == 0
    half0 = jnp.where(first, total, other)
    half1 = jnp.where(first, other, total)
    both = jnp.stack([half0, half1], axis=1)
    window = both[:WIN].reshape(WIN, 2, 1024)
    small = jnp.concatenate([both[WIN:], jnp.zeros((1, 2, 8, 128), F32)], axis=0).reshape(6, 2, 1024)
    follow = jnp.stack([next0, next1], axis=1).reshape(6, 2, 1024)
    follow = jnp.where(chip == 127, small, follow)
    pairs = jnp.concatenate([window, follow], axis=0)
    as_lift = pairs.reshape(18, 2048)
    as_proj = pairs.reshape(18, 2, 2, 512).transpose(0, 2, 1, 3).reshape(18, 2048)
    number = chip * WIN + jnp.arange(18, dtype=jnp.int32)
    proj = (number >= 1024) & (number < 1536)
    flat = jnp.where(proj[:, None], as_proj, as_lift).reshape(-1)
    begin = (2 * chip + core) * chunk - chip * (WIN * 2048)
    return lax.dynamic_slice(flat, (begin,), (chunk,)) * grad_scale


def pair_swap(array):
    return lax.ppermute(array, "c", [(0, 1), (1, 0)])


def compute(x, g, first_row, length, norm_gain, lift_weight, conv_kernel, proj_weight):
    rows, width = x.shape
    own = slice(HALO, rows - HALO)
    positions = first_row - HALO + jnp.arange(rows, dtype=jnp.int32)
    validity = ((positions >= 0) & (positions < length)).astype(F32)[:, None]
    values = x.astype(F32)
    center = values - jnp.mean(values, axis=-1, keepdims=True)
    inverse_std = lax.rsqrt(jnp.mean(center * center, axis=-1, keepdims=True) + eps_norm)
    unit_rows = center * inverse_std
    normed = (unit_rows * norm_gain).astype(BF)
    lifted = jnp.dot(normed, lift_weight, preferred_element_type=F32)
    first_half = lifted[:, :width]
    gate_sigmoid = jax.nn.sigmoid(lifted[:, width:])
    gated = (first_half * gate_sigmoid * validity).astype(BF)
    mid = rows - 8
    convolved = conv_kernel[0] * gated[0:mid]
    for k in range(1, 9):
        convolved = convolved + conv_kernel[k] * gated[k : k + mid]
    sig = jax.nn.sigmoid(convolved)
    activated = (convolved * sig)[4:-4].astype(BF)
    branch = jnp.dot(activated, proj_weight, preferred_element_type=F32)
    output = (values[own] + validity[own] * branch).astype(BF)
    grad_branch = (g.astype(F32) * validity).astype(BF)
    grad_act = lax.dot_general(grad_branch[4:-4], proj_weight, (((1,), (1,)), ((), ())), preferred_element_type=F32)
    grad_conv = (grad_act * sig * (1.0 + convolved * (1.0 - sig))).astype(BF)
    n = rows - 2 * HALO
    grad_gated = conv_kernel[0] * grad_conv[8 : 8 + n]
    for k in range(1, 9):
        grad_gated = grad_gated + conv_kernel[k] * grad_conv[8 - k : 8 - k + n]
    masked = grad_gated * validity[own]
    gs = gate_sigmoid[own]
    grad_first = (masked * gs).astype(BF)
    grad_second = (masked * first_half[own] * gs * (1.0 - gs)).astype(BF)
    gc32 = grad_conv[4:-4].astype(F32)
    term_kernel = jnp.stack([jnp.sum(gc32 * gated[4 + k : 4 + k + n], axis=0) for k in range(9)])
    return output, normed[own], grad_first, grad_second, activated, grad_branch[own], term_kernel, unit_rows[own], inverse_std[own]


def local(features, cotangent, lengths, norm_gain, lift_weight, conv_kernel, proj_weight):
    x, g = features[0], cotangent[0]
    frames, width = x.shape
    core = lax.axis_index("c")
    edge = jnp.stack([x[-HALO:], g[-HALO:]])
    start = jnp.stack([x[:HALO], g[:HALO]])
    before = lax.ppermute(edge, ("yh", "x"), [(i, i + 1) for i in range(7)])
    after = lax.ppermute(start, ("yh", "x"), [(i + 1, i) for i in range(7)])
    first_row = lax.axis_index(("yh", "x")) * frames
    xx = jnp.concatenate([before[0], x, after[0]], axis=0)
    gg = jnp.concatenate([before[1], g, after[1]], axis=0)
    output, normed, grad_first, grad_second, activated, grad_branch, term_kernel, unit_rows, inverse_std = compute(
        xx, gg, first_row, lengths[0], norm_gain, lift_weight, conv_kernel, proj_weight
    )
    mine = core == 0
    keep = jnp.where(mine, grad_first, grad_second)
    give = jnp.where(mine, grad_second, grad_first)
    normed_other = pair_swap(normed)
    keep_other = pair_swap(give)
    act_other = pair_swap(activated)
    half = width // 2
    gb_give = jnp.where(mine, grad_branch[:, half:], grad_branch[:, :half])
    gb_keep = jnp.where(mine, grad_branch[:, :half], grad_branch[:, half:])
    gb_other = pair_swap(gb_give)
    contract = (((0,), (0,)), ((), ()))
    lift_half = lax.dot_general(
        jnp.concatenate([normed, normed_other]), jnp.concatenate([keep, keep_other]), contract, preferred_element_type=F32
    )
    proj_half = lax.dot_general(
        jnp.concatenate([activated, act_other]), jnp.concatenate([gb_keep, gb_other]), contract, preferred_element_type=F32
    )
    grad_lifted = jnp.concatenate([grad_first, grad_second], axis=-1)
    grad_normed = lax.dot_general(grad_lifted, lift_weight, (((1,), (1,)), ((), ())), preferred_element_type=F32)
    grad_unit = grad_normed * norm_gain
    grad_input = inverse_std * (
        grad_unit
        - jnp.mean(grad_unit, axis=-1, keepdims=True)
        - unit_rows * jnp.mean(grad_unit * unit_rows, axis=-1, keepdims=True)
    )
    grad_features = (g.astype(F32) + grad_input).astype(BF)
    term_gain = jnp.sum(grad_normed * unit_rows, axis=0)
    small = jnp.concatenate([term_kernel, term_gain[None]]).reshape(5, 2, 8, 128)
    small_keep = jnp.where(mine, small[:, 0], small[:, 1])
    small_give = jnp.where(mine, small[:, 1], small[:, 0])
    extra = (small_keep + pair_swap(small_give)).astype(BF)
    tiles = jnp.concatenate(
        [lift_half.astype(BF).reshape(1024, 8, 128), proj_half.astype(BF).reshape(512, 8, 128)]
    ).reshape(2, 4, 8, 2, WIN, 8, 128)
    total = reduce_terms(tiles[..., : WIN // 2, :, :], tiles[..., WIN // 2 :, :, :], extra)
    chunk = (2 * width * width + width * width + 10 * width) // 256
    grads = own_chunk(total, chunk, float(frames * 256) ** (-0.5))
    return output[None], grad_features[None], grads


def solution(mesh):
    fine = Mesh(mesh.devices.reshape(2, 4, 8, 2, 2), ALL)
    act = P(("z", "yl", "c"), ("yh", "x"), None)
    return jax.shard_map(
        local,
        mesh=fine,
        in_specs=(act, act, P(("z", "yl", "c")), P(), P(), P(), P()),
        out_specs=(act, act, P(ALL)),
        check_vma=False,
    )
```

```python
import jax
import jax.numpy as jnp
from jax import lax
from jax.experimental import pallas as pl
from jax.experimental.pallas import tpu as pltpu
from jax.sharding import Mesh, PartitionSpec as P

eps_norm = 1e-05
BF = jnp.bfloat16
F32 = jnp.float32
HALO = 8
WIN = 12


def any_spec():
    return pl.BlockSpec(memory_space=pl.ANY)


def vmem_spec():
    return pl.BlockSpec(memory_space=pltpu.VMEM)


def smem_spec():
    return pl.BlockSpec(memory_space=pltpu.SMEM)


def place(part_a, part_b, wide, begin, count):
    at = 0
    while at < count:
        window, inside = divmod(begin + at, 96)
        low = inside % 48
        step = min(48 - low, count - at)
        rows = wide[at : at + step, :].astype(BF)
        yh, rest = divmod(window, 64)
        if inside < 48:
            part_a[yh, rest, low : low + step, :] = rows
        else:
            part_b[yh * 2 + rest % 2, rest // 2, low : low + step, :] = rows
        at += step


def weight_kernel(place_ref, n0, n1, k0, k1, a0, a1, g0, g1, extra, *rest):
    outs, (part_a, part_b, wide, sem) = rest[:8], rest[8:]
    contract = (((0,), (0,)), ((), ()))
    for m in range(4):
        cols = slice(256 * m, 256 * m + 256)
        done = lax.dot_general(n0[:, cols], k0[...], contract, preferred_element_type=F32)
        done = done + lax.dot_general(n1[:, cols], k1[...], contract, preferred_element_type=F32)
        for v in range(8):
            wide[pl.ds(v, 256, stride=8), :] = done[:, 128 * v : 128 * v + 128]
        place(part_a, part_b, wide, 2048 * m, 2048)
    for m in range(4):
        cols = slice(256 * m, 256 * m + 256)
        done = lax.dot_general(a0[:, cols], g0[...], contract, preferred_element_type=F32)
        done = done + lax.dot_general(a1[:, cols], g1[...], contract, preferred_element_type=F32)
        for v in range(4):
            wide[pl.ds(v, 256, stride=4), :] = done[:, 128 * v : 128 * v + 128]
        place(part_a, part_b, wide, 8192 + 1024 * m, 1024)
    copies = []
    for s in range(4):
        x = (place_ref[0] + s) % 4
        y = (place_ref[1] + s) % 4
        for yh in range(2):
            copies.append((part_a.at[yh, pl.ds(x * 16, 16)], outs[s].at[pl.ds(yh * 16, 16)]))
        copies.append((extra, outs[s].at[32]))
        copies.append((part_b.at[y], outs[4 + s]))
    copies = [pltpu.make_async_copy(src, dst, sem.at[i]) for i, (src, dst) in enumerate(copies)]
    for copy in copies:
        copy.start()
    for copy in copies:
        copy.wait()


def weight_blocks(position, operands, extra):
    blocks = [jax.ShapeDtypeStruct((33, 48, 128), BF)] * 4 + [jax.ShapeDtypeStruct((32, 48, 128), BF)] * 4
    return pl.pallas_call(
        weight_kernel,
        out_shape=blocks,
        in_specs=[smem_spec()] + [vmem_spec()] * 9,
        out_specs=[any_spec()] * 8,
        scratch_shapes=[
            pltpu.VMEM((2, 64, 48, 128), BF),
            pltpu.VMEM((4, 32, 48, 128), BF),
            pltpu.VMEM((2048, 128), F32),
            pltpu.SemaphoreType.DMA((16,)),
        ],
        name="weight_grads",
    )(position, *operands, extra)


def sum_of(refs, index):
    total = refs[0][index].astype(F32)
    for ref in refs[1:]:
        total = total + ref[index].astype(F32)
    return total.astype(BF)


def first_x_kernel(place_ref, i0, i1, i2, i3, d0, d1, *outs):
    for s in range(4):
        y = (place_ref[1] + s) % 4
        base = (y // 2) * 16 + y % 2
        for z in range(8):
            outs[s][z] = sum_of((i0, i1, i2, i3), base + 2 * z)
        outs[s][8] = sum_of((i0, i1, i2, i3), 32)


def first_y_kernel(place_ref, i0, i1, i2, i3, *outs):
    for s in range(4):
        x = (place_ref[0] + s) % 4
        for z in range(8):
            outs[s][z] = sum_of((i0, i1, i2, i3), x * 8 + z)


def second_kernel(a0, a1, a2, a3, b0, b1, b2, b3, out):
    small = sum_of((a0, a1, a2, a3), 8)
    for z in range(8):
        out[z, 0:48, :] = sum_of((a0, a1, a2, a3), z)
        out[z, 48:96, :] = sum_of((b0, b1, b2, b3), z)
        out[z, 96:144, :] = small


def send(blocks, axes):
    n = 4
    got = [blocks[0]]
    for step in (2, 1, 3):
        got.append(lax.ppermute(blocks[step], axes, [(i, (i + step) % n) for i in range(n)]))
    return got


def reduce_terms(position, blocks, cover):
    got_x = send(blocks[:4], "x")
    got_y = send(blocks[4:], ("yh", "yl"))
    block9 = jax.ShapeDtypeStruct((9, 48, 128), BF)
    block8 = jax.ShapeDtypeStruct((8, 48, 128), BF)
    after_x = pl.pallas_call(
        first_x_kernel,
        out_shape=[block9] * 4,
        in_specs=[smem_spec()] + [vmem_spec()] * 4 + [any_spec()] * 2,
        out_specs=[vmem_spec()] * 4,
        name="sum_after_x",
    )(position, *got_x, *cover)
    after_y = pl.pallas_call(
        first_y_kernel,
        out_shape=[block8] * 4,
        in_specs=[smem_spec()] + [vmem_spec()] * 4,
        out_specs=[vmem_spec()] * 4,
        name="sum_after_y",
    )(position, *got_y)
    got_a = send(after_x, ("yh", "yl"))
    got_b = send(after_y, "x")
    ready = pl.pallas_call(
        second_kernel,
        out_shape=jax.ShapeDtypeStruct((8, 144, 128), BF),
        in_specs=[vmem_spec()] * 8,
        out_specs=vmem_spec(),
        name="sum_before_z",
    )(*got_a, *got_b)
    swapped = lax.all_to_all(ready, "z", split_axis=0, concat_axis=0, tiled=True)
    return swapped.astype(F32).sum(axis=0).reshape(18, 8, 128)


ALL = ("yh", "x", "z", "yl", "c")


def own_chunk(total, chunk, grad_scale):
    core = lax.axis_index("c")
    chip = lax.axis_index(("yh", "x", "z", "yl"))
    other = lax.ppermute(total, "c", [(0, 1), (1, 0)])
    head = total[:6]
    next0 = lax.ppermute(head, ALL, [(2 * j, 2 * j - 1) for j in range(1, 128)])
    next1 = lax.ppermute(head, ALL, [(2 * j + 1, 2 * j - 1) for j in range(1, 128)])
    first = core == 0
    half0 = jnp.where(first, total, other)
    half1 = jnp.where(first, other, total)
    both = jnp.stack([half0, half1], axis=1)
    window = both[:WIN].reshape(WIN, 2, 1024)
    small = both[WIN:].reshape(6, 2, 1024)
    follow = jnp.stack([next0, next1], axis=1).reshape(6, 2, 1024)
    follow = jnp.where(chip == 127, small, follow)
    pairs = jnp.concatenate([window, follow], axis=0)
    as_lift = pairs.reshape(18, 2048)
    as_proj = pairs.reshape(18, 2, 2, 512).transpose(0, 2, 1, 3).reshape(18, 2048)
    number = chip * WIN + jnp.arange(18, dtype=jnp.int32)
    proj = (number >= 1024) & (number < 1536)
    flat = jnp.where(proj[:, None], as_proj, as_lift).reshape(-1)
    begin = (2 * chip + core) * chunk - chip * (WIN * 2048)
    return lax.dynamic_slice(flat, (begin,), (chunk,)) * grad_scale


def pair_swap(array):
    return lax.ppermute(array, "c", [(0, 1), (1, 0)])


def compute(x, g, first_row, length, norm_gain, lift_weight, conv_kernel, proj_weight):
    rows, width = x.shape
    own = slice(HALO, rows - HALO)
    positions = first_row - HALO + jnp.arange(rows, dtype=jnp.int32)
    validity = ((positions >= 0) & (positions < length)).astype(F32)[:, None]
    values = x.astype(F32)
    center = values - jnp.mean(values, axis=-1, keepdims=True)
    inverse_std = lax.rsqrt(jnp.mean(center * center, axis=-1, keepdims=True) + eps_norm)
    unit_rows = center * inverse_std
    normed = (unit_rows * norm_gain).astype(BF)
    lifted = jnp.dot(normed, lift_weight, preferred_element_type=F32)
    first_half = lifted[:, :width]
    gate_sigmoid = jax.nn.sigmoid(lifted[:, width:])
    gated = (first_half * gate_sigmoid * validity).astype(BF)
    mid = rows - 8
    convolved = conv_kernel[0] * gated[0:mid]
    for k in range(1, 9):
        convolved = convolved + conv_kernel[k] * gated[k : k + mid]
    sig = jax.nn.sigmoid(convolved)
    activated = (convolved * sig)[4:-4].astype(BF)
    branch = jnp.dot(activated, proj_weight, preferred_element_type=F32)
    output = (values[own] + validity[own] * branch).astype(BF)
    grad_branch = (g.astype(F32) * validity).astype(BF)
    grad_act = lax.dot_general(grad_branch[4:-4], proj_weight, (((1,), (1,)), ((), ())), preferred_element_type=F32)
    grad_conv = (grad_act * sig * (1.0 + convolved * (1.0 - sig))).astype(BF)
    n = rows - 2 * HALO
    grad_gated = conv_kernel[0] * grad_conv[8 : 8 + n]
    for k in range(1, 9):
        grad_gated = grad_gated + conv_kernel[k] * grad_conv[8 - k : 8 - k + n]
    masked = grad_gated * validity[own]
    gs = gate_sigmoid[own]
    grad_first = (masked * gs).astype(BF)
    grad_second = (masked * first_half[own] * gs * (1.0 - gs)).astype(BF)
    gc32 = grad_conv[4:-4].astype(F32)
    term_kernel = jnp.stack([jnp.sum(gc32 * gated[4 + k : 4 + k + n], axis=0) for k in range(9)])
    return output, normed[own], grad_first, grad_second, activated, grad_branch[own], term_kernel, unit_rows[own], inverse_std[own]


def local(features, cotangent, lengths, norm_gain, lift_weight, conv_kernel, proj_weight):
    x, g = features[0], cotangent[0]
    frames, width = x.shape
    core = lax.axis_index("c")
    edge = jnp.stack([x[-HALO:], g[-HALO:]])
    start = jnp.stack([x[:HALO], g[:HALO]])
    before = lax.ppermute(edge, ("yh", "x"), [(i, i + 1) for i in range(7)])
    after = lax.ppermute(start, ("yh", "x"), [(i + 1, i) for i in range(7)])
    first_row = lax.axis_index(("yh", "x")) * frames
    xx = jnp.concatenate([before[0], x, after[0]], axis=0)
    gg = jnp.concatenate([before[1], g, after[1]], axis=0)
    output, normed, grad_first, grad_second, activated, grad_branch, term_kernel, unit_rows, inverse_std = compute(
        xx, gg, first_row, lengths[0], norm_gain, lift_weight, conv_kernel, proj_weight
    )
    mine = core == 0
    keep = jnp.where(mine, grad_first, grad_second)
    give = jnp.where(mine, grad_second, grad_first)
    normed_other = pair_swap(normed)
    keep_other = pair_swap(give)
    act_other = pair_swap(activated)
    half = width // 2
    gb_give = jnp.where(mine, grad_branch[:, half:], grad_branch[:, :half])
    gb_keep = jnp.where(mine, grad_branch[:, :half], grad_branch[:, half:])
    gb_other = pair_swap(gb_give)
    grad_lifted = jnp.concatenate([grad_first, grad_second], axis=-1)
    grad_normed = lax.dot_general(grad_lifted, lift_weight, (((1,), (1,)), ((), ())), preferred_element_type=F32)
    grad_unit = grad_normed * norm_gain
    grad_input = inverse_std * (
        grad_unit
        - jnp.mean(grad_unit, axis=-1, keepdims=True)
        - unit_rows * jnp.mean(grad_unit * unit_rows, axis=-1, keepdims=True)
    )
    grad_features = (g.astype(F32) + grad_input).astype(BF)
    term_gain = jnp.sum(grad_normed * unit_rows, axis=0)
    small = jnp.concatenate([term_kernel, term_gain[None]]).reshape(5, 2, 8, 128)
    small_keep = jnp.where(mine, small[:, 0], small[:, 1])
    small_give = jnp.where(mine, small[:, 1], small[:, 0])
    extra = (small_keep + pair_swap(small_give)).astype(BF).reshape(40, 128)
    extra = jnp.concatenate([extra, jnp.zeros((8, 128), BF)])
    position = jnp.stack([lax.axis_index("x"), lax.axis_index(("yh", "yl"))]).astype(jnp.int32)
    operands = (normed, normed_other, keep, keep_other, activated, act_other, gb_keep, gb_other)
    blocks = weight_blocks(position, operands, extra)
    total = reduce_terms(position, blocks, (output, grad_features))
    chunk = (2 * width * width + width * width + 10 * width) // 256
    grads = own_chunk(total, chunk, float(frames * 256) ** (-0.5))
    return output[None], grad_features[None], grads


def solution(mesh):
    fine = Mesh(mesh.devices.reshape(2, 4, 8, 2, 2), ALL)
    act = P(("z", "yl", "c"), ("yh", "x"), None)
    return jax.shard_map(
        local,
        mesh=fine,
        in_specs=(act, act, P(("z", "yl", "c")), P(), P(), P(), P()),
        out_specs=(act, act, P(ALL)),
        check_vma=False,
    )
```

```python
import jax
import jax.numpy as jnp
from jax import lax
from jax.experimental import pallas as pl
from jax.experimental.pallas import tpu as pltpu
from jax.sharding import Mesh, PartitionSpec as P

eps_norm = 1e-05
BF = jnp.bfloat16
F32 = jnp.float32
WIN = 12


def any_spec():
    return pl.BlockSpec(memory_space=pl.ANY)


def vmem_spec():
    return pl.BlockSpec(memory_space=pltpu.VMEM)


def smem_spec():
    return pl.BlockSpec(memory_space=pltpu.SMEM)


def place(part_a, part_b, wide, begin, count):
    at = 0
    while at < count:
        window, inside = divmod(begin + at, 96)
        low = inside % 48
        step = min(48 - low, count - at)
        rows = wide[at : at + step, :].astype(BF)
        yh, rest = divmod(window, 64)
        if inside < 48:
            part_a[yh, rest, low : low + step, :] = rows
        else:
            part_b[yh * 2 + rest % 2, rest // 2, low : low + step, :] = rows
        at += step


def weight_kernel(place_ref, gain_ref, ck_ref, n0h, n1h, k0h, k1h, a0h, a1h, g0h, g1h, wh, *rest):
    outs, rest = rest[:8], rest[8:]
    n0, n1, k0, k1, a0, a1, g0, g1, w, part_a, part_b, wide, extra, sem, sem_in = rest
    core = place_ref[2]
    loads = [
        pltpu.make_async_copy(src, dst, sem_in.at[i])
        for i, (src, dst) in enumerate(
            zip(
                (a0h, g0h, a1h, g1h, n0h, k0h, n1h, k1h, wh.at[:, pl.ds(core * 1024, 1024)]),
                (a0, g0, a1, g1, n0, k0, n1, k1, w),
            )
        )
    ]
    for load in loads:
        load.start()
    contract = (((0,), (0,)), ((), ()))
    for load in loads[:4]:
        load.wait()
    for m in range(4):
        cols = slice(256 * m, 256 * m + 256)
        done = lax.dot_general(a0[:, cols], g0[...], contract, preferred_element_type=F32)
        done = done + lax.dot_general(a1[:, cols], g1[...], contract, preferred_element_type=F32)
        for v in range(4):
            wide[pl.ds(v, 256, stride=4), :] = done[:, 128 * v : 128 * v + 128]
        place(part_a, part_b, wide, 8192 + 1024 * m, 1024)
    for load in loads[4:]:
        load.wait()
    gains = []
    for m in range(4):
        cols = slice(256 * m, 256 * m + 256)
        done = lax.dot_general(n0[:, cols], k0[...], contract, preferred_element_type=F32)
        done = done + lax.dot_general(n1[:, cols], k1[...], contract, preferred_element_type=F32)
        folded = jnp.zeros((256, 128), F32)
        for v in range(8):
            piece = done[:, 128 * v : 128 * v + 128]
            wide[pl.ds(v, 256, stride=8), :] = piece
            folded = folded + piece * w[cols, 128 * v : 128 * v + 128].astype(F32)
        gains.append(jnp.sum(folded.T, axis=0, keepdims=True))
        place(part_a, part_b, wide, 2048 * m, 2048)
    for m in range(4):
        for j in range(2):
            at = 256 * m + 128 * j
            extra[40 + 2 * m + j : 41 + 2 * m + j, :] = gains[m][:, 128 * j : 128 * j + 128] / gain_ref[:, at : at + 128]
    extra[0:40, :] = ck_ref[...]
    small = part_b.at[4, 0]
    small[...] = extra[...].astype(BF)
    copies = []
    for s in range(4):
        x = (place_ref[0] + s) % 4
        y = (place_ref[1] + s) % 4
        for yh in range(2):
            copies.append((part_a.at[yh, pl.ds(x * 16, 16)], outs[s].at[pl.ds(yh * 16, 16)]))
        copies.append((small, outs[s].at[32]))
        copies.append((part_b.at[y], outs[4 + s]))
    copies = [pltpu.make_async_copy(src, dst, sem.at[i]) for i, (src, dst) in enumerate(copies)]
    for copy in copies:
        copy.start()
    for copy in copies:
        copy.wait()


def weight_blocks(position, gain, kernel_tiles, operands):
    blocks = [jax.ShapeDtypeStruct((33, 48, 128), BF)] * 4 + [jax.ShapeDtypeStruct((32, 48, 128), BF)] * 4
    return pl.pallas_call(
        weight_kernel,
        out_shape=blocks,
        in_specs=[smem_spec(), vmem_spec(), vmem_spec()] + [any_spec()] * 9,
        out_specs=[any_spec()] * 8,
        scratch_shapes=[pltpu.VMEM(o.shape, BF) for o in operands[:8]]
        + [
            pltpu.VMEM((1024, 1024), BF),
            pltpu.VMEM((2, 64, 48, 128), BF),
            pltpu.VMEM((5, 32, 48, 128), BF),
            pltpu.VMEM((2048, 128), F32),
            pltpu.VMEM((48, 128), F32),
            pltpu.SemaphoreType.DMA((16,)),
            pltpu.SemaphoreType.DMA((9,)),
        ],
        name="weight_grads",
    )(position, gain, kernel_tiles, *operands)


def sum_of(refs, index):
    total = refs[0][index].astype(F32)
    for ref in refs[1:]:
        total = total + ref[index].astype(F32)
    return total.astype(BF)


def first_x_kernel(place_ref, i0, i1, i2, i3, d0, d1, *outs):
    for s in range(4):
        y = (place_ref[1] + s) % 4
        base = (y // 2) * 16 + y % 2
        for z in range(8):
            outs[s][z] = sum_of((i0, i1, i2, i3), base + 2 * z)
        outs[s][8] = sum_of((i0, i1, i2, i3), 32)


def first_y_kernel(place_ref, i0, i1, i2, i3, *outs):
    for s in range(4):
        x = (place_ref[0] + s) % 4
        for z in range(8):
            outs[s][z] = sum_of((i0, i1, i2, i3), x * 8 + z)


def second_kernel(a0, a1, a2, a3, b0, b1, b2, b3, out):
    small = sum_of((a0, a1, a2, a3), 8)
    for z in range(8):
        out[z, 0:48, :] = sum_of((a0, a1, a2, a3), z)
        out[z, 48:96, :] = sum_of((b0, b1, b2, b3), z)
        out[z, 96:144, :] = small


def send(blocks, axes):
    n = 4
    got = [blocks[0]]
    for step in (2, 1, 3):
        got.append(lax.ppermute(blocks[step], axes, [(i, (i + step) % n) for i in range(n)]))
    return got


def reduce_terms(position, blocks, cover):
    got_x = send(blocks[:4], "x")
    got_y = send(blocks[4:], ("yh", "yl"))
    block9 = jax.ShapeDtypeStruct((9, 48, 128), BF)
    block8 = jax.ShapeDtypeStruct((8, 48, 128), BF)
    after_x = pl.pallas_call(
        first_x_kernel,
        out_shape=[block9] * 4,
        in_specs=[smem_spec()] + [vmem_spec()] * 4 + [any_spec()] * 2,
        out_specs=[vmem_spec()] * 4,
        name="sum_after_x",
    )(position, *got_x, *cover)
    after_y = pl.pallas_call(
        first_y_kernel,
        out_shape=[block8] * 4,
        in_specs=[smem_spec()] + [vmem_spec()] * 4,
        out_specs=[vmem_spec()] * 4,
        name="sum_after_y",
    )(position, *got_y)
    got_a = send(after_x, ("yh", "yl"))
    got_b = send(after_y, "x")
    ready = pl.pallas_call(
        second_kernel,
        out_shape=jax.ShapeDtypeStruct((8, 144, 128), BF),
        in_specs=[vmem_spec()] * 8,
        out_specs=vmem_spec(),
        name="sum_before_z",
    )(*got_a, *got_b)
    swapped = lax.all_to_all(ready, "z", split_axis=0, concat_axis=0, tiled=True)
    return swapped.astype(F32).sum(axis=0).reshape(18, 8, 128)


ALL = ("yh", "x", "z", "yl", "c")


def own_chunk(total, chunk, grad_scale):
    core = lax.axis_index("c")
    chip = lax.axis_index(("yh", "x", "z", "yl"))
    other = lax.ppermute(total, "c", [(0, 1), (1, 0)])
    head = total[:6]
    next0 = lax.ppermute(head, ALL, [(2 * j, 2 * j - 1) for j in range(1, 128)])
    next1 = lax.ppermute(head, ALL, [(2 * j + 1, 2 * j - 1) for j in range(1, 128)])
    first = core == 0
    half0 = jnp.where(first, total, other)
    half1 = jnp.where(first, other, total)
    both = jnp.stack([half0, half1], axis=1)
    window = both[:WIN].reshape(WIN, 2, 1024)
    gain_tile = both[WIN + 5, 0] + both[WIN + 5, 1]
    small = both[WIN:].at[4, 1].set(gain_tile).reshape(6, 2, 1024)
    follow = jnp.stack([next0, next1], axis=1).reshape(6, 2, 1024)
    follow = jnp.where(chip == 127, small, follow)
    pairs = jnp.concatenate([window, follow], axis=0)
    as_lift = pairs.reshape(18, 2048)
    as_proj = pairs.reshape(18, 2, 2, 512).transpose(0, 2, 1, 3).reshape(18, 2048)
    number = chip * WIN + jnp.arange(18, dtype=jnp.int32)
    proj = (number >= 1024) & (number < 1536)
    flat = jnp.where(proj[:, None], as_proj, as_lift).reshape(-1)
    begin = (2 * chip + core) * chunk - chip * (WIN * 2048)
    return lax.dynamic_slice(flat, (begin,), (chunk,)) * grad_scale


def pair_swap(array):
    return lax.ppermute(array, "c", [(0, 1), (1, 0)])


ROWS = 384
EDGE = 16
LONG = ROWS + 2 * EDGE


def inside(info_ref, first, shape):
    at = info_ref[0] + first + lax.broadcasted_iota(jnp.int32, shape, 0)
    return (at >= 0) & (at < info_ref[1])


def sweep(begin, count, step, body):
    def one(i, _):
        body(pl.multiple_of(begin + i * step, 8))
        return 0

    lax.fori_loop(0, count, one, 0)


def main_kernel(info_ref, gain_ref, taps_ref, xh, gh, beforeh, afterh, wh, pwh, *rest):
    normed_o, act_o, both_o, keep_o, give_o, gb_keep_o, gb_give_o, kern_o = rest[:8]
    xs, gs, w, pw, nm, act, both, val, sig, gat, gact, gcon, acf, kacc, sem, sem_out = rest[8:]
    pairs = [
        (xh, xs.at[pl.ds(EDGE, ROWS)]),
        (beforeh.at[0], xs.at[pl.ds(0, EDGE)]),
        (afterh.at[0], xs.at[pl.ds(EDGE + ROWS, EDGE)]),
        (gh, gs.at[pl.ds(EDGE, ROWS)]),
        (beforeh.at[1], gs.at[pl.ds(0, EDGE)]),
        (afterh.at[1], gs.at[pl.ds(EDGE + ROWS, EDGE)]),
    ]
    for n in range(4):
        pairs.append((wh.at[:, pl.ds(256 * n, 256)], w.at[:, pl.ds(256 * n, 256)]))
        pairs.append((wh.at[:, pl.ds(1024 + 256 * n, 256)], w.at[:, pl.ds(1024 + 256 * n, 256)]))
        pairs.append((pwh.at[pl.ds(256 * n, 256)], pw.at[pl.ds(256 * n, 256)]))
    loads = [pltpu.make_async_copy(src, dst, sem.at[i]) for i, (src, dst) in enumerate(pairs)]
    for load in loads:
        load.start()
    for load in loads[:6]:
        load.wait()

    def norm_rows(r):
        rows = pl.ds(r, 32)
        values = xs[rows, :].astype(F32)
        center = values - jnp.mean(values, axis=-1, keepdims=True)
        scale = lax.rsqrt(jnp.mean(center * center, axis=-1, keepdims=True) + eps_norm)
        nm[rows, :] = (center * scale * gain_ref[...]).astype(BF)
        gs[rows, :] = jnp.where(inside(info_ref, r - EDGE, (32, 1024)), gs[rows, :].astype(F32), 0.0).astype(BF)

    def norm_step(i, _):
        norm_rows(pl.multiple_of(i * 32, 32))
        return 0

    lax.fori_loop(0, LONG // 32, norm_step, 0)
    zeros = jnp.zeros((16, 128), F32)
    for n in range(4):
        for load in loads[6 + 3 * n : 9 + 3 * n]:
            load.wait()
        lanes = slice(256 * n, 256 * n + 256)
        lift_value = jnp.dot(nm[...], w[:, lanes], preferred_element_type=F32)
        lift_gate = jnp.dot(nm[...], w[:, 1024 + 256 * n : 1280 + 256 * n], preferred_element_type=F32)
        back = lax.dot_general(gs[...], pw[lanes, :], (((1,), (1,)), ((), ())), preferred_element_type=F32)
        for h in range(2):
            val[h] = lift_value[:, 128 * h : 128 * h + 128]
            sig[h] = lift_gate[:, 128 * h : 128 * h + 128]
            gact[h] = back[:, 128 * h : 128 * h + 128]
        for h in range(2):
            at = 256 * n + 128 * h
            taps = [taps_ref[k : k + 1, at : at + 128] for k in range(9)]

            def gate_rows(r, h=h):
                rows = pl.ds(r, 80)
                s = jax.nn.sigmoid(sig[h, rows, :])
                sig[h, rows, :] = s
                gated = jnp.where(inside(info_ref, r - EDGE, (80, 128)), val[h, rows, :] * s, 0.0)
                gat[rows, :] = gated.astype(BF).astype(F32)

            def conv_rows(r, h=h, taps=taps):
                conv = taps[0] * gat[pl.ds(r - 4, 56), :]
                for k in range(1, 9):
                    conv = conv + taps[k] * gat[pl.ds(r + k - 4, 56), :]
                s = jax.nn.sigmoid(conv)
                rows = pl.ds(r, 56)
                acf[rows, :] = conv * s
                grad = gact[h, rows, :] * s * (1.0 + conv * (1.0 - s))
                gcon[rows, :] = grad.astype(BF).astype(F32)

            def back_rows(r, h=h, taps=taps, at=at):
                rows = pl.ds(r, 64)
                own = pl.ds(pl.multiple_of(r - EDGE, 16), 64)
                grad = taps[0] * gcon[pl.ds(r + 4, 64), :]
                for k in range(1, 9):
                    grad = grad + taps[k] * gcon[pl.ds(r + 4 - k, 64), :]
                grad = jnp.where(inside(info_ref, r - EDGE, (64, 128)), grad, 0.0)
                s = sig[h, rows, :]
                first = grad * s
                both[0, own, at : at + 128] = first.astype(BF)
                both[1, own, at : at + 128] = (first * val[h, rows, :] * (1.0 - s)).astype(BF)
                act[own, at : at + 128] = acf[rows, :].astype(BF)
                here = gcon[rows, :]
                for k in range(9):
                    product = here * gat[pl.ds(r + k - 4, 64), :]
                    kacc[k] += jnp.sum(product.reshape(8, 8, 128), axis=0)

            kacc[...] = jnp.zeros((9, 8, 128), F32)
            sweep(8, 5, 80, gate_rows)
            lax.fori_loop(0, 7, lambda i, c: (conv_rows(12 + i * 56), c)[1], 0)
            sweep(EDGE, 6, 64, back_rows)
            for k in range(9):
                kern_o[k : k + 1, at : at + 128] = jnp.sum(kacc[k], axis=0, keepdims=True)
    core = info_ref[2]
    sends = [
        (nm.at[pl.ds(EDGE, ROWS)], normed_o),
        (act, act_o),
        (both, both_o),
        (both.at[core], keep_o),
        (both.at[1 - core], give_o),
        (gs.at[pl.ds(EDGE, ROWS), pl.ds(core * 512, 512)], gb_keep_o),
        (gs.at[pl.ds(EDGE, ROWS), pl.ds(512 - core * 512, 512)], gb_give_o),
    ]
    sends = [pltpu.make_async_copy(src, dst, sem_out.at[i]) for i, (src, dst) in enumerate(sends)]
    for copy in sends:
        copy.start()
    for copy in sends:
        copy.wait()


def forward_backward(info, gain, taps, x, g, before, after, w, pw):
    wide = jax.ShapeDtypeStruct((ROWS, 1024), BF)
    half = jax.ShapeDtypeStruct((ROWS, 512), BF)
    return pl.pallas_call(
        main_kernel,
        out_shape=[
            wide, wide, jax.ShapeDtypeStruct((2, ROWS, 1024), BF), wide, wide, half, half,
            jax.ShapeDtypeStruct((9, 1024), F32),
        ],
        in_specs=[smem_spec(), vmem_spec(), vmem_spec()] + [any_spec()] * 6,
        out_specs=[any_spec()] * 7 + [vmem_spec()],
        scratch_shapes=[
            pltpu.VMEM((LONG, 1024), BF),
            pltpu.VMEM((LONG, 1024), BF),
            pltpu.VMEM((1024, 2048), BF),
            pltpu.VMEM((1024, 1024), BF),
            pltpu.VMEM((LONG, 1024), BF),
            pltpu.VMEM((ROWS, 1024), BF),
            pltpu.VMEM((2, ROWS, 1024), BF),
            pltpu.VMEM((2, LONG, 128), F32),
            pltpu.VMEM((2, LONG, 128), F32),
            pltpu.VMEM((LONG, 128), F32),
            pltpu.VMEM((2, LONG, 128), F32),
            pltpu.VMEM((LONG, 128), F32),
            pltpu.VMEM((LONG, 128), F32),
            pltpu.VMEM((9, 8, 128), F32),
            pltpu.SemaphoreType.DMA((18,)),
            pltpu.SemaphoreType.DMA((7,)),
        ],
        name="forward_backward",
    )(info, gain, taps, x, g, before, after, w, pw)


def outputs_kernel(info_ref, gain_ref, xh, gh, acth, bothh, wh, pwh, after_this, out_o, grad_o, *rest):
    x, g, act, both, w, pw, sem, sem_out = rest
    pairs = [(acth, act), (pwh, pw), (xh, x), (bothh, both), (wh, w), (gh, g)]
    loads = [pltpu.make_async_copy(src, dst, sem.at[i]) for i, (src, dst) in enumerate(pairs)]
    for load in loads:
        load.start()
    for load in loads[:3]:
        load.wait()
    contract = (((1,), (1,)), ((), ()))
    for i in range(3):
        rows = slice(128 * i, 128 * i + 128)
        branch = jnp.dot(act[rows, :], pw[...], preferred_element_type=F32)
        branch = jnp.where(inside(info_ref, 128 * i, (128, 1024)), branch, 0.0)
        act[rows, :] = (x[rows, :].astype(F32) + branch).astype(BF)
    first = pltpu.make_async_copy(act, out_o, sem_out.at[0])
    first.start()
    for load in loads[3:]:
        load.wait()
    for i in range(3):
        rows = slice(128 * i, 128 * i + 128)
        grad = lax.dot_general(both[0, rows, :], w[:, :1024], contract, preferred_element_type=F32)
        grad = grad + lax.dot_general(both[1, rows, :], w[:, 1024:], contract, preferred_element_type=F32)
        u = grad * gain_ref[...]
        values = x[rows, :].astype(F32)
        center = values - jnp.mean(values, axis=-1, keepdims=True)
        scale = lax.rsqrt(jnp.mean(center * center, axis=-1, keepdims=True) + eps_norm)
        xhat = center * scale
        u = scale * (u - jnp.mean(u, axis=-1, keepdims=True) - xhat * jnp.mean(u * xhat, axis=-1, keepdims=True))
        g[rows, :] = (g[rows, :].astype(F32) + u).astype(BF)
    second = pltpu.make_async_copy(g, grad_o, sem_out.at[1])
    second.start()
    first.wait()
    second.wait()


def outputs(info, gain, x, g, act, both, w, pw, after_this):
    wide = jax.ShapeDtypeStruct((ROWS, 1024), BF)
    return pl.pallas_call(
        outputs_kernel,
        out_shape=[wide, wide],
        in_specs=[smem_spec(), vmem_spec()] + [any_spec()] * 7,
        out_specs=[any_spec()] * 2,
        scratch_shapes=[
            pltpu.VMEM((ROWS, 1024), BF),
            pltpu.VMEM((ROWS, 1024), BF),
            pltpu.VMEM((ROWS, 1024), BF),
            pltpu.VMEM((2, ROWS, 1024), BF),
            pltpu.VMEM((1024, 2048), BF),
            pltpu.VMEM((1024, 1024), BF),
            pltpu.SemaphoreType.DMA((6,)),
            pltpu.SemaphoreType.DMA((2,)),
        ],
        name="outputs",
    )(info, gain, x, g, act, both, w, pw, after_this)


def local(features, cotangent, lengths, norm_gain, lift_weight, conv_kernel, proj_weight):
    x, g = features[0], cotangent[0]
    frames, width = x.shape
    core = lax.axis_index("c")
    edge = jnp.stack([x[-EDGE:], g[-EDGE:]])
    start = jnp.stack([x[:EDGE], g[:EDGE]])
    before = lax.ppermute(edge, ("yh", "x"), [(i, i + 1) for i in range(7)])
    after = lax.ppermute(start, ("yh", "x"), [(i + 1, i) for i in range(7)])
    first_row = lax.axis_index(("yh", "x")) * frames
    info = jnp.stack([first_row, lengths[0], core]).astype(jnp.int32)
    gain = norm_gain[None]
    normed, activated, both, keep, give, gb_keep, gb_give, term_kernel = forward_backward(
        info, gain, conv_kernel, x, g, before, after, lift_weight, proj_weight
    )
    mine = core == 0
    normed_other = pair_swap(normed)
    keep_other = pair_swap(give)
    act_other = pair_swap(activated)
    gb_other = pair_swap(gb_give)
    small = jnp.concatenate([term_kernel, jnp.zeros((1, width), F32)]).reshape(5, 2, 8, 128)
    small_keep = jnp.where(mine, small[:, 0], small[:, 1])
    small_give = jnp.where(mine, small[:, 1], small[:, 0])
    kernel_tiles = (small_keep + pair_swap(small_give)).reshape(40, 128)
    position = jnp.stack([lax.axis_index("x"), lax.axis_index(("yh", "yl")), core]).astype(jnp.int32)
    operands = (normed, normed_other, keep, keep_other, activated, act_other, gb_keep, gb_other, lift_weight)
    blocks = weight_blocks(position, gain, kernel_tiles, operands)
    cover = outputs(info, gain, x, g, activated, both, lift_weight, proj_weight, blocks[0])
    total = reduce_terms(position, blocks, cover)
    chunk = (2 * width * width + width * width + 10 * width) // 256
    grads = own_chunk(total, chunk, float(frames * 256) ** (-0.5))
    return cover[0][None], cover[1][None], grads


def solution(mesh):
    fine = Mesh(mesh.devices.reshape(2, 4, 8, 2, 2), ALL)
    act = P(("z", "yl", "c"), ("yh", "x"), None)
    return jax.shard_map(
        local,
        mesh=fine,
        in_specs=(act, act, P(("z", "yl", "c")), P(), P(), P(), P()),
        out_specs=(act, act, P(ALL)),
        check_vma=False,
    )
```

```python
import jax
import jax.numpy as jnp
from jax import lax
from jax.experimental import pallas as pl
from jax.experimental.pallas import tpu as pltpu
from jax.sharding import Mesh, PartitionSpec as P

eps_norm = 1e-05
BF = jnp.bfloat16
F32 = jnp.float32
WIN = 12


def any_spec():
    return pl.BlockSpec(memory_space=pl.ANY)


def hbm_spec():
    return pl.BlockSpec(memory_space=pltpu.HBM)


def vmem_spec():
    return pl.BlockSpec(memory_space=pltpu.VMEM)


def smem_spec():
    return pl.BlockSpec(memory_space=pltpu.SMEM)


def place(part_a, part_b, wide, begin, count):
    at = 0
    while at < count:
        window, inside = divmod(begin + at, 96)
        low = inside % 48
        step = min(48 - low, count - at)
        rows = wide[at : at + step, :].astype(BF)
        yh, rest = divmod(window, 64)
        if inside < 48:
            part_a[yh, rest, low : low + step, :] = rows
        else:
            part_b[yh * 2 + rest % 2, rest // 2, low : low + step, :] = rows
        at += step


def weight_kernel(place_ref, gain_ref, n0h, n1h, k0h, k1h, a0h, a1h, g0h, g1h, wh, *rest):
    outs, rest = rest[:8], rest[8:]
    n0, n1, k0, k1, a0, a1, g0, g1, w, part_a, part_b, wide, extra, sem, sem_in = rest
    core = place_ref[2]
    loads = [
        pltpu.make_async_copy(src, dst, sem_in.at[i])
        for i, (src, dst) in enumerate(
            zip(
                (a0h, g0h, a1h, g1h, n0h, k0h, n1h, k1h, wh.at[:, pl.ds(core * 1024, 1024)]),
                (a0, g0, a1, g1, n0, k0, n1, k1, w),
            )
        )
    ]
    for load in loads:
        load.start()
    contract = (((0,), (0,)), ((), ()))
    for load in loads[:4]:
        load.wait()
    for m in range(4):
        cols = slice(256 * m, 256 * m + 256)
        done = lax.dot_general(a0[:, cols], g0[...], contract, preferred_element_type=F32)
        done = done + lax.dot_general(a1[:, cols], g1[...], contract, preferred_element_type=F32)
        for v in range(4):
            wide[pl.ds(v, 256, stride=4), :] = done[:, 128 * v : 128 * v + 128]
        place(part_a, part_b, wide, 8192 + 1024 * m, 1024)
    for load in loads[4:]:
        load.wait()
    gains = []
    for m in range(4):
        cols = slice(256 * m, 256 * m + 256)
        done = lax.dot_general(n0[:, cols], k0[0:ROWS, :], contract, preferred_element_type=F32)
        done = done + lax.dot_general(n1[:, cols], k1[0:ROWS, :], contract, preferred_element_type=F32)
        folded = jnp.zeros((256, 128), F32)
        for v in range(8):
            piece = done[:, 128 * v : 128 * v + 128]
            wide[pl.ds(v, 256, stride=8), :] = piece
            folded = folded + piece * w[cols, 128 * v : 128 * v + 128].astype(F32)
        gains.append(jnp.sum(folded.T, axis=0, keepdims=True))
        place(part_a, part_b, wide, 2048 * m, 2048)
    for m in range(4):
        for j in range(2):
            at = 256 * m + 128 * j
            extra[40 + 2 * m + j : 41 + 2 * m + j, :] = gains[m][:, 128 * j : 128 * j + 128] / gain_ref[:, at : at + 128]
    taps = k0[ROWS:, :].astype(F32) + k1[ROWS:, :].astype(F32)
    for p in range(5):
        for v in range(8):
            extra[8 * p + v : 8 * p + v + 1, :] = taps[p : p + 1, 128 * v : 128 * v + 128]
    small = part_b.at[4, 0]
    small[...] = extra[...].astype(BF)
    copies = []
    for s in range(4):
        x = (place_ref[0] + s) % 4
        y = (place_ref[1] + s) % 4
        for yh in range(2):
            copies.append((part_a.at[yh, pl.ds(x * 16, 16)], outs[s].at[pl.ds(yh * 16, 16)]))
        copies.append((small, outs[s].at[32]))
        copies.append((part_b.at[y], outs[4 + s]))
    copies = [pltpu.make_async_copy(src, dst, sem.at[i]) for i, (src, dst) in enumerate(copies)]
    for copy in copies:
        copy.start()
    for copy in copies:
        copy.wait()


def weight_blocks(position, gain, operands):
    blocks = [jax.ShapeDtypeStruct((33, 48, 128), BF)] * 4 + [jax.ShapeDtypeStruct((32, 48, 128), BF)] * 4
    return pl.pallas_call(
        weight_kernel,
        out_shape=blocks,
        in_specs=[smem_spec(), vmem_spec()] + [hbm_spec(), any_spec()] * 4 + [hbm_spec()],
        out_specs=[hbm_spec()] * 8,
        scratch_shapes=[pltpu.VMEM(o.shape, BF) for o in operands[:8]]
        + [
            pltpu.VMEM((1024, 1024), BF),
            pltpu.VMEM((2, 64, 48, 128), BF),
            pltpu.VMEM((5, 32, 48, 128), BF),
            pltpu.VMEM((2048, 128), F32),
            pltpu.VMEM((48, 128), F32),
            pltpu.SemaphoreType.DMA((16,)),
            pltpu.SemaphoreType.DMA((9,)),
        ],
        name="weight_grads",
    )(position, gain, *operands)


def sum_of(refs, index):
    total = refs[0][index].astype(F32)
    for ref in refs[1:]:
        total = total + ref[index].astype(F32)
    return total.astype(BF)


def first_x_kernel(place_ref, i0, i1, i2, i3, mark, *outs):
    for s in range(4):
        y = (place_ref[1] + s) % 4
        base = (y // 2) * 16 + y % 2
        for z in range(8):
            outs[s][z] = sum_of((i0, i1, i2, i3), base + 2 * z)
        outs[s][8] = sum_of((i0, i1, i2, i3), 32)


def first_y_kernel(place_ref, i0, i1, i2, i3, *outs):
    for s in range(4):
        x = (place_ref[0] + s) % 4
        for z in range(8):
            outs[s][z] = sum_of((i0, i1, i2, i3), x * 8 + z)


def second_kernel(place_ref, a0, a1, a2, a3, b0, b1, b2, b3, out):
    small = sum_of((a0, a1, a2, a3), 8)
    for z in range(8):
        out[z, 0:48, :] = sum_of((a0, a1, a2, a3), z)
        out[z, 48:96, :] = sum_of((b0, b1, b2, b3), z)
        out[z, 96:144, :] = small


def send(blocks, axes):
    n = 4
    got = [blocks[0]]
    for step in (2, 1, 3):
        got.append(lax.ppermute(blocks[step], axes, [(i, (i + step) % n) for i in range(n)]))
    return got


def reduce_terms(position, blocks, mark):
    got_x = send(blocks[:4], "x")
    got_y = send(blocks[4:], ("yh", "yl"))
    block9 = jax.ShapeDtypeStruct((9, 48, 128), BF)
    block8 = jax.ShapeDtypeStruct((8, 48, 128), BF)
    after_x = pl.pallas_call(
        first_x_kernel,
        out_shape=[block9] * 4,
        in_specs=[smem_spec()] + [vmem_spec()] * 5,
        out_specs=[vmem_spec()] * 4,
        compiler_params=pltpu.CompilerParams(vmem_limit_bytes=8 << 20),
        name="sum_after_x",
    )(position, *got_x, mark)
    after_y = pl.pallas_call(
        first_y_kernel,
        out_shape=[block8] * 4,
        in_specs=[smem_spec()] + [vmem_spec()] * 4,
        out_specs=[vmem_spec()] * 4,
        compiler_params=pltpu.CompilerParams(vmem_limit_bytes=8 << 20),
        name="sum_after_y",
    )(position, *got_y)
    got_a = send(after_x, ("yh", "yl"))
    got_b = send(after_y, "x")
    ready = pl.pallas_call(
        second_kernel,
        out_shape=jax.ShapeDtypeStruct((8, 144, 128), BF),
        in_specs=[smem_spec()] + [vmem_spec()] * 8,
        out_specs=vmem_spec(),
        compiler_params=pltpu.CompilerParams(vmem_limit_bytes=6 << 20),
        name="sum_before_z",
    )(position, *got_a, *got_b)
    swapped = lax.all_to_all(ready, "z", split_axis=0, concat_axis=0, tiled=True)
    return swapped.astype(F32).sum(axis=0).reshape(18, 8, 128)


ALL = ("yh", "x", "z", "yl", "c")


def own_chunk(total, core, chip, begin, chunk, grad_scale):
    other = lax.ppermute(total, "c", [(0, 1), (1, 0)])
    head = total[:6]
    next0 = lax.ppermute(head, ALL, [(2 * j, 2 * j - 1) for j in range(1, 128)])
    next1 = lax.ppermute(head, ALL, [(2 * j + 1, 2 * j - 1) for j in range(1, 128)])
    first = core == 0
    half0 = jnp.where(first, total, other)
    half1 = jnp.where(first, other, total)
    both = jnp.stack([half0, half1], axis=1)
    window = both[:WIN].reshape(WIN, 2, 1024)
    gain_tile = both[WIN + 5, 0] + both[WIN + 5, 1]
    small = both[WIN:].at[4, 1].set(gain_tile).reshape(6, 2, 1024)
    follow = jnp.stack([next0, next1], axis=1).reshape(6, 2, 1024)
    follow = jnp.where(chip == 127, small, follow)
    pairs = jnp.concatenate([window, follow], axis=0)
    as_lift = pairs.reshape(18, 2048)
    as_proj = pairs.reshape(18, 2, 2, 512).transpose(0, 2, 1, 3).reshape(18, 2048)
    number = chip * WIN + jnp.arange(18, dtype=jnp.int32)
    proj = (number >= 1024) & (number < 1536)
    flat = jnp.where(proj[:, None], as_proj, as_lift).reshape(-1)
    return lax.dynamic_slice(flat, (begin,), (chunk,)) * grad_scale


def pair_swap(array):
    return lax.ppermute(array, "c", [(0, 1), (1, 0)])


ROWS = 384
EDGE = 16
LONG = ROWS + 2 * EDGE


def inside(info_ref, first, shape):
    at = info_ref[0] + first + lax.broadcasted_iota(jnp.int32, shape, 0)
    return (at >= 0) & (at < info_ref[1])


def main_kernel(info_ref, gain_ref, taps_ref, xh, gh, beforeh, afterh, wh, pwh, *rest):
    normed_o, act_o, both_o, keep_o, give_o, gb_keep_o, gb_give_o = rest[:7]
    xs, gs, w, pw, nm, act, both, lifts0, lifts1, gat, gcon, acf, mask, krows, sem, sem_out = rest[7:]
    pairs = [
        (xh, xs.at[pl.ds(EDGE, ROWS)]),
        (beforeh.at[0], xs.at[pl.ds(0, EDGE)]),
        (afterh.at[0], xs.at[pl.ds(EDGE + ROWS, EDGE)]),
        (gh, gs.at[pl.ds(EDGE, ROWS)]),
        (beforeh.at[1], gs.at[pl.ds(0, EDGE)]),
        (afterh.at[1], gs.at[pl.ds(EDGE + ROWS, EDGE)]),
    ]
    for n in range(4):
        pairs.append((wh.at[:, pl.ds(256 * n, 256)], w.at[:, pl.ds(256 * n, 256)]))
        pairs.append((wh.at[:, pl.ds(1024 + 256 * n, 256)], w.at[:, pl.ds(1024 + 256 * n, 256)]))
        pairs.append((pwh.at[pl.ds(256 * n, 256)], pw.at[pl.ds(256 * n, 256)]))
    loads = [pltpu.make_async_copy(src, dst, sem.at[i]) for i, (src, dst) in enumerate(pairs)]
    for load in loads:
        load.start()
    mask[...] = inside(info_ref, -EDGE, (LONG, 128)).astype(F32)
    krows[...] = jnp.zeros((2, 16, 1024), F32)
    for load in loads[:6]:
        load.wait()

    def norm_step(i, _):
        r = pl.multiple_of(i * 32, 32)
        rows = pl.ds(r, 32)
        values = xs[rows, :].astype(F32)
        center = values - jnp.mean(values, axis=-1, keepdims=True)
        scale = lax.rsqrt(jnp.mean(center * center, axis=-1, keepdims=True) + eps_norm)
        nm[rows, :] = (center * scale * gain_ref[...]).astype(BF)
        gs[rows, :] = jnp.where(inside(info_ref, r - EDGE, (32, 1024)), gs[rows, :].astype(F32), 0.0).astype(BF)
        return 0

    lax.fori_loop(0, LONG // 32, norm_step, 0)

    def multiply(n, lifts):
        for load in loads[6 + 3 * n : 9 + 3 * n]:
            load.wait()
        lanes = slice(256 * n, 256 * n + 256)
        lift_value = jnp.dot(nm[...], w[:, lanes], preferred_element_type=F32)
        lift_gate = jnp.dot(nm[...], w[:, 1024 + 256 * n : 1280 + 256 * n], preferred_element_type=F32)
        back = lax.dot_general(gs[...], pw[lanes, :], (((1,), (1,)), ((), ())), preferred_element_type=F32)
        for h in range(2):
            lifts[h] = lift_value[:, 128 * h : 128 * h + 128]
            lifts[2 + h] = lift_gate[:, 128 * h : 128 * h + 128]
            lifts[4 + h] = back[:, 128 * h : 128 * h + 128]

    def channels(n, h, lifts):
        at = 256 * n + 128 * h
        taps = [taps_ref[k : k + 1, at : at + 128] for k in range(9)]
        for i in range(10):
            rows = pl.ds(8 + 40 * i, 40)
            s = jax.nn.sigmoid(lifts[2 + h, rows, :])
            lifts[2 + h, rows, :] = s
            gat[h, rows, :] = (lifts[h, rows, :] * s * mask[rows, :]).astype(BF).astype(F32)
        for i in range(7):
            r = 12 + 56 * i
            rows = pl.ds(r, 56)
            conv = taps[0] * gat[h, pl.ds(r - 4, 56), :]
            for k in range(1, 9):
                conv = conv + taps[k] * gat[h, pl.ds(r + k - 4, 56), :]
            s = jax.nn.sigmoid(conv)
            acf[h, rows, :] = conv * s
            grad = lifts[4 + h, rows, :] * s * (1.0 + conv * (1.0 - s))
            gcon[h, rows, :] = grad.astype(BF).astype(F32)
        sums = [jnp.zeros((8, 128), F32) for _ in range(9)]
        for i in range(8):
            r = EDGE + 48 * i
            rows = pl.ds(r, 48)
            own = pl.ds(r - EDGE, 48)
            grad = taps[0] * gcon[h, pl.ds(r + 4, 48), :]
            for k in range(1, 9):
                grad = grad + taps[k] * gcon[h, pl.ds(r + 4 - k, 48), :]
            s = lifts[2 + h, rows, :]
            first = grad * mask[rows, :] * s
            both[0, own, at : at + 128] = first.astype(BF)
            both[1, own, at : at + 128] = (first * lifts[h, rows, :] * (1.0 - s)).astype(BF)
            act[own, at : at + 128] = acf[h, rows, :].astype(BF)
            here = gcon[h, rows, :]
            for k in range(9):
                product = here * gat[h, pl.ds(r + k - 4, 48), :]
                sums[k] = sums[k] + jnp.sum(product.reshape(6, 8, 128), axis=0)
        for k in range(9):
            krows[k % 2, k // 2 : k // 2 + 1, at : at + 128] = jnp.sum(sums[k], axis=0, keepdims=True)

    lifts = (lifts0, lifts1)
    multiply(0, lifts0)
    for n in range(4):
        if n < 3:
            multiply(n + 1, lifts[(n + 1) % 2])
        for h in range(2):
            channels(n, h, lifts[n % 2])
    core = info_ref[2]
    for c in range(2):
        both[c, ROWS:, :] = krows[c].astype(BF)
    sends = [
        (both.at[1 - core], give_o),
        (act, act_o),
        (nm.at[pl.ds(EDGE, ROWS)], normed_o),
        (gs.at[pl.ds(EDGE, ROWS), pl.ds(512 - core * 512, 512)], gb_give_o),
        (gs.at[pl.ds(EDGE, ROWS), pl.ds(core * 512, 512)], gb_keep_o),
        (both.at[core], keep_o),
        (both, both_o),
    ]
    sends = [pltpu.make_async_copy(src, dst, sem_out.at[i]) for i, (src, dst) in enumerate(sends)]
    for copy in sends:
        copy.start()
    for copy in sends:
        copy.wait()


def forward_backward(info, gain, taps, x, g, before, after, w, pw):
    wide = jax.ShapeDtypeStruct((ROWS, 1024), BF)
    tall = jax.ShapeDtypeStruct((ROWS + 16, 1024), BF)
    half = jax.ShapeDtypeStruct((ROWS, 512), BF)
    return pl.pallas_call(
        main_kernel,
        out_shape=[wide, wide, jax.ShapeDtypeStruct((2, ROWS + 16, 1024), BF), tall, tall, half, half],
        in_specs=[smem_spec(), vmem_spec(), vmem_spec()] + [hbm_spec()] * 6,
        out_specs=[hbm_spec()] * 7,
        scratch_shapes=[
            pltpu.VMEM((LONG, 1024), BF),
            pltpu.VMEM((LONG, 1024), BF),
            pltpu.VMEM((1024, 2048), BF),
            pltpu.VMEM((1024, 1024), BF),
            pltpu.VMEM((LONG, 1024), BF),
            pltpu.VMEM((ROWS, 1024), BF),
            pltpu.VMEM((2, ROWS + 16, 1024), BF),
            pltpu.VMEM((6, LONG, 128), F32),
            pltpu.VMEM((6, LONG, 128), F32),
            pltpu.VMEM((2, LONG, 128), F32),
            pltpu.VMEM((2, LONG, 128), F32),
            pltpu.VMEM((2, LONG, 128), F32),
            pltpu.VMEM((LONG, 128), F32),
            pltpu.VMEM((2, 16, 1024), F32),
            pltpu.SemaphoreType.DMA((18,)),
            pltpu.SemaphoreType.DMA((7,)),
        ],
        name="forward_backward",
    )(info, gain, taps, x, g, before, after, w, pw)


def outputs_kernel(info_ref, gain_ref, xh, gh, acth, bothh, wh, pwh, after_this, out_o, grad_o, mark_o, *rest):
    mark_o[...] = jnp.zeros((8, 128), F32)
    x, g, act, both, w, pw, sem, sem_out = rest
    pairs = [(acth, act), (pwh, pw), (xh, x), (bothh, both), (wh, w), (gh, g)]
    loads = [pltpu.make_async_copy(src, dst, sem.at[i]) for i, (src, dst) in enumerate(pairs)]
    for load in loads:
        load.start()
    for load in loads[:3]:
        load.wait()
    contract = (((1,), (1,)), ((), ()))
    for i in range(3):
        rows = slice(128 * i, 128 * i + 128)
        branch = jnp.dot(act[rows, :], pw[...], preferred_element_type=F32)
        branch = jnp.where(inside(info_ref, 128 * i, (128, 1024)), branch, 0.0)
        act[rows, :] = (x[rows, :].astype(F32) + branch).astype(BF)
    first = pltpu.make_async_copy(act, out_o, sem_out.at[0])
    first.start()
    for load in loads[3:]:
        load.wait()
    for i in range(3):
        rows = slice(128 * i, 128 * i + 128)
        grad = lax.dot_general(both[0, rows, :], w[:, :1024], contract, preferred_element_type=F32)
        grad = grad + lax.dot_general(both[1, rows, :], w[:, 1024:], contract, preferred_element_type=F32)
        u = grad * gain_ref[...]
        values = x[rows, :].astype(F32)
        center = values - jnp.mean(values, axis=-1, keepdims=True)
        scale = lax.rsqrt(jnp.mean(center * center, axis=-1, keepdims=True) + eps_norm)
        xhat = center * scale
        u = scale * (u - jnp.mean(u, axis=-1, keepdims=True) - xhat * jnp.mean(u * xhat, axis=-1, keepdims=True))
        g[rows, :] = (g[rows, :].astype(F32) + u).astype(BF)
    second = pltpu.make_async_copy(g, grad_o, sem_out.at[1])
    second.start()
    first.wait()
    second.wait()


def outputs(info, gain, x, g, act, both, w, pw, after_this):
    wide = jax.ShapeDtypeStruct((ROWS, 1024), BF)
    return pl.pallas_call(
        outputs_kernel,
        out_shape=[wide, wide, jax.ShapeDtypeStruct((8, 128), F32)],
        in_specs=[smem_spec(), vmem_spec()] + [hbm_spec()] * 7,
        out_specs=[hbm_spec()] * 2 + [vmem_spec()],
        scratch_shapes=[
            pltpu.VMEM((ROWS, 1024), BF),
            pltpu.VMEM((ROWS, 1024), BF),
            pltpu.VMEM((ROWS, 1024), BF),
            pltpu.VMEM((2, ROWS + 16, 1024), BF),
            pltpu.VMEM((1024, 2048), BF),
            pltpu.VMEM((1024, 1024), BF),
            pltpu.SemaphoreType.DMA((6,)),
            pltpu.SemaphoreType.DMA((2,)),
        ],
        name="outputs",
    )(info, gain, x, g, act, both, w, pw, after_this)


def local(features, cotangent, lengths, norm_gain, lift_weight, conv_kernel, proj_weight):
    x, g = features[0], cotangent[0]
    frames, width = x.shape
    core = lax.axis_index("c")
    edge = jnp.stack([x[-EDGE:], g[-EDGE:]])
    start = jnp.stack([x[:EDGE], g[:EDGE]])
    before = lax.ppermute(edge, ("yh", "x"), [(i, i + 1) for i in range(7)])
    after = lax.ppermute(start, ("yh", "x"), [(i + 1, i) for i in range(7)])
    first_row = lax.axis_index(("yh", "x")) * frames
    info = jnp.stack([first_row, lengths[0], core]).astype(jnp.int32)
    gain = norm_gain[None]
    normed, activated, both, keep, give, gb_keep, gb_give = forward_backward(
        info, gain, conv_kernel, x, g, before, after, lift_weight, proj_weight
    )
    keep_other = pair_swap(give)
    act_other = pair_swap(activated)
    normed_other = pair_swap(normed)
    gb_other = pair_swap(gb_give)
    chunk = (2 * width * width + width * width + 10 * width) // 256
    chip = lax.axis_index(("yh", "x", "z", "yl"))
    begin = (2 * chip + core) * chunk - chip * (WIN * 2048)
    position = jnp.stack([lax.axis_index("x"), lax.axis_index(("yh", "yl")), core, chip, begin]).astype(jnp.int32)
    operands = (normed, normed_other, keep, keep_other, activated, act_other, gb_keep, gb_other, lift_weight)
    blocks = weight_blocks(position, gain, operands)
    output, grad_features, mark = outputs(info, gain, x, g, activated, both, lift_weight, proj_weight, blocks[0])
    total = reduce_terms(position, blocks, mark)
    grads = own_chunk(total, core, chip, begin, chunk, float(frames * 256) ** (-0.5))
    return output[None], grad_features[None], grads


def solution(mesh):
    fine = Mesh(mesh.devices.reshape(2, 4, 8, 2, 2), ALL)
    act = P(("z", "yl", "c"), ("yh", "x"), None)
    return jax.shard_map(
        local,
        mesh=fine,
        in_specs=(act, act, P(("z", "yl", "c")), P(), P(), P(), P()),
        out_specs=(act, act, P(ALL)),
        check_vma=False,
    )
```

```python
import functools

import jax
import jax.numpy as jnp
from jax import lax
from jax.experimental import pallas as pl
from jax.experimental.pallas import tpu as pltpu
from jax.sharding import Mesh, PartitionSpec as P


eps_norm = 1e-05
BF = jnp.bfloat16
F32 = jnp.float32
WIN = 12


def any_spec():
    return pl.BlockSpec(memory_space=pl.ANY)


def hbm_spec():
    return pl.BlockSpec(memory_space=pltpu.HBM)


def vmem_spec():
    return pl.BlockSpec(memory_space=pltpu.VMEM)


def smem_spec():
    return pl.BlockSpec(memory_space=pltpu.SMEM)


def place(part_a, part_b, wide, begin, count):
    at = 0
    while at < count:
        window, inside = divmod(begin + at, 96)
        low = inside % 48
        step = min(48 - low, count - at)
        rows = wide[at : at + step, :].astype(BF)
        yh, rest = divmod(window, 64)
        if inside < 48:
            part_a[yh, rest, low : low + step, :] = rows
        else:
            part_b[yh * 2 + rest % 2, rest // 2, low : low + step, :] = rows
        at += step


def weight_kernel(gain_ref, n0h, n1h, k0h, k1h, a0h, a1h, g0h, g1h, wh, *rest):
    outs, rest = rest[:8], rest[8:]
    n0, n1, k0, k1, a0, a1, g0, g1, w, part_a, part_b, wide, extra, sem, sem_in = rest
    core = lax.axis_index("c")
    loads = [
        pltpu.make_async_copy(src, dst, sem_in.at[i])
        for i, (src, dst) in enumerate(
            zip(
                (a0h, g0h, a1h, g1h, n0h, k0h, n1h, k1h, wh.at[:, pl.ds(core * 1024, 1024)]),
                (a0, g0, a1, g1, n0, k0, n1, k1, w),
            )
        )
    ]
    for load in loads:
        load.start()
    contract = (((0,), (0,)), ((), ()))
    for load in loads[:4]:
        load.wait()
    for m in range(4):
        cols = slice(256 * m, 256 * m + 256)
        done = lax.dot_general(a0[:, cols], g0[...], contract, preferred_element_type=F32)
        done = done + lax.dot_general(a1[:, cols], g1[...], contract, preferred_element_type=F32)
        for v in range(4):
            wide[pl.ds(v, 256, stride=4), :] = done[:, 128 * v : 128 * v + 128]
        place(part_a, part_b, wide, 8192 + 1024 * m, 1024)
    for load in loads[4:]:
        load.wait()
    gains = []
    for m in range(4):
        cols = slice(256 * m, 256 * m + 256)
        done = lax.dot_general(n0[:, cols], k0[0:ROWS, :], contract, preferred_element_type=F32)
        done = done + lax.dot_general(n1[:, cols], k1[0:ROWS, :], contract, preferred_element_type=F32)
        folded = jnp.zeros((256, 128), F32)
        for v in range(8):
            piece = done[:, 128 * v : 128 * v + 128]
            wide[pl.ds(v, 256, stride=8), :] = piece
            folded = folded + piece * w[cols, 128 * v : 128 * v + 128].astype(F32)
        gains.append(jnp.sum(folded.T, axis=0, keepdims=True))
        place(part_a, part_b, wide, 2048 * m, 2048)
    for m in range(4):
        for j in range(2):
            at = 256 * m + 128 * j
            extra[40 + 2 * m + j : 41 + 2 * m + j, :] = gains[m][:, 128 * j : 128 * j + 128] / gain_ref[:, at : at + 128]
    taps = k0[ROWS:, :].astype(F32) + k1[ROWS:, :].astype(F32)
    for p in range(5):
        for v in range(8):
            extra[8 * p + v : 8 * p + v + 1, :] = taps[p : p + 1, 128 * v : 128 * v + 128]
    small = part_b.at[4, 0]
    small[...] = extra[...].astype(BF)
    copies = []
    for s in range(4):
        x = (lax.axis_index("x") + s) % 4
        y = (lax.axis_index(("yh", "yl")) + s) % 4
        for yh in range(2):
            copies.append((part_a.at[yh, pl.ds(x * 16, 16)], outs[s].at[pl.ds(yh * 16, 16)]))
        copies.append((small, outs[s].at[32]))
        copies.append((part_b.at[y], outs[4 + s]))
    copies = [pltpu.make_async_copy(src, dst, sem.at[i]) for i, (src, dst) in enumerate(copies)]
    for copy in copies:
        copy.start()
    for copy in copies:
        copy.wait()


def weight_blocks(gain, operands):
    blocks = [jax.ShapeDtypeStruct((33, 48, 128), BF)] * 4 + [jax.ShapeDtypeStruct((32, 48, 128), BF)] * 4
    return pl.pallas_call(
        weight_kernel,
        out_shape=blocks,
        in_specs=[vmem_spec()] + [hbm_spec(), any_spec()] * 4 + [hbm_spec()],
        out_specs=[hbm_spec()] * 8,
        scratch_shapes=[pltpu.VMEM(o.shape, BF) for o in operands[:8]]
        + [
            pltpu.VMEM((1024, 1024), BF),
            pltpu.VMEM((2, 64, 48, 128), BF),
            pltpu.VMEM((5, 32, 48, 128), BF),
            pltpu.VMEM((2048, 128), F32),
            pltpu.VMEM((48, 128), F32),
            pltpu.SemaphoreType.DMA((16,)),
            pltpu.SemaphoreType.DMA((9,)),
        ],
        compiler_params=pltpu.CompilerParams(vmem_limit_bytes=57 << 20),
        name="weight_grads",
    )(gain, *operands)


def sum_of(refs, index):
    total = refs[0][index].astype(F32)
    for ref in refs[1:]:
        total = total + ref[index].astype(F32)
    return total.astype(BF)


def first_x_kernel(i0, i1, i2, i3, mark, *outs):
    for s in range(4):
        y = (lax.axis_index(("yh", "yl")) + s) % 4
        base = (y // 2) * 16 + y % 2
        for z in range(8):
            outs[s][z] = sum_of((i0, i1, i2, i3), base + 2 * z)
        outs[s][8] = sum_of((i0, i1, i2, i3), 32)


def first_y_kernel(i0, i1, i2, i3, *outs):
    for s in range(4):
        x = (lax.axis_index("x") + s) % 4
        for z in range(8):
            outs[s][z] = sum_of((i0, i1, i2, i3), x * 8 + z)


def second_kernel(a0, a1, a2, a3, b0, b1, b2, b3, out):
    small = sum_of((a0, a1, a2, a3), 8)
    for z in range(8):
        out[z, 0:48, :] = sum_of((a0, a1, a2, a3), z)
        out[z, 48:96, :] = sum_of((b0, b1, b2, b3), z)
        out[z, 96:144, :] = small


def send(blocks, axes):
    n = 4
    got = [blocks[0]]
    for step in (2, 1, 3):
        got.append(lax.ppermute(blocks[step], axes, [(i, (i + step) % n) for i in range(n)]))
    return got


def reduce_terms(blocks, mark):
    got_x = send(blocks[:4], "x")
    got_y = send(blocks[4:], ("yh", "yl"))
    block9 = jax.ShapeDtypeStruct((9, 48, 128), BF)
    block8 = jax.ShapeDtypeStruct((8, 48, 128), BF)
    after_x = pl.pallas_call(
        first_x_kernel,
        out_shape=[block9] * 4,
        in_specs=[vmem_spec()] * 5,
        out_specs=[vmem_spec()] * 4,
        compiler_params=pltpu.CompilerParams(vmem_limit_bytes=8 << 20),
        name="sum_after_x",
    )(*got_x, mark)
    after_y = pl.pallas_call(
        first_y_kernel,
        out_shape=[block8] * 4,
        in_specs=[vmem_spec()] * 4,
        out_specs=[vmem_spec()] * 4,
        compiler_params=pltpu.CompilerParams(vmem_limit_bytes=8 << 20),
        name="sum_after_y",
    )(*got_y)
    got_a = send(after_x, ("yh", "yl"))
    got_b = send(after_y, "x")
    ready = pl.pallas_call(
        second_kernel,
        out_shape=jax.ShapeDtypeStruct((8, 144, 128), BF),
        in_specs=[vmem_spec()] * 8,
        out_specs=vmem_spec(),
        compiler_params=pltpu.CompilerParams(vmem_limit_bytes=6 << 20),
        name="sum_before_z",
    )(*got_a, *got_b)
    return lax.all_to_all(ready, "z", split_axis=0, concat_axis=0, tiled=True)


ALL = ("yh", "x", "z", "yl", "c")


def total_kernel(parts, total, head):
    done = parts[0].astype(F32)
    for z in range(1, 8):
        done = done + parts[z].astype(F32)
    total[...] = done
    head[...] = done[0:48, :]


def chunk_kernel(own, other, next0, next1, out, half0, half1, flat, *, chunk, scale):
    core = lax.axis_index("c")
    chip = lax.axis_index(("yh", "x", "z", "yl"))
    first = core == 0
    mine, others = own[...], other[...]
    half0[0:96, :] = jnp.where(first, mine[0:96], others[0:96])
    half1[0:96, :] = jnp.where(first, others[0:96], mine[0:96])
    small0 = jnp.where(first, mine[96:144], others[96:144])
    small1 = jnp.where(first, others[96:144], mine[96:144])
    both = small0[40:48] + small1[40:48]
    last = chip == 127
    half0[96:144, :] = jnp.where(last, small0, next0[...])
    half1[96:144, :] = jnp.where(last, small1, next1[...])

    @pl.when(last)
    def _():
        half1[128:136, :] = both

    for p in range(18):
        pair = chip * WIN + p
        proj = (pair >= 1024) & (pair < 1536)
        for h, half in ((0, half0), (1, half1)):
            tile = half[8 * p : 8 * p + 8, :] * scale

            @pl.when(proj)
            def _(p=p, h=h, tile=tile):
                flat[16 * p + 4 * h : 16 * p + 4 * h + 4, :] = tile[0:4]
                flat[16 * p + 8 + 4 * h : 16 * p + 12 + 4 * h, :] = tile[4:8]

            @pl.when(jnp.logical_not(proj))
            def _(p=p, h=h, tile=tile):
                flat[16 * p + 8 * h : 16 * p + 8 * h + 8, :] = tile

    begin = (2 * chip + core) * chunk - chip * (WIN * 2048)
    row, lane = begin // 128, begin % 128
    low = pltpu.roll(flat[pl.ds(row, 104), :], (128 - lane) % 128, axis=1)
    high = pltpu.roll(flat[pl.ds(row + 1, 104), :], (128 - lane) % 128, axis=1)
    at = lax.broadcasted_iota(jnp.int32, (104, 128), 1)
    out[...] = jnp.where(at < 128 - lane, low, high)


def own_chunk(swapped, chunk, grad_scale):
    total, head = pl.pallas_call(
        total_kernel,
        out_shape=[jax.ShapeDtypeStruct((144, 128), F32), jax.ShapeDtypeStruct((48, 128), F32)],
        in_specs=[vmem_spec()],
        out_specs=[vmem_spec()] * 2,
        compiler_params=pltpu.CompilerParams(vmem_limit_bytes=4 << 20),
        name="sum_after_z",
    )(swapped)
    next0 = lax.ppermute(head, ALL, [(2 * j, 2 * j - 1) for j in range(1, 128)])
    next1 = lax.ppermute(head, ALL, [(2 * j + 1, 2 * j - 1) for j in range(1, 128)])
    other = lax.ppermute(total, "c", [(0, 1), (1, 0)])
    out = pl.pallas_call(
        functools.partial(chunk_kernel, chunk=chunk, scale=grad_scale),
        out_shape=jax.ShapeDtypeStruct((104, 128), F32),
        in_specs=[vmem_spec()] * 4,
        out_specs=vmem_spec(),
        scratch_shapes=[pltpu.VMEM((144, 128), F32), pltpu.VMEM((144, 128), F32), pltpu.VMEM((312, 128), F32)],
        compiler_params=pltpu.CompilerParams(vmem_limit_bytes=4 << 20),
        name="own_chunk",
    )(total, other, next0, next1)
    return out.reshape(-1)[:chunk]


def pair_swap(array):
    return lax.ppermute(array, "c", [(0, 1), (1, 0)])


ROWS = 384
EDGE = 16
LONG = ROWS + 2 * EDGE


def inside(length_ref, first, shape):
    at = lax.axis_index(("yh", "x")) * ROWS + first + lax.broadcasted_iota(jnp.int32, shape, 0)
    return (at >= 0) & (at < length_ref[0])


def normed_rows(rows, gain):
    values = rows.astype(F32)
    center = values - jnp.mean(values, axis=-1, keepdims=True)
    scale = lax.rsqrt(jnp.mean(center * center, axis=-1, keepdims=True) + eps_norm)
    return (center * scale * gain).astype(BF)


def early_kernel(length_ref, gain_ref, xh, gh, normed_o, keep_o, give_o, x, g, sem, sem_out):
    core = lax.axis_index("c")
    loads = [pltpu.make_async_copy(xh, x, sem.at[0]), pltpu.make_async_copy(gh, g, sem.at[1])]
    for load in loads:
        load.start()
    for load in loads:
        load.wait()
    gain = gain_ref[...]

    def step(i, _):
        for j in range(2):
            r = pl.multiple_of(i * 64 + 32 * j, 32)
            rows = pl.ds(r, 32)
            x[rows, :] = normed_rows(x[rows, :], gain)
            g[rows, :] = jnp.where(inside(length_ref, r, (32, 1024)), g[rows, :].astype(F32), 0.0).astype(BF)
        return 0

    lax.fori_loop(0, ROWS // 64, step, 0)
    sends = [
        pltpu.make_async_copy(x, normed_o, sem_out.at[0]),
        pltpu.make_async_copy(g.at[:, pl.ds(core * 512, 512)], keep_o, sem_out.at[1]),
        pltpu.make_async_copy(g.at[:, pl.ds(512 - core * 512, 512)], give_o, sem_out.at[2]),
    ]
    for copy in sends:
        copy.start()
    for copy in sends:
        copy.wait()


def early(lengths, gain, x, g):
    wide = jax.ShapeDtypeStruct((ROWS, 1024), BF)
    half = jax.ShapeDtypeStruct((ROWS, 512), BF)
    return pl.pallas_call(
        early_kernel,
        out_shape=[wide, half, half],
        in_specs=[smem_spec(), vmem_spec()] + [hbm_spec()] * 2,
        out_specs=[hbm_spec()] * 3,
        scratch_shapes=[
            pltpu.VMEM((ROWS, 1024), BF),
            pltpu.VMEM((ROWS, 1024), BF),
            pltpu.SemaphoreType.DMA((2,)),
            pltpu.SemaphoreType.DMA((3,)),
        ],
        name="early",
    )(lengths, gain, x, g)


def main_kernel(info_ref, gain_ref, taps_ref, nh, gkh, ggh, beforeh, afterh, wh, pwh, *rest):
    act_o, both_o, keep_o, give_o = rest[:4]
    gs, w, pw, nm, act, both, lifts0, lifts1, gat, gcon, acf, mask, krows, sem, sem_out = rest[4:]
    core = lax.axis_index("c")
    pairs = [
        (beforeh.at[0], nm.at[pl.ds(0, EDGE)]),
        (afterh.at[0], nm.at[pl.ds(EDGE + ROWS, EDGE)]),
        (beforeh.at[1], gs.at[pl.ds(0, EDGE)]),
        (afterh.at[1], gs.at[pl.ds(EDGE + ROWS, EDGE)]),
        (nh, nm.at[pl.ds(EDGE, ROWS)]),
        (gkh, gs.at[pl.ds(EDGE, ROWS), pl.ds(core * 512, 512)]),
        (ggh, gs.at[pl.ds(EDGE, ROWS), pl.ds(512 - core * 512, 512)]),
    ]
    for n in range(4):
        pairs.append((wh.at[:, pl.ds(256 * n, 256)], w.at[:, pl.ds(256 * n, 256)]))
        pairs.append((wh.at[:, pl.ds(1024 + 256 * n, 256)], w.at[:, pl.ds(1024 + 256 * n, 256)]))
        pairs.append((pwh.at[pl.ds(256 * n, 256)], pw.at[pl.ds(256 * n, 256)]))
    loads = [pltpu.make_async_copy(src, dst, sem.at[i]) for i, (src, dst) in enumerate(pairs)]
    for load in loads:
        load.start()
    mask[...] = inside(info_ref, -EDGE, (LONG, 128)).astype(F32)
    krows[...] = jnp.zeros((2, 16, 1024), F32)
    for load in loads[:4]:
        load.wait()
    for first in (0, EDGE + ROWS):
        rows = pl.ds(first, EDGE)
        nm[rows, :] = normed_rows(nm[rows, :], gain_ref[...])
        gs[rows, :] = jnp.where(inside(info_ref, first - EDGE, (EDGE, 1024)), gs[rows, :].astype(F32), 0.0).astype(BF)
    for load in loads[4:7]:
        load.wait()

    def multiply(n, lifts):
        for load in loads[7 + 3 * n : 10 + 3 * n]:
            load.wait()
        lanes = slice(256 * n, 256 * n + 256)
        lift_value = jnp.dot(nm[...], w[:, lanes], preferred_element_type=F32)
        lift_gate = jnp.dot(nm[...], w[:, 1024 + 256 * n : 1280 + 256 * n], preferred_element_type=F32)
        back = lax.dot_general(gs[...], pw[lanes, :], (((1,), (1,)), ((), ())), preferred_element_type=F32)
        for h in range(2):
            lifts[h] = lift_value[:, 128 * h : 128 * h + 128]
            lifts[2 + h] = lift_gate[:, 128 * h : 128 * h + 128]
            lifts[4 + h] = back[:, 128 * h : 128 * h + 128]

    def channels(n, h, lifts):
        at = 256 * n + 128 * h
        taps = [taps_ref[k : k + 1, at : at + 128] for k in range(9)]
        for i in range(10):
            rows = pl.ds(8 + 40 * i, 40)
            s = jax.nn.sigmoid(lifts[2 + h, rows, :])
            lifts[2 + h, rows, :] = s
            gat[h, rows, :] = (lifts[h, rows, :] * s * mask[rows, :]).astype(BF).astype(F32)
        for i in range(7):
            r = 12 + 56 * i
            rows = pl.ds(r, 56)
            conv = taps[0] * gat[h, pl.ds(r - 4, 56), :]
            for k in range(1, 9):
                conv = conv + taps[k] * gat[h, pl.ds(r + k - 4, 56), :]
            s = jax.nn.sigmoid(conv)
            acf[h, rows, :] = conv * s
            grad = lifts[4 + h, rows, :] * s * (1.0 + conv * (1.0 - s))
            gcon[h, rows, :] = grad.astype(BF).astype(F32)
        sums = [jnp.zeros((8, 128), F32) for _ in range(9)]
        for i in range(8):
            r = EDGE + 48 * i
            rows = pl.ds(r, 48)
            own = pl.ds(r - EDGE, 48)
            grad = taps[0] * gcon[h, pl.ds(r + 4, 48), :]
            for k in range(1, 9):
                grad = grad + taps[k] * gcon[h, pl.ds(r + 4 - k, 48), :]
            s = lifts[2 + h, rows, :]
            first = grad * mask[rows, :] * s
            both[0, own, at : at + 128] = first.astype(BF)
            both[1, own, at : at + 128] = (first * lifts[h, rows, :] * (1.0 - s)).astype(BF)
            act[own, at : at + 128] = acf[h, rows, :].astype(BF)
            here = gcon[h, rows, :]
            for k in range(9):
                product = here * gat[h, pl.ds(r + k - 4, 48), :]
                sums[k] = sums[k] + jnp.sum(product.reshape(6, 8, 128), axis=0)
        for k in range(9):
            krows[k % 2, k // 2 : k // 2 + 1, at : at + 128] = jnp.sum(sums[k], axis=0, keepdims=True)

    lifts = (lifts0, lifts1)
    multiply(0, lifts0)
    for n in range(4):
        if n < 3:
            multiply(n + 1, lifts[(n + 1) % 2])
        for h in range(2):
            channels(n, h, lifts[n % 2])
    for c in range(2):
        both[c, ROWS:, :] = krows[c].astype(BF)
    sends = [
        (both.at[1 - core], give_o),
        (act, act_o),
        (both.at[core], keep_o),
        (both, both_o),
    ]
    sends = [pltpu.make_async_copy(src, dst, sem_out.at[i]) for i, (src, dst) in enumerate(sends)]
    for copy in sends:
        copy.start()
    for copy in sends:
        copy.wait()


def forward_backward(lengths, gain, taps, normed, gb_keep, gb_give, before, after, w, pw):
    wide = jax.ShapeDtypeStruct((ROWS, 1024), BF)
    tall = jax.ShapeDtypeStruct((ROWS + 16, 1024), BF)
    return pl.pallas_call(
        main_kernel,
        out_shape=[wide, jax.ShapeDtypeStruct((2, ROWS + 16, 1024), BF), tall, tall],
        in_specs=[smem_spec(), vmem_spec(), vmem_spec()] + [hbm_spec()] * 7,
        out_specs=[hbm_spec()] * 4,
        scratch_shapes=[
            pltpu.VMEM((LONG, 1024), BF),
            pltpu.VMEM((1024, 2048), BF),
            pltpu.VMEM((1024, 1024), BF),
            pltpu.VMEM((LONG, 1024), BF),
            pltpu.VMEM((ROWS, 1024), BF),
            pltpu.VMEM((2, ROWS + 16, 1024), BF),
            pltpu.VMEM((6, LONG, 128), F32),
            pltpu.VMEM((6, LONG, 128), F32),
            pltpu.VMEM((2, LONG, 128), F32),
            pltpu.VMEM((2, LONG, 128), F32),
            pltpu.VMEM((2, LONG, 128), F32),
            pltpu.VMEM((LONG, 128), F32),
            pltpu.VMEM((2, 16, 1024), F32),
            pltpu.SemaphoreType.DMA((19,)),
            pltpu.SemaphoreType.DMA((4,)),
        ],
        name="forward_backward",
    )(lengths, gain, taps, normed, gb_keep, gb_give, before, after, w, pw)


def outputs_kernel(info_ref, gain_ref, xh, gh, acth, bothh, wh, pwh, after_this, out_o, grad_o, mark_o, *rest):
    mark_o[...] = jnp.zeros((8, 128), F32)
    x, g, act, both, w, pw, sem, sem_out = rest
    pairs = [(acth, act), (pwh, pw), (xh, x), (bothh, both), (wh, w), (gh, g)]
    loads = [pltpu.make_async_copy(src, dst, sem.at[i]) for i, (src, dst) in enumerate(pairs)]
    for load in loads:
        load.start()
    for load in loads[:3]:
        load.wait()
    contract = (((1,), (1,)), ((), ()))
    for i in range(3):
        rows = slice(128 * i, 128 * i + 128)
        branch = jnp.dot(act[rows, :], pw[...], preferred_element_type=F32)
        branch = jnp.where(inside(info_ref, 128 * i, (128, 1024)), branch, 0.0)
        act[rows, :] = (x[rows, :].astype(F32) + branch).astype(BF)
    first = pltpu.make_async_copy(act, out_o, sem_out.at[0])
    first.start()
    for load in loads[3:]:
        load.wait()
    for i in range(3):
        rows = slice(128 * i, 128 * i + 128)
        grad = lax.dot_general(both[0, rows, :], w[:, :1024], contract, preferred_element_type=F32)
        grad = grad + lax.dot_general(both[1, rows, :], w[:, 1024:], contract, preferred_element_type=F32)
        u = grad * gain_ref[...]
        values = x[rows, :].astype(F32)
        center = values - jnp.mean(values, axis=-1, keepdims=True)
        scale = lax.rsqrt(jnp.mean(center * center, axis=-1, keepdims=True) + eps_norm)
        xhat = center * scale
        u = scale * (u - jnp.mean(u, axis=-1, keepdims=True) - xhat * jnp.mean(u * xhat, axis=-1, keepdims=True))
        g[rows, :] = (g[rows, :].astype(F32) + u).astype(BF)
    second = pltpu.make_async_copy(g, grad_o, sem_out.at[1])
    second.start()
    first.wait()
    second.wait()


def outputs(info, gain, x, g, act, both, w, pw, after_this):
    wide = jax.ShapeDtypeStruct((ROWS, 1024), BF)
    return pl.pallas_call(
        outputs_kernel,
        out_shape=[wide, wide, jax.ShapeDtypeStruct((8, 128), F32)],
        in_specs=[smem_spec(), vmem_spec()] + [hbm_spec()] * 7,
        out_specs=[hbm_spec()] * 2 + [vmem_spec()],
        scratch_shapes=[
            pltpu.VMEM((ROWS, 1024), BF),
            pltpu.VMEM((ROWS, 1024), BF),
            pltpu.VMEM((ROWS, 1024), BF),
            pltpu.VMEM((2, ROWS + 16, 1024), BF),
            pltpu.VMEM((1024, 2048), BF),
            pltpu.VMEM((1024, 1024), BF),
            pltpu.SemaphoreType.DMA((6,)),
            pltpu.SemaphoreType.DMA((2,)),
        ],
        name="outputs",
    )(info, gain, x, g, act, both, w, pw, after_this)


def local(features, cotangent, lengths, norm_gain, lift_weight, conv_kernel, proj_weight):
    x, g = features[0], cotangent[0]
    frames, width = x.shape
    edge = jnp.stack([x[-EDGE:], g[-EDGE:]])
    start = jnp.stack([x[:EDGE], g[:EDGE]])
    before = lax.ppermute(edge, ("yh", "x"), [(i, i + 1) for i in range(7)])
    after = lax.ppermute(start, ("yh", "x"), [(i + 1, i) for i in range(7)])
    gain = norm_gain[None]
    normed, gb_keep, gb_give = early(lengths, gain, x, g)
    normed_other = pair_swap(normed)
    gb_other = pair_swap(gb_give)
    activated, both, keep, give = forward_backward(
        lengths, gain, conv_kernel, normed, gb_keep, gb_give, before, after, lift_weight, proj_weight
    )
    keep_other = pair_swap(give)
    act_other = pair_swap(activated)
    chunk = (2 * width * width + width * width + 10 * width) // 256
    operands = (normed, normed_other, keep, keep_other, activated, act_other, gb_keep, gb_other, lift_weight)
    blocks = weight_blocks(gain, operands)
    output, grad_features, mark = outputs(lengths, gain, x, g, activated, both, lift_weight, proj_weight, blocks[0])
    grads = own_chunk(reduce_terms(blocks, mark), chunk, float(frames * 256) ** (-0.5))
    return output[None], grad_features[None], grads


def solution(mesh):
    fine = Mesh(mesh.devices.reshape(2, 4, 8, 2, 2), ALL)
    act = P(("z", "yl", "c"), ("yh", "x"), None)

    return jax.shard_map(
        local,
        mesh=fine,
        in_specs=(act, act, P(("z", "yl", "c")), P(), P(), P(), P()),
        out_specs=(act, act, P(ALL)),
        check_vma=False,
    )
```

```python
import functools

import jax
import jax.numpy as jnp
from jax import lax
from jax.experimental import pallas as pl
from jax.experimental.pallas import tpu as pltpu
from jax.sharding import Mesh, PartitionSpec as P


eps_norm = 1e-05
BF = jnp.bfloat16
F32 = jnp.float32
WIN = 12


def any_spec():
    return pl.BlockSpec(memory_space=pl.ANY)


def hbm_spec():
    return pl.BlockSpec(memory_space=pltpu.HBM)


def vmem_spec():
    return pl.BlockSpec(memory_space=pltpu.VMEM)


def smem_spec():
    return pl.BlockSpec(memory_space=pltpu.SMEM)


def place(part_a, part_b, wide, begin, count):
    at = 0
    while at < count:
        window, inside = divmod(begin + at, 96)
        low = inside % 48
        step = min(48 - low, count - at)
        rows = wide[at : at + step, :].astype(BF)
        yh, rest = divmod(window, 64)
        if inside < 48:
            part_a[yh, rest, low : low + step, :] = rows
        else:
            part_b[yh * 2 + rest % 2, rest // 2, low : low + step, :] = rows
        at += step


def weight_kernel(gain_ref, n0h, n1h, k0h, k1h, a0h, a1h, g0h, g1h, wh, *rest):
    outs, rest = rest[:8], rest[8:]
    n0, n1, k0, k1, a0, a1, g0, g1, w, part_a, part_b, wide, extra, sem, sem_in = rest
    core = lax.axis_index("c")
    loads = [
        pltpu.make_async_copy(src, dst, sem_in.at[i])
        for i, (src, dst) in enumerate(
            zip(
                (a0h, g0h, a1h, g1h, n0h, k0h, n1h, k1h, wh.at[:, pl.ds(core * 1024, 1024)]),
                (a0, g0, a1, g1, n0, k0, n1, k1, w),
            )
        )
    ]
    for load in loads:
        load.start()
    contract = (((0,), (0,)), ((), ()))
    for load in loads[:4]:
        load.wait()
    for m in range(4):
        cols = slice(256 * m, 256 * m + 256)
        done = lax.dot_general(a0[:, cols], g0[...], contract, preferred_element_type=F32)
        done = done + lax.dot_general(a1[:, cols], g1[...], contract, preferred_element_type=F32)
        for v in range(4):
            wide[pl.ds(v, 256, stride=4), :] = done[:, 128 * v : 128 * v + 128]
        place(part_a, part_b, wide, 8192 + 1024 * m, 1024)
    for load in loads[4:]:
        load.wait()
    gains = []
    for m in range(4):
        cols = slice(256 * m, 256 * m + 256)
        done = lax.dot_general(n0[:, cols], k0[0:ROWS, :], contract, preferred_element_type=F32)
        done = done + lax.dot_general(n1[:, cols], k1[0:ROWS, :], contract, preferred_element_type=F32)
        folded = jnp.zeros((256, 128), F32)
        for v in range(8):
            piece = done[:, 128 * v : 128 * v + 128]
            wide[pl.ds(v, 256, stride=8), :] = piece
            folded = folded + piece * w[cols, 128 * v : 128 * v + 128].astype(F32)
        gains.append(jnp.sum(folded.T, axis=0, keepdims=True))
        place(part_a, part_b, wide, 2048 * m, 2048)
    for m in range(4):
        for j in range(2):
            at = 256 * m + 128 * j
            extra[40 + 2 * m + j : 41 + 2 * m + j, :] = gains[m][:, 128 * j : 128 * j + 128] / gain_ref[:, at : at + 128]
    taps = k0[ROWS:, :].astype(F32) + k1[ROWS:, :].astype(F32)
    for p in range(5):
        for v in range(8):
            extra[8 * p + v : 8 * p + v + 1, :] = taps[p : p + 1, 128 * v : 128 * v + 128]
    small = part_b.at[4, 0]
    small[...] = extra[...].astype(BF)
    copies = []
    for s in range(4):
        x = (lax.axis_index("x") + s) % 4
        y = (lax.axis_index(("yh", "yl")) + s) % 4
        for yh in range(2):
            copies.append((part_a.at[yh, pl.ds(x * 16, 16)], outs[s].at[pl.ds(yh * 16, 16)]))
        copies.append((small, outs[s].at[32]))
        copies.append((part_b.at[y], outs[4 + s]))
    copies = [pltpu.make_async_copy(src, dst, sem.at[i]) for i, (src, dst) in enumerate(copies)]
    for copy in copies:
        copy.start()
    for copy in copies:
        copy.wait()


def weight_blocks(gain, operands):
    blocks = [jax.ShapeDtypeStruct((33, 48, 128), BF)] * 4 + [jax.ShapeDtypeStruct((32, 48, 128), BF)] * 4
    return pl.pallas_call(
        weight_kernel,
        out_shape=blocks,
        in_specs=[vmem_spec()] + [hbm_spec(), any_spec()] * 4 + [hbm_spec()],
        out_specs=[hbm_spec()] * 8,
        scratch_shapes=[pltpu.VMEM(o.shape, BF) for o in operands[:8]]
        + [
            pltpu.VMEM((1024, 1024), BF),
            pltpu.VMEM((2, 64, 48, 128), BF),
            pltpu.VMEM((5, 32, 48, 128), BF),
            pltpu.VMEM((2048, 128), F32),
            pltpu.VMEM((48, 128), F32),
            pltpu.SemaphoreType.DMA((16,)),
            pltpu.SemaphoreType.DMA((9,)),
        ],
        compiler_params=pltpu.CompilerParams(vmem_limit_bytes=57 << 20),
        name="weight_grads",
    )(gain, *operands)


def sum_of(refs, index):
    total = refs[0][index].astype(F32)
    for ref in refs[1:]:
        total = total + ref[index].astype(F32)
    return total.astype(BF)


def first_x_kernel(i0, i1, i2, i3, mark, *outs):
    for s in range(4):
        y = (lax.axis_index(("yh", "yl")) + s) % 4
        base = (y // 2) * 16 + y % 2
        for z in range(8):
            outs[s][z] = sum_of((i0, i1, i2, i3), base + 2 * z)
        outs[s][8] = sum_of((i0, i1, i2, i3), 32)


def first_y_kernel(i0, i1, i2, i3, *outs):
    for s in range(4):
        x = (lax.axis_index("x") + s) % 4
        for z in range(8):
            outs[s][z] = sum_of((i0, i1, i2, i3), x * 8 + z)


def second_kernel(a0, a1, a2, a3, b0, b1, b2, b3, out):
    small = sum_of((a0, a1, a2, a3), 8)
    for z in range(8):
        out[z, 0:48, :] = sum_of((a0, a1, a2, a3), z)
        out[z, 48:96, :] = sum_of((b0, b1, b2, b3), z)
        out[z, 96:144, :] = small


def send(blocks, axes):
    n = 4
    got = [blocks[0]]
    for step in (2, 1, 3):
        got.append(lax.ppermute(blocks[step], axes, [(i, (i + step) % n) for i in range(n)]))
    return got


def reduce_terms(blocks, mark):
    got_x = send(blocks[:4], "x")
    got_y = send(blocks[4:], ("yh", "yl"))
    block9 = jax.ShapeDtypeStruct((9, 48, 128), BF)
    block8 = jax.ShapeDtypeStruct((8, 48, 128), BF)
    after_x = pl.pallas_call(
        first_x_kernel,
        out_shape=[block9] * 4,
        in_specs=[vmem_spec()] * 4 + [any_spec()],
        out_specs=[vmem_spec()] * 4,
        compiler_params=pltpu.CompilerParams(vmem_limit_bytes=8 << 20),
        name="sum_after_x",
    )(*got_x, mark)
    after_y = pl.pallas_call(
        first_y_kernel,
        out_shape=[block8] * 4,
        in_specs=[vmem_spec()] * 4,
        out_specs=[vmem_spec()] * 4,
        compiler_params=pltpu.CompilerParams(vmem_limit_bytes=8 << 20),
        name="sum_after_y",
    )(*got_y)
    got_a = send(after_x, ("yh", "yl"))
    got_b = send(after_y, "x")
    ready = pl.pallas_call(
        second_kernel,
        out_shape=jax.ShapeDtypeStruct((8, 144, 128), BF),
        in_specs=[vmem_spec()] * 8,
        out_specs=vmem_spec(),
        compiler_params=pltpu.CompilerParams(vmem_limit_bytes=6 << 20),
        name="sum_before_z",
    )(*got_a, *got_b)
    return lax.all_to_all(ready, "z", split_axis=0, concat_axis=0, tiled=True)


ALL = ("yh", "x", "z", "yl", "c")


def total_kernel(parts, total, head):
    done = parts[0].astype(F32)
    for z in range(1, 8):
        done = done + parts[z].astype(F32)
    total[...] = done
    head[...] = done[0:48, :]


def chunk_kernel(own, other, next0, next1, out, half0, half1, flat, *, chunk, scale):
    core = lax.axis_index("c")
    chip = lax.axis_index(("yh", "x", "z", "yl"))
    first = core == 0
    mine, others = own[...], other[...]
    half0[0:96, :] = jnp.where(first, mine[0:96], others[0:96])
    half1[0:96, :] = jnp.where(first, others[0:96], mine[0:96])
    small0 = jnp.where(first, mine[96:144], others[96:144])
    small1 = jnp.where(first, others[96:144], mine[96:144])
    both = small0[40:48] + small1[40:48]
    last = chip == 127
    half0[96:144, :] = jnp.where(last, small0, next0[...])
    half1[96:144, :] = jnp.where(last, small1, next1[...])

    @pl.when(last)
    def _():
        half1[128:136, :] = both

    for p in range(18):
        pair = chip * WIN + p
        proj = (pair >= 1024) & (pair < 1536)
        for h, half in ((0, half0), (1, half1)):
            tile = half[8 * p : 8 * p + 8, :] * scale

            @pl.when(proj)
            def _(p=p, h=h, tile=tile):
                flat[16 * p + 4 * h : 16 * p + 4 * h + 4, :] = tile[0:4]
                flat[16 * p + 8 + 4 * h : 16 * p + 12 + 4 * h, :] = tile[4:8]

            @pl.when(jnp.logical_not(proj))
            def _(p=p, h=h, tile=tile):
                flat[16 * p + 8 * h : 16 * p + 8 * h + 8, :] = tile

    begin = (2 * chip + core) * chunk - chip * (WIN * 2048)
    row, lane = begin // 128, begin % 128
    low = pltpu.roll(flat[pl.ds(row, 104), :], (128 - lane) % 128, axis=1)
    high = pltpu.roll(flat[pl.ds(row + 1, 104), :], (128 - lane) % 128, axis=1)
    at = lax.broadcasted_iota(jnp.int32, (104, 128), 1)
    out[...] = jnp.where(at < 128 - lane, low, high)


def own_chunk(swapped, chunk, grad_scale):
    total, head = pl.pallas_call(
        total_kernel,
        out_shape=[jax.ShapeDtypeStruct((144, 128), F32), jax.ShapeDtypeStruct((48, 128), F32)],
        in_specs=[vmem_spec()],
        out_specs=[vmem_spec()] * 2,
        compiler_params=pltpu.CompilerParams(vmem_limit_bytes=4 << 20),
        name="sum_after_z",
    )(swapped)
    next0 = lax.ppermute(head, ALL, [(2 * j, 2 * j - 1) for j in range(1, 128)])
    next1 = lax.ppermute(head, ALL, [(2 * j + 1, 2 * j - 1) for j in range(1, 128)])
    other = lax.ppermute(total, "c", [(0, 1), (1, 0)])
    out = pl.pallas_call(
        functools.partial(chunk_kernel, chunk=chunk, scale=grad_scale),
        out_shape=jax.ShapeDtypeStruct((104, 128), F32),
        in_specs=[vmem_spec()] * 4,
        out_specs=vmem_spec(),
        scratch_shapes=[pltpu.VMEM((144, 128), F32), pltpu.VMEM((144, 128), F32), pltpu.VMEM((312, 128), F32)],
        compiler_params=pltpu.CompilerParams(vmem_limit_bytes=4 << 20),
        name="own_chunk",
    )(total, other, next0, next1)
    return out.reshape(-1)[:chunk]


def pair_swap(array):
    return lax.ppermute(array, "c", [(0, 1), (1, 0)])


ROWS = 384
EDGE = 16
LONG = ROWS + 2 * EDGE


def inside(length_ref, first, shape):
    at = lax.axis_index(("yh", "x")) * ROWS + first + lax.broadcasted_iota(jnp.int32, shape, 0)
    return (at >= 0) & (at < length_ref[0])


def normed_rows(rows, gain):
    values = rows.astype(F32)
    center = values - jnp.mean(values, axis=-1, keepdims=True)
    scale = lax.rsqrt(jnp.mean(center * center, axis=-1, keepdims=True) + eps_norm)
    return (center * scale * gain).astype(BF)


PART = 96


def early_kernel(length_ref, gain_ref, xh, gh, normed_o, keep_o, give_o, x, g, sem, sem_out):
    core = lax.axis_index("c")
    parts = [pl.ds(PART * i, PART) for i in range(ROWS // PART)]
    loads = [pltpu.make_async_copy(xh.at[p], x.at[p], sem.at[0, i]) for i, p in enumerate(parts)]
    loads += [pltpu.make_async_copy(gh.at[p], g.at[p], sem.at[1, i]) for i, p in enumerate(parts)]
    for load in loads:
        load.start()
    gain = gain_ref[...]
    sends = []
    for i, p in enumerate(parts):
        loads[i].wait()
        for j in range(0, PART, 16):
            rows = pl.ds(PART * i + j, 16)
            x[rows, :] = normed_rows(x[rows, :], gain)
        sends.append(pltpu.make_async_copy(x.at[p], normed_o.at[p], sem_out.at[0, i]))
        sends[-1].start()
    for i, p in enumerate(parts):
        loads[len(parts) + i].wait()
        valid = inside(length_ref, PART * i, (PART, 1024))
        g[p, :] = jnp.where(valid, g[p, :].astype(F32), 0.0).astype(BF)
        for k, (out, at) in enumerate(((keep_o, core * 512), (give_o, 512 - core * 512))):
            sends.append(pltpu.make_async_copy(g.at[p, pl.ds(at, 512)], out.at[p], sem_out.at[1 + k, i]))
            sends[-1].start()
    for copy in sends:
        copy.wait()


def early(lengths, gain, x, g):
    wide = jax.ShapeDtypeStruct((ROWS, 1024), BF)
    half = jax.ShapeDtypeStruct((ROWS, 512), BF)
    return pl.pallas_call(
        early_kernel,
        out_shape=[wide, half, half],
        in_specs=[smem_spec(), vmem_spec()] + [hbm_spec()] * 2,
        out_specs=[hbm_spec()] * 3,
        scratch_shapes=[
            pltpu.VMEM((ROWS, 1024), BF),
            pltpu.VMEM((ROWS, 1024), BF),
            pltpu.SemaphoreType.DMA((2, ROWS // PART)),
            pltpu.SemaphoreType.DMA((3, ROWS // PART)),
        ],
        name="early",
    )(lengths, gain, x, g)


def main_kernel(info_ref, gain_ref, taps_ref, nh, gkh, ggh, beforeh, afterh, wh, pwh, *rest):
    act_o, both_o, keep_o, give_o = rest[:4]
    gs, w, pw, nm, act, both, lifts0, lifts1, gat, gcon, acf, mask, krows, sem, sem_out = rest[4:]
    core = lax.axis_index("c")
    pairs = [
        (beforeh.at[0], nm.at[pl.ds(0, EDGE)]),
        (afterh.at[0], nm.at[pl.ds(EDGE + ROWS, EDGE)]),
        (beforeh.at[1], gs.at[pl.ds(0, EDGE)]),
        (afterh.at[1], gs.at[pl.ds(EDGE + ROWS, EDGE)]),
        (nh, nm.at[pl.ds(EDGE, ROWS)]),
        (gkh, gs.at[pl.ds(EDGE, ROWS), pl.ds(core * 512, 512)]),
        (ggh, gs.at[pl.ds(EDGE, ROWS), pl.ds(512 - core * 512, 512)]),
    ]
    for n in range(4):
        pairs.append((wh.at[:, pl.ds(256 * n, 256)], w.at[:, pl.ds(256 * n, 256)]))
        pairs.append((wh.at[:, pl.ds(1024 + 256 * n, 256)], w.at[:, pl.ds(1024 + 256 * n, 256)]))
        pairs.append((pwh.at[pl.ds(256 * n, 256)], pw.at[pl.ds(256 * n, 256)]))
    loads = [pltpu.make_async_copy(src, dst, sem.at[i]) for i, (src, dst) in enumerate(pairs)]
    for load in loads:
        load.start()
    mask[...] = inside(info_ref, -EDGE, (LONG, 128)).astype(F32)
    krows[...] = jnp.zeros((2, 16, 1024), F32)
    for load in loads[:4]:
        load.wait()
    for first in (0, EDGE + ROWS):
        rows = pl.ds(first, EDGE)
        nm[rows, :] = normed_rows(nm[rows, :], gain_ref[...])
        gs[rows, :] = jnp.where(inside(info_ref, first - EDGE, (EDGE, 1024)), gs[rows, :].astype(F32), 0.0).astype(BF)
    for load in loads[4:7]:
        load.wait()

    def multiply(n, lifts):
        for load in loads[7 + 3 * n : 10 + 3 * n]:
            load.wait()
        lanes = slice(256 * n, 256 * n + 256)
        lift_value = jnp.dot(nm[...], w[:, lanes], preferred_element_type=F32)
        lift_gate = jnp.dot(nm[...], w[:, 1024 + 256 * n : 1280 + 256 * n], preferred_element_type=F32)
        back = lax.dot_general(gs[...], pw[lanes, :], (((1,), (1,)), ((), ())), preferred_element_type=F32)
        for h in range(2):
            lifts[h] = lift_value[:, 128 * h : 128 * h + 128]
            lifts[2 + h] = lift_gate[:, 128 * h : 128 * h + 128]
            lifts[4 + h] = back[:, 128 * h : 128 * h + 128]

    def channels(n, h, lifts):
        at = 256 * n + 128 * h
        taps = [taps_ref[k : k + 1, at : at + 128] for k in range(9)]
        for i in range(10):
            rows = pl.ds(8 + 40 * i, 40)
            s = jax.nn.sigmoid(lifts[2 + h, rows, :])
            lifts[2 + h, rows, :] = s
            gat[h, rows, :] = (lifts[h, rows, :] * s * mask[rows, :]).astype(BF).astype(F32)
        for i in range(7):
            r = 12 + 56 * i
            rows = pl.ds(r, 56)
            conv = taps[0] * gat[h, pl.ds(r - 4, 56), :]
            for k in range(1, 9):
                conv = conv + taps[k] * gat[h, pl.ds(r + k - 4, 56), :]
            s = jax.nn.sigmoid(conv)
            active = conv * s
            acf[h, rows, :] = active
            grad = lifts[4 + h, rows, :] * (s + active * (1.0 - s))
            gcon[h, rows, :] = grad.astype(BF).astype(F32)
        sums = [jnp.zeros((8, 128), F32) for _ in range(9)]
        for i in range(8):
            r = EDGE + 48 * i
            rows = pl.ds(r, 48)
            own = pl.ds(r - EDGE, 48)
            grad = taps[0] * gcon[h, pl.ds(r + 4, 48), :]
            for k in range(1, 9):
                grad = grad + taps[k] * gcon[h, pl.ds(r + 4 - k, 48), :]
            s = lifts[2 + h, rows, :]
            first = grad * mask[rows, :] * s
            both[0, own, at : at + 128] = first.astype(BF)
            both[1, own, at : at + 128] = (first * lifts[h, rows, :] * (1.0 - s)).astype(BF)
            act[own, at : at + 128] = acf[h, rows, :].astype(BF)
            here = gcon[h, rows, :]
            for k in range(9):
                product = here * gat[h, pl.ds(r + k - 4, 48), :]
                sums[k] = sums[k] + jnp.sum(product.reshape(6, 8, 128), axis=0)
        for k in range(9):
            krows[k % 2, k // 2 : k // 2 + 1, at : at + 128] = jnp.sum(sums[k], axis=0, keepdims=True)

    lifts = (lifts0, lifts1)
    multiply(0, lifts0)
    for n in range(4):
        if n < 3:
            multiply(n + 1, lifts[(n + 1) % 2])
        for h in range(2):
            channels(n, h, lifts[n % 2])
    for c in range(2):
        both[c, ROWS:, :] = krows[c].astype(BF)
    sends = [
        (both.at[1 - core], give_o),
        (act, act_o),
        (both.at[core], keep_o),
        (both, both_o),
    ]
    sends = [pltpu.make_async_copy(src, dst, sem_out.at[i]) for i, (src, dst) in enumerate(sends)]
    for copy in sends:
        copy.start()
    for copy in sends:
        copy.wait()


def forward_backward(lengths, gain, taps, normed, gb_keep, gb_give, before, after, w, pw):
    wide = jax.ShapeDtypeStruct((ROWS, 1024), BF)
    tall = jax.ShapeDtypeStruct((ROWS + 16, 1024), BF)
    return pl.pallas_call(
        main_kernel,
        out_shape=[wide, jax.ShapeDtypeStruct((2, ROWS + 16, 1024), BF), tall, tall],
        in_specs=[smem_spec(), vmem_spec(), vmem_spec()] + [hbm_spec()] * 7,
        out_specs=[hbm_spec()] * 4,
        scratch_shapes=[
            pltpu.VMEM((LONG, 1024), BF),
            pltpu.VMEM((1024, 2048), BF),
            pltpu.VMEM((1024, 1024), BF),
            pltpu.VMEM((LONG, 1024), BF),
            pltpu.VMEM((ROWS, 1024), BF),
            pltpu.VMEM((2, ROWS + 16, 1024), BF),
            pltpu.VMEM((6, LONG, 128), F32),
            pltpu.VMEM((6, LONG, 128), F32),
            pltpu.VMEM((2, LONG, 128), F32),
            pltpu.VMEM((2, LONG, 128), F32),
            pltpu.VMEM((2, LONG, 128), F32),
            pltpu.VMEM((LONG, 128), F32),
            pltpu.VMEM((2, 16, 1024), F32),
            pltpu.SemaphoreType.DMA((19,)),
            pltpu.SemaphoreType.DMA((4,)),
        ],
        name="forward_backward",
    )(lengths, gain, taps, normed, gb_keep, gb_give, before, after, w, pw)


def outputs_kernel(info_ref, gain_ref, xh, gh, acth, bothh, wh, pwh, after_this, out_o, grad_o, mark_o, *rest):
    mark_o[...] = jnp.zeros((8, 128), F32)
    x, g, act, both, w, pw, sem, sem_out = rest
    pairs = [(acth, act), (pwh, pw), (xh, x), (bothh, both), (wh, w), (gh, g)]
    loads = [pltpu.make_async_copy(src, dst, sem.at[i]) for i, (src, dst) in enumerate(pairs)]
    for load in loads:
        load.start()
    for load in loads[:3]:
        load.wait()
    contract = (((1,), (1,)), ((), ()))
    for i in range(3):
        rows = slice(128 * i, 128 * i + 128)
        branch = jnp.dot(act[rows, :], pw[...], preferred_element_type=F32)
        branch = jnp.where(inside(info_ref, 128 * i, (128, 1024)), branch, 0.0)
        act[rows, :] = (x[rows, :].astype(F32) + branch).astype(BF)
    first = pltpu.make_async_copy(act, out_o, sem_out.at[0])
    first.start()
    for load in loads[3:]:
        load.wait()
    for i in range(3):
        rows = slice(128 * i, 128 * i + 128)
        grad = lax.dot_general(both[0, rows, :], w[:, :1024], contract, preferred_element_type=F32)
        grad = grad + lax.dot_general(both[1, rows, :], w[:, 1024:], contract, preferred_element_type=F32)
        u = grad * gain_ref[...]
        values = x[rows, :].astype(F32)
        center = values - jnp.mean(values, axis=-1, keepdims=True)
        scale = lax.rsqrt(jnp.mean(center * center, axis=-1, keepdims=True) + eps_norm)
        xhat = center * scale
        u = scale * (u - jnp.mean(u, axis=-1, keepdims=True) - xhat * jnp.mean(u * xhat, axis=-1, keepdims=True))
        g[rows, :] = (g[rows, :].astype(F32) + u).astype(BF)
    second = pltpu.make_async_copy(g, grad_o, sem_out.at[1])
    second.start()
    first.wait()
    second.wait()


def outputs(info, gain, x, g, act, both, w, pw, after_this):
    wide = jax.ShapeDtypeStruct((ROWS, 1024), BF)
    return pl.pallas_call(
        outputs_kernel,
        out_shape=[wide, wide, jax.ShapeDtypeStruct((8, 128), F32)],
        in_specs=[smem_spec(), vmem_spec()] + [hbm_spec()] * 7,
        out_specs=[hbm_spec()] * 2 + [vmem_spec()],
        scratch_shapes=[
            pltpu.VMEM((ROWS, 1024), BF),
            pltpu.VMEM((ROWS, 1024), BF),
            pltpu.VMEM((ROWS, 1024), BF),
            pltpu.VMEM((2, ROWS + 16, 1024), BF),
            pltpu.VMEM((1024, 2048), BF),
            pltpu.VMEM((1024, 1024), BF),
            pltpu.SemaphoreType.DMA((6,)),
            pltpu.SemaphoreType.DMA((2,)),
        ],
        name="outputs",
    )(info, gain, x, g, act, both, w, pw, after_this)


def local(features, cotangent, lengths, norm_gain, lift_weight, conv_kernel, proj_weight):
    x, g = features[0], cotangent[0]
    frames, width = x.shape
    edge = jnp.stack([x[-EDGE:], g[-EDGE:]])
    start = jnp.stack([x[:EDGE], g[:EDGE]])
    before = lax.ppermute(edge, ("yh", "x"), [(i, i + 1) for i in range(7)])
    after = lax.ppermute(start, ("yh", "x"), [(i + 1, i) for i in range(7)])
    gain = norm_gain[None]
    normed, gb_keep, gb_give = early(lengths, gain, x, g)
    normed_other = pair_swap(normed)
    gb_other = pair_swap(gb_give)
    activated, both, keep, give = forward_backward(
        lengths, gain, conv_kernel, normed, gb_keep, gb_give, before, after, lift_weight, proj_weight
    )
    keep_other = pair_swap(give)
    act_other = pair_swap(activated)
    chunk = (2 * width * width + width * width + 10 * width) // 256
    operands = (normed, normed_other, keep, keep_other, activated, act_other, gb_keep, gb_other, lift_weight)
    blocks = weight_blocks(gain, operands)
    output, grad_features, mark = outputs(lengths, gain, x, g, activated, both, lift_weight, proj_weight, blocks[0])
    grads = own_chunk(reduce_terms(blocks, mark), chunk, float(frames * 256) ** (-0.5))
    return output[None], grad_features[None], grads


def solution(mesh):
    fine = Mesh(mesh.devices.reshape(2, 4, 8, 2, 2), ALL)
    act = P(("z", "yl", "c"), ("yh", "x"), None)

    return jax.shard_map(
        local,
        mesh=fine,
        in_specs=(act, act, P(("z", "yl", "c")), P(), P(), P(), P()),
        out_specs=(act, act, P(ALL)),
        check_vma=False,
    )
```

```python
import functools

import jax
import jax.numpy as jnp
from jax import lax
from jax.experimental import pallas as pl
from jax.experimental.pallas import tpu as pltpu
from jax.sharding import Mesh, PartitionSpec as P


eps_norm = 1e-05
BF = jnp.bfloat16
F32 = jnp.float32
WIN = 12


def any_spec():
    return pl.BlockSpec(memory_space=pl.ANY)


def hbm_spec():
    return pl.BlockSpec(memory_space=pltpu.HBM)


def vmem_spec():
    return pl.BlockSpec(memory_space=pltpu.VMEM)


def smem_spec():
    return pl.BlockSpec(memory_space=pltpu.SMEM)


def place(part_a, part_b, wide, begin, count):
    at = 0
    while at < count:
        window, inside = divmod(begin + at, 96)
        low = inside % 48
        step = min(48 - low, count - at)
        rows = wide[at : at + step, :].astype(BF)
        yh, rest = divmod(window, 64)
        if inside < 48:
            part_a[yh, rest, low : low + step, :] = rows
        else:
            part_b[yh * 2 + rest % 2, rest // 2, low : low + step, :] = rows
        at += step


def weight_kernel(gain_ref, n0h, n1h, k0h, k1h, a0h, a1h, g0h, g1h, wh, *rest):
    outs, rest = rest[:8], rest[8:]
    n0, n1, k0, k1, a0, a1, g0, g1, w, part_a, part_b, wide, extra, sem, sem_in = rest
    core = lax.axis_index("c")
    loads = [
        pltpu.make_async_copy(src, dst, sem_in.at[i])
        for i, (src, dst) in enumerate(
            zip(
                (a0h, g0h, a1h, g1h, n0h, k0h, n1h, k1h, wh.at[:, pl.ds(core * 1024, 1024)]),
                (a0, g0, a1, g1, n0, k0, n1, k1, w),
            )
        )
    ]
    for load in loads[:4]:
        load.start()
    contract = (((0,), (0,)), ((), ()))
    for load in loads[:4]:
        load.wait()
    for load in loads[4:]:
        load.start()
    for m in range(4):
        cols = slice(256 * m, 256 * m + 256)
        done = lax.dot_general(a0[:, cols], g0[...], contract, preferred_element_type=F32)
        done = done + lax.dot_general(a1[:, cols], g1[...], contract, preferred_element_type=F32)
        for v in range(4):
            wide[pl.ds(v, 256, stride=4), :] = done[:, 128 * v : 128 * v + 128]
        place(part_a, part_b, wide, 8192 + 1024 * m, 1024)
    for load in loads[4:]:
        load.wait()
    gains = []
    for m in range(4):
        cols = slice(256 * m, 256 * m + 256)
        done = lax.dot_general(n0[:, cols], k0[0:ROWS, :], contract, preferred_element_type=F32)
        done = done + lax.dot_general(n1[:, cols], k1[0:ROWS, :], contract, preferred_element_type=F32)
        folded = jnp.zeros((256, 128), F32)
        for v in range(8):
            piece = done[:, 128 * v : 128 * v + 128]
            wide[pl.ds(v, 256, stride=8), :] = piece
            folded = folded + piece * w[cols, 128 * v : 128 * v + 128].astype(F32)
        gains.append(jnp.sum(folded.T, axis=0, keepdims=True))
        place(part_a, part_b, wide, 2048 * m, 2048)
    for m in range(4):
        for j in range(2):
            at = 256 * m + 128 * j
            extra[40 + 2 * m + j : 41 + 2 * m + j, :] = gains[m][:, 128 * j : 128 * j + 128] / gain_ref[:, at : at + 128]
    taps = k0[ROWS:, :].astype(F32) + k1[ROWS:, :].astype(F32)
    for p in range(5):
        for v in range(8):
            extra[8 * p + v : 8 * p + v + 1, :] = taps[p : p + 1, 128 * v : 128 * v + 128]
    small = part_b.at[4, 0]
    small[...] = extra[...].astype(BF)
    copies = []
    for s in range(4):
        x = (lax.axis_index("x") + s) % 4
        y = (lax.axis_index(("yh", "yl")) + s) % 4
        for yh in range(2):
            copies.append((part_a.at[yh, pl.ds(x * 16, 16)], outs[s].at[pl.ds(yh * 16, 16)]))
        copies.append((small, outs[s].at[32]))
        copies.append((part_b.at[y], outs[4 + s]))
    copies = [pltpu.make_async_copy(src, dst, sem.at[i]) for i, (src, dst) in enumerate(copies)]
    for copy in copies:
        copy.start()
    for copy in copies:
        copy.wait()


def weight_blocks(gain, operands):
    blocks = [jax.ShapeDtypeStruct((33, 48, 128), BF)] * 4 + [jax.ShapeDtypeStruct((32, 48, 128), BF)] * 4
    return pl.pallas_call(
        weight_kernel,
        out_shape=blocks,
        in_specs=[vmem_spec()] + [hbm_spec(), any_spec()] * 4 + [hbm_spec()],
        out_specs=[hbm_spec()] * 8,
        scratch_shapes=[pltpu.VMEM(o.shape, BF) for o in operands[:8]]
        + [
            pltpu.VMEM((1024, 1024), BF),
            pltpu.VMEM((2, 64, 48, 128), BF),
            pltpu.VMEM((5, 32, 48, 128), BF),
            pltpu.VMEM((2048, 128), F32),
            pltpu.VMEM((48, 128), F32),
            pltpu.SemaphoreType.DMA((16,)),
            pltpu.SemaphoreType.DMA((9,)),
        ],
        compiler_params=pltpu.CompilerParams(vmem_limit_bytes=57 << 20),
        name="weight_grads",
    )(gain, *operands)


def sum_of(refs, index):
    total = refs[0][index].astype(F32)
    for ref in refs[1:]:
        total = total + ref[index].astype(F32)
    return total.astype(BF)


def first_x_kernel(i0, i1, i2, i3, mark, *outs):
    for s in range(4):
        y = (lax.axis_index(("yh", "yl")) + s) % 4
        base = (y // 2) * 16 + y % 2
        for z in range(8):
            outs[s][z] = sum_of((i0, i1, i2, i3), base + 2 * z)
        outs[s][8] = sum_of((i0, i1, i2, i3), 32)


def first_y_kernel(i0, i1, i2, i3, *outs):
    for s in range(4):
        x = (lax.axis_index("x") + s) % 4
        for z in range(8):
            outs[s][z] = sum_of((i0, i1, i2, i3), x * 8 + z)


def second_kernel(a0, a1, a2, a3, b0, b1, b2, b3, out):
    small = sum_of((a0, a1, a2, a3), 8)
    for z in range(8):
        out[z, 0:48, :] = sum_of((a0, a1, a2, a3), z)
        out[z, 48:96, :] = sum_of((b0, b1, b2, b3), z)
        out[z, 96:144, :] = small


def send(blocks, axes):
    n = 4
    got = [blocks[0]]
    for step in (2, 1, 3):
        got.append(lax.ppermute(blocks[step], axes, [(i, (i + step) % n) for i in range(n)]))
    return got


def reduce_terms(blocks, mark):
    got_x = send(blocks[:4], "x")
    got_y = send(blocks[4:], ("yh", "yl"))
    block9 = jax.ShapeDtypeStruct((9, 48, 128), BF)
    block8 = jax.ShapeDtypeStruct((8, 48, 128), BF)
    after_x = pl.pallas_call(
        first_x_kernel,
        out_shape=[block9] * 4,
        in_specs=[vmem_spec()] * 4 + [any_spec()],
        out_specs=[vmem_spec()] * 4,
        compiler_params=pltpu.CompilerParams(vmem_limit_bytes=8 << 20),
        name="sum_after_x",
    )(*got_x, mark)
    after_y = pl.pallas_call(
        first_y_kernel,
        out_shape=[block8] * 4,
        in_specs=[vmem_spec()] * 4,
        out_specs=[vmem_spec()] * 4,
        compiler_params=pltpu.CompilerParams(vmem_limit_bytes=8 << 20),
        name="sum_after_y",
    )(*got_y)
    got_a = send(after_x, ("yh", "yl"))
    got_b = send(after_y, "x")
    ready = pl.pallas_call(
        second_kernel,
        out_shape=jax.ShapeDtypeStruct((8, 144, 128), BF),
        in_specs=[vmem_spec()] * 8,
        out_specs=vmem_spec(),
        compiler_params=pltpu.CompilerParams(vmem_limit_bytes=6 << 20),
        name="sum_before_z",
    )(*got_a, *got_b)
    return lax.all_to_all(ready, "z", split_axis=0, concat_axis=0, tiled=True)


ALL = ("yh", "x", "z", "yl", "c")


def total_kernel(parts, total):
    done = parts[0].astype(F32)
    for z in range(1, 8):
        done = done + parts[z].astype(F32)
    total[...] = done


def chunk_kernel(own, other, follow, out, half0, half1, flat, *, chunk, scale):
    core = lax.axis_index("c")
    chip = lax.axis_index(("yh", "x", "z", "yl"))
    first = core == 0
    mine, others = own[...], other[...]
    half0[0:96, :] = jnp.where(first, mine[0:96], others[0:96])
    half1[0:96, :] = jnp.where(first, others[0:96], mine[0:96])
    small0 = jnp.where(first, mine[96:144], others[96:144])
    small1 = jnp.where(first, others[96:144], mine[96:144])
    both = small0[40:48] + small1[40:48]
    last = chip == 127
    half0[96:144, :] = jnp.where(last, small0, follow[0:48])
    half1[96:144, :] = jnp.where(last, small1, follow[48:96])

    @pl.when(last)
    def _():
        half1[128:136, :] = both

    for p in range(18):
        pair = chip * WIN + p
        proj = (pair >= 1024) & (pair < 1536)
        for h, half in ((0, half0), (1, half1)):
            tile = half[8 * p : 8 * p + 8, :] * scale

            @pl.when(proj)
            def _(p=p, h=h, tile=tile):
                flat[16 * p + 4 * h : 16 * p + 4 * h + 4, :] = tile[0:4]
                flat[16 * p + 8 + 4 * h : 16 * p + 12 + 4 * h, :] = tile[4:8]

            @pl.when(jnp.logical_not(proj))
            def _(p=p, h=h, tile=tile):
                flat[16 * p + 8 * h : 16 * p + 8 * h + 8, :] = tile

    begin = (2 * chip + core) * chunk - chip * (WIN * 2048)
    row, lane = begin // 128, begin % 128
    low = pltpu.roll(flat[pl.ds(row, 104), :], (128 - lane) % 128, axis=1)
    high = pltpu.roll(flat[pl.ds(row + 1, 104), :], (128 - lane) % 128, axis=1)
    at = lax.broadcasted_iota(jnp.int32, (104, 128), 1)
    out[...] = jnp.where(at < 128 - lane, low, high)


def own_chunk(swapped, chunk, grad_scale):
    total = pl.pallas_call(
        total_kernel,
        out_shape=jax.ShapeDtypeStruct((144, 128), F32),
        in_specs=[vmem_spec()],
        out_specs=vmem_spec(),
        compiler_params=pltpu.CompilerParams(vmem_limit_bytes=4 << 20),
        name="sum_after_z",
    )(swapped)
    other = lax.ppermute(total, "c", [(0, 1), (1, 0)])
    heads = jnp.concatenate([other[:48], total[:48]])
    follow = lax.ppermute(heads, ALL, [(2 * j + 1, 2 * j - 1) for j in range(1, 128)])
    out = pl.pallas_call(
        functools.partial(chunk_kernel, chunk=chunk, scale=grad_scale),
        out_shape=jax.ShapeDtypeStruct((104, 128), F32),
        in_specs=[vmem_spec()] * 3,
        out_specs=vmem_spec(),
        scratch_shapes=[pltpu.VMEM((144, 128), F32), pltpu.VMEM((144, 128), F32), pltpu.VMEM((312, 128), F32)],
        compiler_params=pltpu.CompilerParams(vmem_limit_bytes=4 << 20),
        name="own_chunk",
    )(total, other, follow)
    return out.reshape(-1)[:chunk]


def pair_swap(array):
    return lax.ppermute(array, "c", [(0, 1), (1, 0)])


ROWS = 384
EDGE = 16
LONG = ROWS + 2 * EDGE


def inside(length_ref, first, shape):
    at = lax.axis_index(("yh", "x")) * ROWS + first + lax.broadcasted_iota(jnp.int32, shape, 0)
    return (at >= 0) & (at < length_ref[0])


def normed_rows(rows, gain):
    values = rows.astype(F32)
    center = values - jnp.mean(values, axis=-1, keepdims=True)
    scale = lax.rsqrt(jnp.mean(center * center, axis=-1, keepdims=True) + eps_norm)
    return (center * scale * gain).astype(BF)


PART = 96


def early_kernel(length_ref, gain_ref, xh, gh, normed_o, keep_o, give_o, x, g, sem, sem_out):
    core = lax.axis_index("c")
    parts = [pl.ds(PART * i, PART) for i in range(ROWS // PART)]
    loads = [pltpu.make_async_copy(xh.at[p], x.at[p], sem.at[0, i]) for i, p in enumerate(parts)]
    loads += [pltpu.make_async_copy(gh.at[p], g.at[p], sem.at[1, i]) for i, p in enumerate(parts)]
    for load in loads:
        load.start()
    gain = gain_ref[...]
    sends = []
    for i, p in enumerate(parts):
        loads[i].wait()
        for j in range(0, PART, 16):
            rows = pl.ds(PART * i + j, 16)
            x[rows, :] = normed_rows(x[rows, :], gain)
        sends.append(pltpu.make_async_copy(x.at[p], normed_o.at[p], sem_out.at[0, i]))
        sends[-1].start()
    for i, p in enumerate(parts):
        loads[len(parts) + i].wait()
        valid = inside(length_ref, PART * i, (PART, 1024))
        g[p, :] = jnp.where(valid, g[p, :].astype(F32), 0.0).astype(BF)
        for k, (out, at) in enumerate(((keep_o, core * 512), (give_o, 512 - core * 512))):
            sends.append(pltpu.make_async_copy(g.at[p, pl.ds(at, 512)], out.at[p], sem_out.at[1 + k, i]))
            sends[-1].start()
    for copy in sends:
        copy.wait()


def early(lengths, gain, x, g):
    wide = jax.ShapeDtypeStruct((ROWS, 1024), BF)
    half = jax.ShapeDtypeStruct((ROWS, 512), BF)
    return pl.pallas_call(
        early_kernel,
        out_shape=[wide, half, half],
        in_specs=[smem_spec(), vmem_spec()] + [hbm_spec()] * 2,
        out_specs=[hbm_spec()] * 3,
        scratch_shapes=[
            pltpu.VMEM((ROWS, 1024), BF),
            pltpu.VMEM((ROWS, 1024), BF),
            pltpu.SemaphoreType.DMA((2, ROWS // PART)),
            pltpu.SemaphoreType.DMA((3, ROWS // PART)),
        ],
        name="early",
    )(lengths, gain, x, g)


def main_kernel(info_ref, gain_ref, taps_ref, nh, gkh, ggh, beforeh, afterh, wh, pwh, *rest):
    act_o, both_o, keep_o, give_o = rest[:4]
    gs, w, pw, nm, act, both, lifts0, lifts1, gat, gcon, acf, mask, krows, sem, sem_out = rest[4:]
    core = lax.axis_index("c")
    pairs = [
        (beforeh.at[0], nm.at[pl.ds(0, EDGE)]),
        (afterh.at[0], nm.at[pl.ds(EDGE + ROWS, EDGE)]),
        (beforeh.at[1], gs.at[pl.ds(0, EDGE)]),
        (afterh.at[1], gs.at[pl.ds(EDGE + ROWS, EDGE)]),
        (nh, nm.at[pl.ds(EDGE, ROWS)]),
        (gkh, gs.at[pl.ds(EDGE, ROWS), pl.ds(core * 512, 512)]),
        (ggh, gs.at[pl.ds(EDGE, ROWS), pl.ds(512 - core * 512, 512)]),
    ]
    for n in range(4):
        pairs.append((wh.at[:, pl.ds(256 * n, 256)], w.at[:, pl.ds(256 * n, 256)]))
        pairs.append((wh.at[:, pl.ds(1024 + 256 * n, 256)], w.at[:, pl.ds(1024 + 256 * n, 256)]))
        pairs.append((pwh.at[pl.ds(256 * n, 256)], pw.at[pl.ds(256 * n, 256)]))
    loads = [pltpu.make_async_copy(src, dst, sem.at[i]) for i, (src, dst) in enumerate(pairs)]
    for load in loads[:10]:
        load.start()
    mask[...] = inside(info_ref, -EDGE, (LONG, 128)).astype(F32)
    krows[...] = jnp.zeros((2, 16, 1024), F32)
    for load in loads[:4]:
        load.wait()
    for first in (0, EDGE + ROWS):
        rows = pl.ds(first, EDGE)
        nm[rows, :] = normed_rows(nm[rows, :], gain_ref[...])
        gs[rows, :] = jnp.where(inside(info_ref, first - EDGE, (EDGE, 1024)), gs[rows, :].astype(F32), 0.0).astype(BF)
    for load in loads[4:7]:
        load.wait()
    for load in loads[10:]:
        load.start()

    def multiply(n, lifts):
        for load in loads[7 + 3 * n : 10 + 3 * n]:
            load.wait()
        lanes = slice(256 * n, 256 * n + 256)
        lift_value = jnp.dot(nm[...], w[:, lanes], preferred_element_type=F32)
        lift_gate = jnp.dot(nm[...], w[:, 1024 + 256 * n : 1280 + 256 * n], preferred_element_type=F32)
        back = lax.dot_general(gs[...], pw[lanes, :], (((1,), (1,)), ((), ())), preferred_element_type=F32)
        for h in range(2):
            lifts[h] = lift_value[:, 128 * h : 128 * h + 128]
            lifts[2 + h] = lift_gate[:, 128 * h : 128 * h + 128]
            lifts[4 + h] = back[:, 128 * h : 128 * h + 128]

    def channels(n, h, lifts):
        at = 256 * n + 128 * h
        taps = [taps_ref[k : k + 1, at : at + 128] for k in range(9)]
        for i in range(10):
            rows = pl.ds(8 + 40 * i, 40)
            s = jax.nn.sigmoid(lifts[2 + h, rows, :])
            lifts[2 + h, rows, :] = s
            gat[h, rows, :] = (lifts[h, rows, :] * s * mask[rows, :]).astype(BF).astype(F32)
        for i in range(7):
            r = 12 + 56 * i
            rows = pl.ds(r, 56)
            conv = taps[0] * gat[h, pl.ds(r - 4, 56), :]
            for k in range(1, 9):
                conv = conv + taps[k] * gat[h, pl.ds(r + k - 4, 56), :]
            s = jax.nn.sigmoid(conv)
            active = conv * s
            acf[h, rows, :] = active
            grad = lifts[4 + h, rows, :] * (s + active * (1.0 - s))
            gcon[h, rows, :] = grad.astype(BF).astype(F32)
        sums = [jnp.zeros((8, 128), F32) for _ in range(9)]
        for i in range(8):
            r = EDGE + 48 * i
            rows = pl.ds(r, 48)
            own = pl.ds(r - EDGE, 48)
            grad = taps[0] * gcon[h, pl.ds(r + 4, 48), :]
            for k in range(1, 9):
                grad = grad + taps[k] * gcon[h, pl.ds(r + 4 - k, 48), :]
            s = lifts[2 + h, rows, :]
            first = grad * mask[rows, :] * s
            both[0, own, at : at + 128] = first.astype(BF)
            both[1, own, at : at + 128] = (first * lifts[h, rows, :] * (1.0 - s)).astype(BF)
            act[own, at : at + 128] = acf[h, rows, :].astype(BF)
            here = gcon[h, rows, :]
            for k in range(9):
                product = here * gat[h, pl.ds(r + k - 4, 48), :]
                sums[k] = sums[k] + jnp.sum(product.reshape(6, 8, 128), axis=0)
        for k in range(9):
            krows[k % 2, k // 2 : k // 2 + 1, at : at + 128] = jnp.sum(sums[k], axis=0, keepdims=True)

    lifts = (lifts0, lifts1)
    multiply(0, lifts0)
    for n in range(4):
        if n < 3:
            multiply(n + 1, lifts[(n + 1) % 2])
        for h in range(2):
            channels(n, h, lifts[n % 2])
    for c in range(2):
        both[c, ROWS:, :] = krows[c].astype(BF)
    sends = [
        (both.at[1 - core], give_o),
        (act, act_o),
        (both.at[core], keep_o),
        (both, both_o),
    ]
    sends = [pltpu.make_async_copy(src, dst, sem_out.at[i]) for i, (src, dst) in enumerate(sends)]
    for copy in sends:
        copy.start()
    for copy in sends:
        copy.wait()


def forward_backward(lengths, gain, taps, normed, gb_keep, gb_give, before, after, w, pw):
    wide = jax.ShapeDtypeStruct((ROWS, 1024), BF)
    tall = jax.ShapeDtypeStruct((ROWS + 16, 1024), BF)
    return pl.pallas_call(
        main_kernel,
        out_shape=[wide, jax.ShapeDtypeStruct((2, ROWS + 16, 1024), BF), tall, tall],
        in_specs=[smem_spec(), vmem_spec(), vmem_spec()] + [hbm_spec()] * 7,
        out_specs=[hbm_spec()] * 4,
        scratch_shapes=[
            pltpu.VMEM((LONG, 1024), BF),
            pltpu.VMEM((1024, 2048), BF),
            pltpu.VMEM((1024, 1024), BF),
            pltpu.VMEM((LONG, 1024), BF),
            pltpu.VMEM((ROWS, 1024), BF),
            pltpu.VMEM((2, ROWS + 16, 1024), BF),
            pltpu.VMEM((6, LONG, 128), F32),
            pltpu.VMEM((6, LONG, 128), F32),
            pltpu.VMEM((2, LONG, 128), F32),
            pltpu.VMEM((2, LONG, 128), F32),
            pltpu.VMEM((2, LONG, 128), F32),
            pltpu.VMEM((LONG, 128), F32),
            pltpu.VMEM((2, 16, 1024), F32),
            pltpu.SemaphoreType.DMA((19,)),
            pltpu.SemaphoreType.DMA((4,)),
        ],
        name="forward_backward",
    )(lengths, gain, taps, normed, gb_keep, gb_give, before, after, w, pw)


def outputs_kernel(info_ref, gain_ref, xh, gh, acth, bothh, wh, pwh, after_this, out_o, grad_o, mark_o, *rest):
    mark_o[...] = jnp.zeros((8, 128), F32)
    x, g, act, both, w, pw, sem, sem_out = rest
    pairs = [(acth, act), (pwh, pw), (xh, x), (bothh, both), (wh, w), (gh, g)]
    loads = [pltpu.make_async_copy(src, dst, sem.at[i]) for i, (src, dst) in enumerate(pairs)]
    for load in loads:
        load.start()
    for load in loads[:3]:
        load.wait()
    contract = (((1,), (1,)), ((), ()))
    for i in range(3):
        rows = slice(128 * i, 128 * i + 128)
        branch = jnp.dot(act[rows, :], pw[...], preferred_element_type=F32)
        branch = jnp.where(inside(info_ref, 128 * i, (128, 1024)), branch, 0.0)
        act[rows, :] = (x[rows, :].astype(F32) + branch).astype(BF)
    first = pltpu.make_async_copy(act, out_o, sem_out.at[0])
    first.start()
    for load in loads[3:]:
        load.wait()
    for i in range(3):
        rows = slice(128 * i, 128 * i + 128)
        grad = lax.dot_general(both[0, rows, :], w[:, :1024], contract, preferred_element_type=F32)
        grad = grad + lax.dot_general(both[1, rows, :], w[:, 1024:], contract, preferred_element_type=F32)
        u = grad * gain_ref[...]
        values = x[rows, :].astype(F32)
        center = values - jnp.mean(values, axis=-1, keepdims=True)
        scale = lax.rsqrt(jnp.mean(center * center, axis=-1, keepdims=True) + eps_norm)
        xhat = center * scale
        u = scale * (u - jnp.mean(u, axis=-1, keepdims=True) - xhat * jnp.mean(u * xhat, axis=-1, keepdims=True))
        g[rows, :] = (g[rows, :].astype(F32) + u).astype(BF)
    second = pltpu.make_async_copy(g, grad_o, sem_out.at[1])
    second.start()
    first.wait()
    second.wait()


def outputs(info, gain, x, g, act, both, w, pw, after_this):
    wide = jax.ShapeDtypeStruct((ROWS, 1024), BF)
    return pl.pallas_call(
        outputs_kernel,
        out_shape=[wide, wide, jax.ShapeDtypeStruct((8, 128), F32)],
        in_specs=[smem_spec(), vmem_spec()] + [hbm_spec()] * 7,
        out_specs=[hbm_spec()] * 2 + [vmem_spec()],
        scratch_shapes=[
            pltpu.VMEM((ROWS, 1024), BF),
            pltpu.VMEM((ROWS, 1024), BF),
            pltpu.VMEM((ROWS, 1024), BF),
            pltpu.VMEM((2, ROWS + 16, 1024), BF),
            pltpu.VMEM((1024, 2048), BF),
            pltpu.VMEM((1024, 1024), BF),
            pltpu.SemaphoreType.DMA((6,)),
            pltpu.SemaphoreType.DMA((2,)),
        ],
        name="outputs",
    )(info, gain, x, g, act, both, w, pw, after_this)


def local(features, cotangent, lengths, norm_gain, lift_weight, conv_kernel, proj_weight):
    x, g = features[0], cotangent[0]
    frames, width = x.shape
    edge = jnp.stack([x[-EDGE:], g[-EDGE:]])
    start = jnp.stack([x[:EDGE], g[:EDGE]])
    before = lax.ppermute(edge, ("yh", "x"), [(i, i + 1) for i in range(7)])
    after = lax.ppermute(start, ("yh", "x"), [(i + 1, i) for i in range(7)])
    gain = norm_gain[None]
    normed, gb_keep, gb_give = early(lengths, gain, x, g)
    normed_other = pair_swap(normed)
    gb_other = pair_swap(gb_give)
    activated, both, keep, give = forward_backward(
        lengths, gain, conv_kernel, normed, gb_keep, gb_give, before, after, lift_weight, proj_weight
    )
    keep_other = pair_swap(give)
    act_other = pair_swap(activated)
    chunk = (2 * width * width + width * width + 10 * width) // 256
    operands = (normed, normed_other, keep, keep_other, activated, act_other, gb_keep, gb_other, lift_weight)
    blocks = weight_blocks(gain, operands)
    output, grad_features, mark = outputs(lengths, gain, x, g, activated, both, lift_weight, proj_weight, blocks[0])
    grads = own_chunk(reduce_terms(blocks, mark), chunk, float(frames * 256) ** (-0.5))
    return output[None], grad_features[None], grads


def solution(mesh):
    fine = Mesh(mesh.devices.reshape(2, 4, 8, 2, 2), ALL)
    act = P(("z", "yl", "c"), ("yh", "x"), None)

    return jax.shard_map(
        local,
        mesh=fine,
        in_specs=(act, act, P(("z", "yl", "c")), P(), P(), P(), P()),
        out_specs=(act, act, P(ALL)),
        check_vma=False,
    )
```

```python
import functools

import jax
import jax.numpy as jnp
from jax import lax
from jax.experimental import pallas as pl
from jax.experimental.pallas import tpu as pltpu
from jax.sharding import Mesh, PartitionSpec as P


eps_norm = 1e-05
BF = jnp.bfloat16
F32 = jnp.float32
WIN = 12


def any_spec():
    return pl.BlockSpec(memory_space=pl.ANY)


def hbm_spec():
    return pl.BlockSpec(memory_space=pltpu.HBM)


def vmem_spec():
    return pl.BlockSpec(memory_space=pltpu.VMEM)


def smem_spec():
    return pl.BlockSpec(memory_space=pltpu.SMEM)


def place(part_a, part_b, wide, begin, count):
    at = 0
    while at < count:
        window, inside = divmod(begin + at, 96)
        low = inside % 48
        step = min(48 - low, count - at)
        rows = wide[at : at + step, :].astype(BF)
        yh, rest = divmod(window, 64)
        if inside < 48:
            part_a[yh, rest, low : low + step, :] = rows
        else:
            part_b[yh * 2 + rest % 2, rest // 2, low : low + step, :] = rows
        at += step


def weight_kernel(gain_ref, n0h, n1h, k0h, k1h, a0h, a1h, g0h, g1h, wh, *rest):
    outs, rest = rest[:8], rest[8:]
    n0, n1, k0, k1, a0, a1, g0, g1, w, part_a, part_b, wide, extra, sem, sem_in = rest
    core = lax.axis_index("c")
    loads = [
        pltpu.make_async_copy(src, dst, sem_in.at[i])
        for i, (src, dst) in enumerate(
            zip(
                (a0h, g0h, a1h, g1h, n0h, k0h, n1h, k1h, wh.at[:, pl.ds(core * 1024, 1024)]),
                (a0, g0, a1, g1, n0, k0, n1, k1, w),
            )
        )
    ]
    for load in loads:
        load.start()
    contract = (((0,), (0,)), ((), ()))
    for load in loads[:4]:
        load.wait()
    for m in range(4):
        cols = slice(256 * m, 256 * m + 256)
        done = lax.dot_general(a0[:, cols], g0[...], contract, preferred_element_type=F32)
        done = done + lax.dot_general(a1[:, cols], g1[...], contract, preferred_element_type=F32)
        for v in range(4):
            wide[pl.ds(v, 256, stride=4), :] = done[:, 128 * v : 128 * v + 128]
        place(part_a, part_b, wide, 8192 + 1024 * m, 1024)
    for load in loads[4:]:
        load.wait()
    gains = []
    for m in range(4):
        cols = slice(256 * m, 256 * m + 256)
        done = lax.dot_general(n0[:, cols], k0[0:ROWS, :], contract, preferred_element_type=F32)
        done = done + lax.dot_general(n1[:, cols], k1[0:ROWS, :], contract, preferred_element_type=F32)
        folded = jnp.zeros((256, 128), F32)
        for v in range(8):
            piece = done[:, 128 * v : 128 * v + 128]
            wide[pl.ds(v, 256, stride=8), :] = piece
            folded = folded + piece * w[cols, 128 * v : 128 * v + 128].astype(F32)
        gains.append(jnp.sum(folded.T, axis=0, keepdims=True))
        place(part_a, part_b, wide, 2048 * m, 2048)
    for m in range(4):
        for j in range(2):
            at = 256 * m + 128 * j
            extra[40 + 2 * m + j : 41 + 2 * m + j, :] = gains[m][:, 128 * j : 128 * j + 128] / gain_ref[:, at : at + 128]
    taps = k0[ROWS:, :].astype(F32) + k1[ROWS:, :].astype(F32)
    for p in range(5):
        for v in range(8):
            extra[8 * p + v : 8 * p + v + 1, :] = taps[p : p + 1, 128 * v : 128 * v + 128]
    small = part_b.at[4, 0]
    small[...] = extra[...].astype(BF)
    copies = []
    for s in range(4):
        x = (lax.axis_index("x") + s) % 4
        y = (lax.axis_index(("yh", "yl")) + s) % 4
        for yh in range(2):
            copies.append((part_a.at[yh, pl.ds(x * 16, 16)], outs[s].at[pl.ds(yh * 16, 16)]))
        copies.append((small, outs[s].at[32]))
        copies.append((part_b.at[y], outs[4 + s]))
    copies = [pltpu.make_async_copy(src, dst, sem.at[i]) for i, (src, dst) in enumerate(copies)]
    for copy in copies:
        copy.start()
    for copy in copies:
        copy.wait()


def weight_blocks(gain, operands):
    blocks = [jax.ShapeDtypeStruct((33, 48, 128), BF)] * 4 + [jax.ShapeDtypeStruct((32, 48, 128), BF)] * 4
    return pl.pallas_call(
        weight_kernel,
        out_shape=blocks,
        in_specs=[vmem_spec()] + [hbm_spec(), any_spec()] * 4 + [hbm_spec()],
        out_specs=[hbm_spec()] * 8,
        scratch_shapes=[pltpu.VMEM(o.shape, BF) for o in operands[:8]]
        + [
            pltpu.VMEM((1024, 1024), BF),
            pltpu.VMEM((2, 64, 48, 128), BF),
            pltpu.VMEM((5, 32, 48, 128), BF),
            pltpu.VMEM((2048, 128), F32),
            pltpu.VMEM((48, 128), F32),
            pltpu.SemaphoreType.DMA((16,)),
            pltpu.SemaphoreType.DMA((9,)),
        ],
        compiler_params=pltpu.CompilerParams(vmem_limit_bytes=57 << 20),
        name="weight_grads",
    )(gain, *operands)


def sum_of(refs, index):
    total = refs[0][index].astype(F32)
    for ref in refs[1:]:
        total = total + ref[index].astype(F32)
    return total.astype(BF)


def first_x_kernel(i0, i1, i2, i3, mark, *outs):
    for s in range(4):
        y = (lax.axis_index(("yh", "yl")) + s) % 4
        base = (y // 2) * 16 + y % 2
        for z in range(8):
            outs[s][z] = sum_of((i0, i1, i2, i3), base + 2 * z)
        outs[s][8] = sum_of((i0, i1, i2, i3), 32)


def first_y_kernel(i0, i1, i2, i3, *outs):
    for s in range(4):
        x = (lax.axis_index("x") + s) % 4
        for z in range(8):
            outs[s][z] = sum_of((i0, i1, i2, i3), x * 8 + z)


def second_kernel(a0, a1, a2, a3, b0, b1, b2, b3, out):
    small = sum_of((a0, a1, a2, a3), 8)
    for z in range(8):
        out[z, 0:48, :] = sum_of((a0, a1, a2, a3), z)
        out[z, 48:96, :] = sum_of((b0, b1, b2, b3), z)
        out[z, 96:144, :] = small


def send(blocks, axes):
    n = 4
    got = [blocks[0]]
    for step in (2, 1, 3):
        got.append(lax.ppermute(blocks[step], axes, [(i, (i + step) % n) for i in range(n)]))
    return got


def reduce_terms(blocks, mark):
    got_x = send(blocks[:4], "x")
    got_y = send(blocks[4:], ("yh", "yl"))
    block9 = jax.ShapeDtypeStruct((9, 48, 128), BF)
    block8 = jax.ShapeDtypeStruct((8, 48, 128), BF)
    after_x = pl.pallas_call(
        first_x_kernel,
        out_shape=[block9] * 4,
        in_specs=[vmem_spec()] * 4 + [any_spec()],
        out_specs=[vmem_spec()] * 4,
        compiler_params=pltpu.CompilerParams(vmem_limit_bytes=8 << 20),
        name="sum_after_x",
    )(*got_x, mark)
    after_y = pl.pallas_call(
        first_y_kernel,
        out_shape=[block8] * 4,
        in_specs=[vmem_spec()] * 4,
        out_specs=[vmem_spec()] * 4,
        compiler_params=pltpu.CompilerParams(vmem_limit_bytes=8 << 20),
        name="sum_after_y",
    )(*got_y)
    got_a = send(after_x, ("yh", "yl"))
    got_b = send(after_y, "x")
    ready = pl.pallas_call(
        second_kernel,
        out_shape=jax.ShapeDtypeStruct((8, 144, 128), BF),
        in_specs=[vmem_spec()] * 8,
        out_specs=vmem_spec(),
        compiler_params=pltpu.CompilerParams(vmem_limit_bytes=6 << 20),
        name="sum_before_z",
    )(*got_a, *got_b)
    return lax.all_to_all(ready, "z", split_axis=0, concat_axis=0, tiled=True)


ALL = ("yh", "x", "z", "yl", "c")


def total_kernel(parts, total):
    done = parts[0].astype(F32)
    for z in range(1, 8):
        done = done + parts[z].astype(F32)
    total[...] = done


def chunk_kernel(own, other, follow, out, half0, half1, flat, *, chunk, scale):
    core = lax.axis_index("c")
    chip = lax.axis_index(("yh", "x", "z", "yl"))
    first = core == 0
    mine, others = own[...], other[...]
    half0[0:96, :] = jnp.where(first, mine[0:96], others[0:96])
    half1[0:96, :] = jnp.where(first, others[0:96], mine[0:96])
    small0 = jnp.where(first, mine[96:144], others[96:144])
    small1 = jnp.where(first, others[96:144], mine[96:144])
    both = small0[40:48] + small1[40:48]
    last = chip == 127
    half0[96:144, :] = jnp.where(last, small0, follow[0:48])
    half1[96:144, :] = jnp.where(last, small1, follow[48:96])

    @pl.when(last)
    def _():
        half1[128:136, :] = both

    for p in range(18):
        pair = chip * WIN + p
        proj = (pair >= 1024) & (pair < 1536)
        for h, half in ((0, half0), (1, half1)):
            tile = half[8 * p : 8 * p + 8, :] * scale

            @pl.when(proj)
            def _(p=p, h=h, tile=tile):
                flat[16 * p + 4 * h : 16 * p + 4 * h + 4, :] = tile[0:4]
                flat[16 * p + 8 + 4 * h : 16 * p + 12 + 4 * h, :] = tile[4:8]

            @pl.when(jnp.logical_not(proj))
            def _(p=p, h=h, tile=tile):
                flat[16 * p + 8 * h : 16 * p + 8 * h + 8, :] = tile

    begin = (2 * chip + core) * chunk - chip * (WIN * 2048)
    row, lane = begin // 128, begin % 128
    low = pltpu.roll(flat[pl.ds(row, 104), :], (128 - lane) % 128, axis=1)
    high = pltpu.roll(flat[pl.ds(row + 1, 104), :], (128 - lane) % 128, axis=1)
    at = lax.broadcasted_iota(jnp.int32, (104, 128), 1)
    out[...] = jnp.where(at < 128 - lane, low, high)


def own_chunk(swapped, chunk, grad_scale):
    total = pl.pallas_call(
        total_kernel,
        out_shape=jax.ShapeDtypeStruct((144, 128), F32),
        in_specs=[vmem_spec()],
        out_specs=vmem_spec(),
        compiler_params=pltpu.CompilerParams(vmem_limit_bytes=4 << 20),
        name="sum_after_z",
    )(swapped)
    other = lax.ppermute(total, "c", [(0, 1), (1, 0)])
    heads = jnp.concatenate([other[:48], total[:48]])
    follow = lax.ppermute(heads, ALL, [(2 * j + 1, 2 * j - 1) for j in range(1, 128)])
    out = pl.pallas_call(
        functools.partial(chunk_kernel, chunk=chunk, scale=grad_scale),
        out_shape=jax.ShapeDtypeStruct((104, 128), F32),
        in_specs=[vmem_spec()] * 3,
        out_specs=vmem_spec(),
        scratch_shapes=[pltpu.VMEM((144, 128), F32), pltpu.VMEM((144, 128), F32), pltpu.VMEM((312, 128), F32)],
        compiler_params=pltpu.CompilerParams(vmem_limit_bytes=4 << 20),
        name="own_chunk",
    )(total, other, follow)
    return out.reshape(-1)[:chunk]


def pair_swap(array):
    return lax.ppermute(array, "c", [(0, 1), (1, 0)])


ROWS = 384
EDGE = 16
LONG = ROWS + 2 * EDGE


def inside(length_ref, first, shape):
    at = lax.axis_index(("yh", "x")) * ROWS + first + lax.broadcasted_iota(jnp.int32, shape, 0)
    return (at >= 0) & (at < length_ref[0])


def normed_rows(rows, gain):
    values = rows.astype(F32)
    center = values - jnp.mean(values, axis=-1, keepdims=True)
    scale = lax.rsqrt(jnp.mean(center * center, axis=-1, keepdims=True) + eps_norm)
    return (center * scale * gain).astype(BF)


PART = 96


def early_kernel(length_ref, gain_ref, xh, gh, normed_o, keep_o, give_o, x, g, sem, sem_out):
    core = lax.axis_index("c")
    parts = [pl.ds(PART * i, PART) for i in range(ROWS // PART)]
    loads = [pltpu.make_async_copy(xh.at[p], x.at[p], sem.at[0, i]) for i, p in enumerate(parts)]
    loads += [pltpu.make_async_copy(gh.at[p], g.at[p], sem.at[1, i]) for i, p in enumerate(parts)]
    for load in loads:
        load.start()
    gain = gain_ref[...]
    sends = []
    for i, p in enumerate(parts):
        loads[i].wait()
        for j in range(0, PART, 16):
            rows = pl.ds(PART * i + j, 16)
            x[rows, :] = normed_rows(x[rows, :], gain)
        sends.append(pltpu.make_async_copy(x.at[p], normed_o.at[p], sem_out.at[0, i]))
        sends[-1].start()
    for i, p in enumerate(parts):
        loads[len(parts) + i].wait()
        valid = inside(length_ref, PART * i, (PART, 1024))
        g[p, :] = jnp.where(valid, g[p, :].astype(F32), 0.0).astype(BF)
        for k, (out, at) in enumerate(((keep_o, core * 512), (give_o, 512 - core * 512))):
            sends.append(pltpu.make_async_copy(g.at[p, pl.ds(at, 512)], out.at[p], sem_out.at[1 + k, i]))
            sends[-1].start()
    for copy in sends:
        copy.wait()


def early(lengths, gain, x, g):
    wide = jax.ShapeDtypeStruct((ROWS, 1024), BF)
    half = jax.ShapeDtypeStruct((ROWS, 512), BF)
    return pl.pallas_call(
        early_kernel,
        out_shape=[wide, half, half],
        in_specs=[smem_spec(), vmem_spec()] + [hbm_spec()] * 2,
        out_specs=[hbm_spec()] * 3,
        scratch_shapes=[
            pltpu.VMEM((ROWS, 1024), BF),
            pltpu.VMEM((ROWS, 1024), BF),
            pltpu.SemaphoreType.DMA((2, ROWS // PART)),
            pltpu.SemaphoreType.DMA((3, ROWS // PART)),
        ],
        name="early",
    )(lengths, gain, x, g)


def main_kernel(info_ref, gain_ref, taps_ref, nh, gkh, ggh, beforeh, afterh, wh, pwh, *rest):
    act_o, both_o, keep_o, give_o = rest[:4]
    gs, w, pw, nm, act, both, lifts0, lifts1, gat, gcon, acf, mask, krows, sem, sem_out = rest[4:]
    core = lax.axis_index("c")
    pairs = [
        (beforeh.at[0], nm.at[pl.ds(0, EDGE)]),
        (afterh.at[0], nm.at[pl.ds(EDGE + ROWS, EDGE)]),
        (beforeh.at[1], gs.at[pl.ds(0, EDGE)]),
        (afterh.at[1], gs.at[pl.ds(EDGE + ROWS, EDGE)]),
        (nh, nm.at[pl.ds(EDGE, ROWS)]),
        (gkh, gs.at[pl.ds(EDGE, ROWS), pl.ds(core * 512, 512)]),
        (ggh, gs.at[pl.ds(EDGE, ROWS), pl.ds(512 - core * 512, 512)]),
    ]
    for n in range(4):
        pairs.append((wh.at[:, pl.ds(256 * n, 256)], w.at[:, pl.ds(256 * n, 256)]))
        pairs.append((wh.at[:, pl.ds(1024 + 256 * n, 256)], w.at[:, pl.ds(1024 + 256 * n, 256)]))
        pairs.append((pwh.at[pl.ds(256 * n, 256)], pw.at[pl.ds(256 * n, 256)]))
    loads = [pltpu.make_async_copy(src, dst, sem.at[i]) for i, (src, dst) in enumerate(pairs)]
    for load in loads:
        load.start()
    mask[...] = inside(info_ref, -EDGE, (LONG, 128)).astype(F32)
    krows[...] = jnp.zeros((2, 16, 1024), F32)
    for load in loads[:4]:
        load.wait()
    for first in (0, EDGE + ROWS):
        rows = pl.ds(first, EDGE)
        nm[rows, :] = normed_rows(nm[rows, :], gain_ref[...])
        gs[rows, :] = jnp.where(inside(info_ref, first - EDGE, (EDGE, 1024)), gs[rows, :].astype(F32), 0.0).astype(BF)
    for load in loads[4:7]:
        load.wait()

    def multiply(n, lifts):
        for load in loads[7 + 3 * n : 10 + 3 * n]:
            load.wait()
        lanes = slice(256 * n, 256 * n + 256)
        lift_value = jnp.dot(nm[...], w[:, lanes], preferred_element_type=F32)
        lift_gate = jnp.dot(nm[...], w[:, 1024 + 256 * n : 1280 + 256 * n], preferred_element_type=F32)
        back = lax.dot_general(gs[...], pw[lanes, :], (((1,), (1,)), ((), ())), preferred_element_type=F32)
        for h in range(2):
            lifts[h] = lift_value[:, 128 * h : 128 * h + 128]
            lifts[2 + h] = lift_gate[:, 128 * h : 128 * h + 128]
            lifts[4 + h] = back[:, 128 * h : 128 * h + 128]

    def channels(n, h, lifts):
        at = 256 * n + 128 * h
        taps = [taps_ref[k : k + 1, at : at + 128] for k in range(9)]
        for i in range(10):
            rows = pl.ds(8 + 40 * i, 40)
            s = jax.nn.sigmoid(lifts[2 + h, rows, :])
            lifts[2 + h, rows, :] = s
            gat[h, rows, :] = (lifts[h, rows, :] * s * mask[rows, :]).astype(BF).astype(F32)
        for i in range(7):
            r = 12 + 56 * i
            rows = pl.ds(r, 56)
            conv = taps[0] * gat[h, pl.ds(r - 4, 56), :]
            for k in range(1, 9):
                conv = conv + taps[k] * gat[h, pl.ds(r + k - 4, 56), :]
            s = jax.nn.sigmoid(conv)
            active = conv * s
            acf[h, rows, :] = active
            grad = lifts[4 + h, rows, :] * (s + active * (1.0 - s))
            gcon[h, rows, :] = grad.astype(BF).astype(F32)
        sums = [jnp.zeros((8, 128), F32) for _ in range(9)]
        for i in range(8):
            r = EDGE + 48 * i
            rows = pl.ds(r, 48)
            own = pl.ds(r - EDGE, 48)
            grad = taps[0] * gcon[h, pl.ds(r + 4, 48), :]
            for k in range(1, 9):
                grad = grad + taps[k] * gcon[h, pl.ds(r + 4 - k, 48), :]
            s = lifts[2 + h, rows, :]
            first = grad * mask[rows, :] * s
            both[0, own, at : at + 128] = first.astype(BF)
            both[1, own, at : at + 128] = (first * lifts[h, rows, :] * (1.0 - s)).astype(BF)
            act[own, at : at + 128] = acf[h, rows, :].astype(BF)
            here = gcon[h, rows, :]
            for k in range(9):
                product = here * gat[h, pl.ds(r + k - 4, 48), :]
                sums[k] = sums[k] + jnp.sum(product.reshape(6, 8, 128), axis=0)
        for k in range(9):
            krows[k % 2, k // 2 : k // 2 + 1, at : at + 128] = jnp.sum(sums[k], axis=0, keepdims=True)

    lifts = (lifts0, lifts1)
    sends = []
    multiply(0, lifts0)
    for n in range(4):
        if n < 3:
            multiply(n + 1, lifts[(n + 1) % 2])
        for h in range(2):
            channels(n, h, lifts[n % 2])
        own, lanes = pl.ds(0, ROWS), pl.ds(256 * n, 256)
        for i, (src, dst) in enumerate(
            (
                (both.at[1 - core, own, lanes], give_o.at[own, lanes]),
                (act.at[:, lanes], act_o.at[:, lanes]),
                (both.at[core, own, lanes], keep_o.at[own, lanes]),
                (both.at[:, own, lanes], both_o.at[:, :, lanes]),
            )
        ):
            sends.append(pltpu.make_async_copy(src, dst, sem_out.at[n, i]))
            sends[-1].start()
    tail = pl.ds(ROWS, 16)
    for c in range(2):
        both[c, ROWS:, :] = krows[c].astype(BF)
    for i, (c, dst) in enumerate(((1 - core, give_o), (core, keep_o))):
        sends.append(pltpu.make_async_copy(both.at[c, tail], dst.at[tail], sem_out.at[4, i]))
        sends[-1].start()
    for copy in sends:
        copy.wait()


def forward_backward(lengths, gain, taps, normed, gb_keep, gb_give, before, after, w, pw):
    wide = jax.ShapeDtypeStruct((ROWS, 1024), BF)
    tall = jax.ShapeDtypeStruct((ROWS + 16, 1024), BF)
    return pl.pallas_call(
        main_kernel,
        out_shape=[wide, jax.ShapeDtypeStruct((2, ROWS, 1024), BF), tall, tall],
        in_specs=[smem_spec(), vmem_spec(), vmem_spec()] + [hbm_spec()] * 7,
        out_specs=[hbm_spec()] * 4,
        scratch_shapes=[
            pltpu.VMEM((LONG, 1024), BF),
            pltpu.VMEM((1024, 2048), BF),
            pltpu.VMEM((1024, 1024), BF),
            pltpu.VMEM((LONG, 1024), BF),
            pltpu.VMEM((ROWS, 1024), BF),
            pltpu.VMEM((2, ROWS + 16, 1024), BF),
            pltpu.VMEM((6, LONG, 128), F32),
            pltpu.VMEM((6, LONG, 128), F32),
            pltpu.VMEM((2, LONG, 128), F32),
            pltpu.VMEM((2, LONG, 128), F32),
            pltpu.VMEM((2, LONG, 128), F32),
            pltpu.VMEM((LONG, 128), F32),
            pltpu.VMEM((2, 16, 1024), F32),
            pltpu.SemaphoreType.DMA((19,)),
            pltpu.SemaphoreType.DMA((5, 4)),
        ],
        name="forward_backward",
    )(lengths, gain, taps, normed, gb_keep, gb_give, before, after, w, pw)


def outputs_kernel(info_ref, gain_ref, xh, gh, acth, bothh, wh, pwh, after_this, out_o, grad_o, mark_o, *rest):
    mark_o[...] = jnp.zeros((8, 128), F32)
    x, g, act, both, w, pw, sem, sem_out = rest
    pairs = [(acth, act), (pwh, pw), (xh, x), (bothh, both), (wh, w), (gh, g)]
    loads = [pltpu.make_async_copy(src, dst, sem.at[i]) for i, (src, dst) in enumerate(pairs)]
    for load in loads:
        load.start()
    for load in loads[:3]:
        load.wait()
    contract = (((1,), (1,)), ((), ()))
    for i in range(3):
        rows = slice(128 * i, 128 * i + 128)
        branch = jnp.dot(act[rows, :], pw[...], preferred_element_type=F32)
        branch = jnp.where(inside(info_ref, 128 * i, (128, 1024)), branch, 0.0)
        act[rows, :] = (x[rows, :].astype(F32) + branch).astype(BF)
    first = pltpu.make_async_copy(act, out_o, sem_out.at[0])
    first.start()
    for load in loads[3:]:
        load.wait()
    for i in range(3):
        rows = slice(128 * i, 128 * i + 128)
        grad = lax.dot_general(both[0, rows, :], w[:, :1024], contract, preferred_element_type=F32)
        grad = grad + lax.dot_general(both[1, rows, :], w[:, 1024:], contract, preferred_element_type=F32)
        u = grad * gain_ref[...]
        values = x[rows, :].astype(F32)
        center = values - jnp.mean(values, axis=-1, keepdims=True)
        scale = lax.rsqrt(jnp.mean(center * center, axis=-1, keepdims=True) + eps_norm)
        xhat = center * scale
        u = scale * (u - jnp.mean(u, axis=-1, keepdims=True) - xhat * jnp.mean(u * xhat, axis=-1, keepdims=True))
        g[rows, :] = (g[rows, :].astype(F32) + u).astype(BF)
    second = pltpu.make_async_copy(g, grad_o, sem_out.at[1])
    second.start()
    first.wait()
    second.wait()


def outputs(info, gain, x, g, act, both, w, pw, after_this):
    wide = jax.ShapeDtypeStruct((ROWS, 1024), BF)
    return pl.pallas_call(
        outputs_kernel,
        out_shape=[wide, wide, jax.ShapeDtypeStruct((8, 128), F32)],
        in_specs=[smem_spec(), vmem_spec()] + [hbm_spec()] * 7,
        out_specs=[hbm_spec()] * 2 + [vmem_spec()],
        scratch_shapes=[
            pltpu.VMEM((ROWS, 1024), BF),
            pltpu.VMEM((ROWS, 1024), BF),
            pltpu.VMEM((ROWS, 1024), BF),
            pltpu.VMEM((2, ROWS, 1024), BF),
            pltpu.VMEM((1024, 2048), BF),
            pltpu.VMEM((1024, 1024), BF),
            pltpu.SemaphoreType.DMA((6,)),
            pltpu.SemaphoreType.DMA((2,)),
        ],
        name="outputs",
    )(info, gain, x, g, act, both, w, pw, after_this)


def local(features, cotangent, lengths, norm_gain, lift_weight, conv_kernel, proj_weight):
    x, g = features[0], cotangent[0]
    frames, width = x.shape
    edge = jnp.stack([x[-EDGE:], g[-EDGE:]])
    start = jnp.stack([x[:EDGE], g[:EDGE]])
    before = lax.ppermute(edge, ("yh", "x"), [(i, i + 1) for i in range(7)])
    after = lax.ppermute(start, ("yh", "x"), [(i + 1, i) for i in range(7)])
    gain = norm_gain[None]
    normed, gb_keep, gb_give = early(lengths, gain, x, g)
    normed_other = pair_swap(normed)
    gb_other = pair_swap(gb_give)
    activated, both, keep, give = forward_backward(
        lengths, gain, conv_kernel, normed, gb_keep, gb_give, before, after, lift_weight, proj_weight
    )
    keep_other = pair_swap(give)
    act_other = pair_swap(activated)
    chunk = (2 * width * width + width * width + 10 * width) // 256
    operands = (normed, normed_other, keep, keep_other, activated, act_other, gb_keep, gb_other, lift_weight)
    blocks = weight_blocks(gain, operands)
    output, grad_features, mark = outputs(lengths, gain, x, g, activated, both, lift_weight, proj_weight, blocks[0])
    grads = own_chunk(reduce_terms(blocks, mark), chunk, float(frames * 256) ** (-0.5))
    return output[None], grad_features[None], grads


def solution(mesh):
    fine = Mesh(mesh.devices.reshape(2, 4, 8, 2, 2), ALL)
    act = P(("z", "yl", "c"), ("yh", "x"), None)

    return jax.shard_map(
        local,
        mesh=fine,
        in_specs=(act, act, P(("z", "yl", "c")), P(), P(), P(), P()),
        out_specs=(act, act, P(ALL)),
        check_vma=False,
    )
```

```python
import functools

import jax
import jax.numpy as jnp
from jax import lax
from jax.experimental import pallas as pl
from jax.experimental.pallas import tpu as pltpu
from jax.sharding import Mesh, PartitionSpec as P


eps_norm = 1e-05
BF = jnp.bfloat16
F32 = jnp.float32
WIN = 12


def any_spec():
    return pl.BlockSpec(memory_space=pl.ANY)


def hbm_spec():
    return pl.BlockSpec(memory_space=pltpu.HBM)


def vmem_spec():
    return pl.BlockSpec(memory_space=pltpu.VMEM)


def smem_spec():
    return pl.BlockSpec(memory_space=pltpu.SMEM)


def place(part_a, part_b, wide, begin, count):
    at = 0
    while at < count:
        window, inside = divmod(begin + at, 96)
        low = inside % 48
        step = min(48 - low, count - at)
        rows = wide[at : at + step, :].astype(BF)
        yh, rest = divmod(window, 64)
        if inside < 48:
            part_a[yh, rest, low : low + step, :] = rows
        else:
            part_b[yh * 2 + rest % 2, rest // 2, low : low + step, :] = rows
        at += step


def weight_kernel(gain_ref, n0h, n1h, k0h, k1h, a0h, a1h, g0h, g1h, wh, *rest):
    outs, rest = rest[:8], rest[8:]
    n0, n1, k0, k1, a0, a1, g0, g1, w, part_a, part_b, wide, extra, sem, sem_in = rest
    core = lax.axis_index("c")
    loads = [
        pltpu.make_async_copy(src, dst, sem_in.at[i])
        for i, (src, dst) in enumerate(
            zip(
                (a0h, g0h, a1h, g1h, n0h, k0h, n1h, k1h, wh.at[:, pl.ds(core * 1024, 1024)]),
                (a0, g0, a1, g1, n0, k0, n1, k1, w),
            )
        )
    ]
    for load in loads:
        load.start()
    contract = (((0,), (0,)), ((), ()))
    copies = []

    def ship(yh, x):
        moves = [(part_a.at[yh, pl.ds(16 * x, 16)], outs[:4], pl.ds(16 * yh, 16), (x - lax.axis_index("x") + 4) % 4)]
        for yl in range(2):
            y = 2 * yh + yl
            slot = (y - lax.axis_index(("yh", "yl")) + 4) % 4
            moves.append((part_b.at[y, pl.ds(8 * x, 8)], outs[4:], pl.ds(8 * x, 8), slot))
        for i, (src, blocks, rows, slot) in enumerate(moves):
            at = sem.at[3 * (4 * yh + x) + i]
            for s in range(4):

                @pl.when(slot == s)
                def _(s=s, src=src, blocks=blocks, rows=rows, at=at):
                    pltpu.make_async_copy(src, blocks[s].at[rows], at).start()

            copies.append(pltpu.make_async_copy(src, blocks[0].at[rows], at))

    for load in loads[:4]:
        load.wait()
    for m in range(4):
        cols = slice(256 * m, 256 * m + 256)
        done = lax.dot_general(a0[:, cols], g0[...], contract, preferred_element_type=F32)
        done = done + lax.dot_general(a1[:, cols], g1[...], contract, preferred_element_type=F32)
        for v in range(4):
            wide[pl.ds(v, 256, stride=4), :] = done[:, 128 * v : 128 * v + 128]
        place(part_a, part_b, wide, 8192 + 1024 * m, 1024)
    ship(1, 2)
    ship(1, 3)
    for load in loads[4:]:
        load.wait()
    gains = []
    for m in range(4):
        cols = slice(256 * m, 256 * m + 256)
        done = lax.dot_general(n0[:, cols], k0[0:ROWS, :], contract, preferred_element_type=F32)
        done = done + lax.dot_general(n1[:, cols], k1[0:ROWS, :], contract, preferred_element_type=F32)
        folded = jnp.zeros((256, 128), F32)
        for v in range(8):
            piece = done[:, 128 * v : 128 * v + 128]
            wide[pl.ds(v, 256, stride=8), :] = piece
            folded = folded + piece * w[cols, 128 * v : 128 * v + 128].astype(F32)
        gains.append(jnp.sum(folded.T, axis=0, keepdims=True))
        place(part_a, part_b, wide, 2048 * m, 2048)
        for group in ((0,), (1,), (2, 3), (4, 5))[m]:
            ship(*divmod(group, 4))
    for m in range(4):
        for j in range(2):
            at = 256 * m + 128 * j
            extra[40 + 2 * m + j : 41 + 2 * m + j, :] = gains[m][:, 128 * j : 128 * j + 128] / gain_ref[:, at : at + 128]
    taps = k0[ROWS:, :].astype(F32) + k1[ROWS:, :].astype(F32)
    for p in range(5):
        for v in range(8):
            extra[8 * p + v : 8 * p + v + 1, :] = taps[p : p + 1, 128 * v : 128 * v + 128]
    small = part_b.at[4, 0]
    small[...] = extra[...].astype(BF)
    for s in range(4):
        copies.append(pltpu.make_async_copy(small, outs[s].at[32], sem.at[24 + s]))
        copies[-1].start()
    for copy in copies:
        copy.wait()


def weight_blocks(gain, operands):
    blocks = [jax.ShapeDtypeStruct((33, 48, 128), BF)] * 4 + [jax.ShapeDtypeStruct((32, 48, 128), BF)] * 4
    return pl.pallas_call(
        weight_kernel,
        out_shape=blocks,
        in_specs=[vmem_spec()] + [hbm_spec(), any_spec()] * 4 + [hbm_spec()],
        out_specs=[hbm_spec()] * 8,
        scratch_shapes=[pltpu.VMEM(o.shape, BF) for o in operands[:8]]
        + [
            pltpu.VMEM((1024, 1024), BF),
            pltpu.VMEM((2, 64, 48, 128), BF),
            pltpu.VMEM((5, 32, 48, 128), BF),
            pltpu.VMEM((2048, 128), F32),
            pltpu.VMEM((48, 128), F32),
            pltpu.SemaphoreType.DMA((28,)),
            pltpu.SemaphoreType.DMA((9,)),
        ],
        compiler_params=pltpu.CompilerParams(vmem_limit_bytes=57 << 20),
        name="weight_grads",
    )(gain, *operands)


def sum_of(refs, index):
    total = refs[0][index].astype(F32)
    for ref in refs[1:]:
        total = total + ref[index].astype(F32)
    return total.astype(BF)


def first_x_kernel(i0, i1, i2, i3, mark, *outs):
    for s in range(4):
        y = (lax.axis_index(("yh", "yl")) + s) % 4
        base = (y // 2) * 16 + y % 2
        for z in range(8):
            outs[s][z] = sum_of((i0, i1, i2, i3), base + 2 * z)
        outs[s][8] = sum_of((i0, i1, i2, i3), 32)


def first_y_kernel(i0, i1, i2, i3, *outs):
    for s in range(4):
        x = (lax.axis_index("x") + s) % 4
        for z in range(8):
            outs[s][z] = sum_of((i0, i1, i2, i3), x * 8 + z)


def second_kernel(a0, a1, a2, a3, b0, b1, b2, b3, out):
    small = sum_of((a0, a1, a2, a3), 8)
    for z in range(8):
        out[z, 0:48, :] = sum_of((a0, a1, a2, a3), z)
        out[z, 48:96, :] = sum_of((b0, b1, b2, b3), z)
        out[z, 96:144, :] = small


def send(blocks, axes):
    n = 4
    got = [blocks[0]]
    for step in (2, 1, 3):
        got.append(lax.ppermute(blocks[step], axes, [(i, (i + step) % n) for i in range(n)]))
    return got


def reduce_terms(blocks, mark):
    got_x = send(blocks[:4], "x")
    got_y = send(blocks[4:], ("yh", "yl"))
    block9 = jax.ShapeDtypeStruct((9, 48, 128), BF)
    block8 = jax.ShapeDtypeStruct((8, 48, 128), BF)
    after_x = pl.pallas_call(
        first_x_kernel,
        out_shape=[block9] * 4,
        in_specs=[vmem_spec()] * 4 + [any_spec()],
        out_specs=[vmem_spec()] * 4,
        compiler_params=pltpu.CompilerParams(vmem_limit_bytes=8 << 20),
        name="sum_after_x",
    )(*got_x, mark)
    after_y = pl.pallas_call(
        first_y_kernel,
        out_shape=[block8] * 4,
        in_specs=[vmem_spec()] * 4,
        out_specs=[vmem_spec()] * 4,
        compiler_params=pltpu.CompilerParams(vmem_limit_bytes=8 << 20),
        name="sum_after_y",
    )(*got_y)
    got_a = send(after_x, ("yh", "yl"))
    got_b = send(after_y, "x")
    ready = pl.pallas_call(
        second_kernel,
        out_shape=jax.ShapeDtypeStruct((8, 144, 128), BF),
        in_specs=[vmem_spec()] * 8,
        out_specs=vmem_spec(),
        compiler_params=pltpu.CompilerParams(vmem_limit_bytes=6 << 20),
        name="sum_before_z",
    )(*got_a, *got_b)
    return lax.all_to_all(ready, "z", split_axis=0, concat_axis=0, tiled=True)


ALL = ("yh", "x", "z", "yl", "c")


def total_kernel(parts, total):
    done = parts[0].astype(F32)
    for z in range(1, 8):
        done = done + parts[z].astype(F32)
    total[...] = done


def chunk_kernel(own, other, follow, out, half0, half1, flat, *, chunk, scale):
    core = lax.axis_index("c")
    chip = lax.axis_index(("yh", "x", "z", "yl"))
    first = core == 0
    mine, others = own[...], other[...]
    half0[0:96, :] = jnp.where(first, mine[0:96], others[0:96])
    half1[0:96, :] = jnp.where(first, others[0:96], mine[0:96])
    small0 = jnp.where(first, mine[96:144], others[96:144])
    small1 = jnp.where(first, others[96:144], mine[96:144])
    both = small0[40:48] + small1[40:48]
    last = chip == 127
    half0[96:144, :] = jnp.where(last, small0, follow[0:48])
    half1[96:144, :] = jnp.where(last, small1, follow[48:96])

    @pl.when(last)
    def _():
        half1[128:136, :] = both

    for p in range(18):
        pair = chip * WIN + p
        proj = (pair >= 1024) & (pair < 1536)
        for h, half in ((0, half0), (1, half1)):
            tile = half[8 * p : 8 * p + 8, :] * scale

            @pl.when(proj)
            def _(p=p, h=h, tile=tile):
                flat[16 * p + 4 * h : 16 * p + 4 * h + 4, :] = tile[0:4]
                flat[16 * p + 8 + 4 * h : 16 * p + 12 + 4 * h, :] = tile[4:8]

            @pl.when(jnp.logical_not(proj))
            def _(p=p, h=h, tile=tile):
                flat[16 * p + 8 * h : 16 * p + 8 * h + 8, :] = tile

    begin = (2 * chip + core) * chunk - chip * (WIN * 2048)
    row, lane = begin // 128, begin % 128
    low = pltpu.roll(flat[pl.ds(row, 104), :], (128 - lane) % 128, axis=1)
    high = pltpu.roll(flat[pl.ds(row + 1, 104), :], (128 - lane) % 128, axis=1)
    at = lax.broadcasted_iota(jnp.int32, (104, 128), 1)
    out[...] = jnp.where(at < 128 - lane, low, high)


def own_chunk(swapped, chunk, grad_scale):
    total = pl.pallas_call(
        total_kernel,
        out_shape=jax.ShapeDtypeStruct((144, 128), F32),
        in_specs=[vmem_spec()],
        out_specs=vmem_spec(),
        compiler_params=pltpu.CompilerParams(vmem_limit_bytes=4 << 20),
        name="sum_after_z",
    )(swapped)
    other = lax.ppermute(total, "c", [(0, 1), (1, 0)])
    heads = jnp.concatenate([other[:48], total[:48]])
    follow = lax.ppermute(heads, ALL, [(2 * j + 1, 2 * j - 1) for j in range(1, 128)])
    out = pl.pallas_call(
        functools.partial(chunk_kernel, chunk=chunk, scale=grad_scale),
        out_shape=jax.ShapeDtypeStruct((104, 128), F32),
        in_specs=[vmem_spec()] * 3,
        out_specs=vmem_spec(),
        scratch_shapes=[pltpu.VMEM((144, 128), F32), pltpu.VMEM((144, 128), F32), pltpu.VMEM((312, 128), F32)],
        compiler_params=pltpu.CompilerParams(vmem_limit_bytes=4 << 20),
        name="own_chunk",
    )(total, other, follow)
    return out.reshape(-1)[:chunk]


def pair_swap(array):
    return lax.ppermute(array, "c", [(0, 1), (1, 0)])


ROWS = 384
EDGE = 16
LONG = ROWS + 2 * EDGE


def inside(length_ref, first, shape):
    at = lax.axis_index(("yh", "x")) * ROWS + first + lax.broadcasted_iota(jnp.int32, shape, 0)
    return (at >= 0) & (at < length_ref[0])


def normed_rows(rows, gain):
    values = rows.astype(F32)
    center = values - jnp.mean(values, axis=-1, keepdims=True)
    scale = lax.rsqrt(jnp.mean(center * center, axis=-1, keepdims=True) + eps_norm)
    return (center * scale * gain).astype(BF)


PART = 96


def early_kernel(length_ref, gain_ref, xh, gh, normed_o, keep_o, give_o, x, g, sem, sem_out):
    core = lax.axis_index("c")
    parts = [pl.ds(PART * i, PART) for i in range(ROWS // PART)]
    loads = [pltpu.make_async_copy(xh.at[p], x.at[p], sem.at[0, i]) for i, p in enumerate(parts)]
    loads += [pltpu.make_async_copy(gh.at[p], g.at[p], sem.at[1, i]) for i, p in enumerate(parts)]
    for load in loads:
        load.start()
    gain = gain_ref[...]
    sends = []
    for i, p in enumerate(parts):
        loads[i].wait()
        for j in range(0, PART, 16):
            rows = pl.ds(PART * i + j, 16)
            x[rows, :] = normed_rows(x[rows, :], gain)
        sends.append(pltpu.make_async_copy(x.at[p], normed_o.at[p], sem_out.at[0, i]))
        sends[-1].start()
    for i, p in enumerate(parts):
        loads[len(parts) + i].wait()
        valid = inside(length_ref, PART * i, (PART, 1024))
        g[p, :] = jnp.where(valid, g[p, :].astype(F32), 0.0).astype(BF)
        for k, (out, at) in enumerate(((keep_o, core * 512), (give_o, 512 - core * 512))):
            sends.append(pltpu.make_async_copy(g.at[p, pl.ds(at, 512)], out.at[p], sem_out.at[1 + k, i]))
            sends[-1].start()
    for copy in sends:
        copy.wait()


def early(lengths, gain, x, g):
    wide = jax.ShapeDtypeStruct((ROWS, 1024), BF)
    half = jax.ShapeDtypeStruct((ROWS, 512), BF)
    return pl.pallas_call(
        early_kernel,
        out_shape=[wide, half, half],
        in_specs=[smem_spec(), vmem_spec()] + [hbm_spec()] * 2,
        out_specs=[hbm_spec()] * 3,
        scratch_shapes=[
            pltpu.VMEM((ROWS, 1024), BF),
            pltpu.VMEM((ROWS, 1024), BF),
            pltpu.SemaphoreType.DMA((2, ROWS // PART)),
            pltpu.SemaphoreType.DMA((3, ROWS // PART)),
        ],
        name="early",
    )(lengths, gain, x, g)


def main_kernel(info_ref, gain_ref, taps_ref, nh, gkh, ggh, beforeh, afterh, wh, pwh, *rest):
    act_o, both_o, keep_o, give_o = rest[:4]
    gs, w, pw, nm, act, both, lifts0, lifts1, gat, gcon, acf, mask, krows, sem, sem_out = rest[4:]
    core = lax.axis_index("c")
    pairs = [
        (beforeh.at[0], nm.at[pl.ds(0, EDGE)]),
        (afterh.at[0], nm.at[pl.ds(EDGE + ROWS, EDGE)]),
        (beforeh.at[1], gs.at[pl.ds(0, EDGE)]),
        (afterh.at[1], gs.at[pl.ds(EDGE + ROWS, EDGE)]),
        (nh, nm.at[pl.ds(EDGE, ROWS)]),
        (gkh, gs.at[pl.ds(EDGE, ROWS), pl.ds(core * 512, 512)]),
        (ggh, gs.at[pl.ds(EDGE, ROWS), pl.ds(512 - core * 512, 512)]),
    ]
    for n in range(4):
        pairs.append((wh.at[:, pl.ds(256 * n, 256)], w.at[:, pl.ds(256 * n, 256)]))
        pairs.append((wh.at[:, pl.ds(1024 + 256 * n, 256)], w.at[:, pl.ds(1024 + 256 * n, 256)]))
        pairs.append((pwh.at[pl.ds(256 * n, 256)], pw.at[pl.ds(256 * n, 256)]))
    loads = [pltpu.make_async_copy(src, dst, sem.at[i]) for i, (src, dst) in enumerate(pairs)]
    for load in loads:
        load.start()
    mask[...] = inside(info_ref, -EDGE, (LONG, 128)).astype(F32)
    krows[...] = jnp.zeros((2, 16, 1024), F32)
    for load in loads[:4]:
        load.wait()
    for first in (0, EDGE + ROWS):
        rows = pl.ds(first, EDGE)
        nm[rows, :] = normed_rows(nm[rows, :], gain_ref[...])
        gs[rows, :] = jnp.where(inside(info_ref, first - EDGE, (EDGE, 1024)), gs[rows, :].astype(F32), 0.0).astype(BF)
    for load in loads[4:7]:
        load.wait()

    def multiply(n, lifts):
        for load in loads[7 + 3 * n : 10 + 3 * n]:
            load.wait()
        lanes = slice(256 * n, 256 * n + 256)
        lift_value = jnp.dot(nm[...], w[:, lanes], preferred_element_type=F32)
        lift_gate = jnp.dot(nm[...], w[:, 1024 + 256 * n : 1280 + 256 * n], preferred_element_type=F32)
        back = lax.dot_general(gs[...], pw[lanes, :], (((1,), (1,)), ((), ())), preferred_element_type=F32)
        for h in range(2):
            lifts[h] = lift_value[:, 128 * h : 128 * h + 128]
            lifts[2 + h] = lift_gate[:, 128 * h : 128 * h + 128]
            lifts[4 + h] = back[:, 128 * h : 128 * h + 128]

    def channels(n, h, lifts):
        at = 256 * n + 128 * h
        taps = [taps_ref[k : k + 1, at : at + 128] for k in range(9)]
        for i in range(10):
            rows = pl.ds(8 + 40 * i, 40)
            s = jax.nn.sigmoid(lifts[2 + h, rows, :])
            lifts[2 + h, rows, :] = s
            gat[h, rows, :] = (lifts[h, rows, :] * s * mask[rows, :]).astype(BF).astype(F32)
        for i in range(7):
            r = 12 + 56 * i
            rows = pl.ds(r, 56)
            conv = taps[0] * gat[h, pl.ds(r - 4, 56), :]
            for k in range(1, 9):
                conv = conv + taps[k] * gat[h, pl.ds(r + k - 4, 56), :]
            s = jax.nn.sigmoid(conv)
            active = conv * s
            acf[h, rows, :] = active
            grad = lifts[4 + h, rows, :] * (s + active * (1.0 - s))
            gcon[h, rows, :] = grad.astype(BF).astype(F32)
        sums = [jnp.zeros((8, 128), F32) for _ in range(9)]
        for i in range(8):
            r = EDGE + 48 * i
            rows = pl.ds(r, 48)
            own = pl.ds(r - EDGE, 48)
            grad = taps[0] * gcon[h, pl.ds(r + 4, 48), :]
            for k in range(1, 9):
                grad = grad + taps[k] * gcon[h, pl.ds(r + 4 - k, 48), :]
            s = lifts[2 + h, rows, :]
            first = grad * mask[rows, :] * s
            both[0, own, at : at + 128] = first.astype(BF)
            both[1, own, at : at + 128] = (first * lifts[h, rows, :] * (1.0 - s)).astype(BF)
            act[own, at : at + 128] = acf[h, rows, :].astype(BF)
            here = gcon[h, rows, :]
            for k in range(9):
                product = here * gat[h, pl.ds(r + k - 4, 48), :]
                sums[k] = sums[k] + jnp.sum(product.reshape(6, 8, 128), axis=0)
        for k in range(9):
            krows[k % 2, k // 2 : k // 2 + 1, at : at + 128] = jnp.sum(sums[k], axis=0, keepdims=True)

    lifts = (lifts0, lifts1)
    sends = []
    multiply(0, lifts0)
    for n in range(4):
        if n < 3:
            multiply(n + 1, lifts[(n + 1) % 2])
        for h in range(2):
            channels(n, h, lifts[n % 2])
        own, lanes = pl.ds(0, ROWS), pl.ds(256 * n, 256)
        for i, (src, dst) in enumerate(
            (
                (both.at[1 - core, own, lanes], give_o.at[own, lanes]),
                (act.at[:, lanes], act_o.at[:, lanes]),
                (both.at[core, own, lanes], keep_o.at[own, lanes]),
                (both.at[:, own, lanes], both_o.at[:, :, lanes]),
            )
        ):
            sends.append(pltpu.make_async_copy(src, dst, sem_out.at[n, i]))
            sends[-1].start()
    tail = pl.ds(ROWS, 16)
    for c in range(2):
        both[c, ROWS:, :] = krows[c].astype(BF)
    for i, (c, dst) in enumerate(((1 - core, give_o), (core, keep_o))):
        sends.append(pltpu.make_async_copy(both.at[c, tail], dst.at[tail], sem_out.at[4, i]))
        sends[-1].start()
    for copy in sends:
        copy.wait()


def forward_backward(lengths, gain, taps, normed, gb_keep, gb_give, before, after, w, pw):
    wide = jax.ShapeDtypeStruct((ROWS, 1024), BF)
    tall = jax.ShapeDtypeStruct((ROWS + 16, 1024), BF)
    return pl.pallas_call(
        main_kernel,
        out_shape=[wide, jax.ShapeDtypeStruct((2, ROWS, 1024), BF), tall, tall],
        in_specs=[smem_spec(), vmem_spec(), vmem_spec()] + [hbm_spec()] * 7,
        out_specs=[hbm_spec()] * 4,
        scratch_shapes=[
            pltpu.VMEM((LONG, 1024), BF),
            pltpu.VMEM((1024, 2048), BF),
            pltpu.VMEM((1024, 1024), BF),
            pltpu.VMEM((LONG, 1024), BF),
            pltpu.VMEM((ROWS, 1024), BF),
            pltpu.VMEM((2, ROWS + 16, 1024), BF),
            pltpu.VMEM((6, LONG, 128), F32),
            pltpu.VMEM((6, LONG, 128), F32),
            pltpu.VMEM((2, LONG, 128), F32),
            pltpu.VMEM((2, LONG, 128), F32),
            pltpu.VMEM((2, LONG, 128), F32),
            pltpu.VMEM((LONG, 128), F32),
            pltpu.VMEM((2, 16, 1024), F32),
            pltpu.SemaphoreType.DMA((19,)),
            pltpu.SemaphoreType.DMA((5, 4)),
        ],
        name="forward_backward",
    )(lengths, gain, taps, normed, gb_keep, gb_give, before, after, w, pw)


def outputs_kernel(info_ref, gain_ref, xh, gh, acth, bothh, wh, pwh, after_this, out_o, grad_o, mark_o, *rest):
    mark_o[...] = jnp.zeros((8, 128), F32)
    x, g, act, both, w, pw, sem, sem_out = rest
    pairs = [(acth, act), (pwh, pw), (xh, x), (bothh, both), (wh, w), (gh, g)]
    loads = [pltpu.make_async_copy(src, dst, sem.at[i]) for i, (src, dst) in enumerate(pairs)]
    for load in loads:
        load.start()
    for load in loads[:3]:
        load.wait()
    contract = (((1,), (1,)), ((), ()))
    for i in range(3):
        rows = slice(128 * i, 128 * i + 128)
        branch = jnp.dot(act[rows, :], pw[...], preferred_element_type=F32)
        branch = jnp.where(inside(info_ref, 128 * i, (128, 1024)), branch, 0.0)
        act[rows, :] = (x[rows, :].astype(F32) + branch).astype(BF)
    first = pltpu.make_async_copy(act, out_o, sem_out.at[0])
    first.start()
    for load in loads[3:]:
        load.wait()
    for i in range(3):
        rows = slice(128 * i, 128 * i + 128)
        grad = lax.dot_general(both[0, rows, :], w[:, :1024], contract, preferred_element_type=F32)
        grad = grad + lax.dot_general(both[1, rows, :], w[:, 1024:], contract, preferred_element_type=F32)
        u = grad * gain_ref[...]
        values = x[rows, :].astype(F32)
        center = values - jnp.mean(values, axis=-1, keepdims=True)
        scale = lax.rsqrt(jnp.mean(center * center, axis=-1, keepdims=True) + eps_norm)
        xhat = center * scale
        u = scale * (u - jnp.mean(u, axis=-1, keepdims=True) - xhat * jnp.mean(u * xhat, axis=-1, keepdims=True))
        g[rows, :] = (g[rows, :].astype(F32) + u).astype(BF)
    second = pltpu.make_async_copy(g, grad_o, sem_out.at[1])
    second.start()
    first.wait()
    second.wait()


def outputs(info, gain, x, g, act, both, w, pw, after_this):
    wide = jax.ShapeDtypeStruct((ROWS, 1024), BF)
    return pl.pallas_call(
        outputs_kernel,
        out_shape=[wide, wide, jax.ShapeDtypeStruct((8, 128), F32)],
        in_specs=[smem_spec(), vmem_spec()] + [hbm_spec()] * 7,
        out_specs=[hbm_spec()] * 2 + [vmem_spec()],
        scratch_shapes=[
            pltpu.VMEM((ROWS, 1024), BF),
            pltpu.VMEM((ROWS, 1024), BF),
            pltpu.VMEM((ROWS, 1024), BF),
            pltpu.VMEM((2, ROWS, 1024), BF),
            pltpu.VMEM((1024, 2048), BF),
            pltpu.VMEM((1024, 1024), BF),
            pltpu.SemaphoreType.DMA((6,)),
            pltpu.SemaphoreType.DMA((2,)),
        ],
        name="outputs",
    )(info, gain, x, g, act, both, w, pw, after_this)


def local(features, cotangent, lengths, norm_gain, lift_weight, conv_kernel, proj_weight):
    x, g = features[0], cotangent[0]
    frames, width = x.shape
    edge = jnp.stack([x[-EDGE:], g[-EDGE:]])
    start = jnp.stack([x[:EDGE], g[:EDGE]])
    before = lax.ppermute(edge, ("yh", "x"), [(i, i + 1) for i in range(7)])
    after = lax.ppermute(start, ("yh", "x"), [(i + 1, i) for i in range(7)])
    gain = norm_gain[None]
    normed, gb_keep, gb_give = early(lengths, gain, x, g)
    normed_other = pair_swap(normed)
    gb_other = pair_swap(gb_give)
    activated, both, keep, give = forward_backward(
        lengths, gain, conv_kernel, normed, gb_keep, gb_give, before, after, lift_weight, proj_weight
    )
    keep_other = pair_swap(give)
    act_other = pair_swap(activated)
    chunk = (2 * width * width + width * width + 10 * width) // 256
    operands = (normed, normed_other, keep, keep_other, activated, act_other, gb_keep, gb_other, lift_weight)
    blocks = weight_blocks(gain, operands)
    output, grad_features, mark = outputs(lengths, gain, x, g, activated, both, lift_weight, proj_weight, blocks[0])
    grads = own_chunk(reduce_terms(blocks, mark), chunk, float(frames * 256) ** (-0.5))
    return output[None], grad_features[None], grads


def solution(mesh):
    fine = Mesh(mesh.devices.reshape(2, 4, 8, 2, 2), ALL)
    act = P(("z", "yl", "c"), ("yh", "x"), None)

    return jax.shard_map(
        local,
        mesh=fine,
        in_specs=(act, act, P(("z", "yl", "c")), P(), P(), P(), P()),
        out_specs=(act, act, P(ALL)),
        check_vma=False,
    )
```
